512 devices in a mesh: fil: 128 (over x, y_hi, z), row: 4 (over y_lo, core).
Axes of the slice: x: 4, y: 8 (y_hi: 4, y_lo: 2; y = y_hi * 2 + y_lo), z: 8, core: 2. Of those that a mesh axis runs over, the one named last changes fastest.
Arguments:
- images: bfloat16 [1024, 2, 256, 128], P('fil', None, 'row'), may hold values from -6 to 6
- defocus: float32 [1024], P('fil'), may hold values from 0.5 to 2
- references: bfloat16 [128, 2, 256, 128], P('fil', None, 'row'), may hold values from -0.0234375 to 0.0234375
- offsets: int32 [1024, 32, 2], P('fil'), may hold values from -8 to 8
- posterior: int32 [1024, 32], P('fil'), may hold values from 0 to 255
- class_ids: int32 [1024], P('fil'), may hold values from 0 to 15
- seg_count: int32 [128], P('fil'), may hold values from 1 to 8, as said below
Outputs:
- scores: float32 [1024, 32, 128], P('fil', 'row')
- averages: float32 [16, 65536], P(None, ('row', 'fil'))
The draws below stay inside these ranges and needn't reach their ends.
Inputs may be any that keep to these rules, and one draw needn't show every extreme that they name: `seg_count`: each filament has its segments in the first slots of its 8; some filament has exactly 8.
All inputs are finite; a program needn't handle non-finite values.
Results may differ from the reference program's by a relative error of at most 0.0029.
Values may be sent and summed in bfloat16 or wider, within the bound.
No kernel may reach another device: no remote copies, remote signals or barrier semaphores. Data moves between devices by JAX's collectives and lax.ppermute only.
A program may use at most 128 MiB of HBM per device.

```python
import math
import jax
import jax.numpy as jnp
from jax import lax

FROWS = 256
FCOLS = 128
SHIFTS = 32
CLASSES = 16
SEG_FIL = 8
FILS = 128
SEGS = 1024
REFS = 128


def draw_seg_count(key, part):
    first = jax.random.fold_in(key, 11)
    second = jax.random.fold_in(key, 23)
    counts = jax.random.randint(first, (FILS,), 1, SEG_FIL + 1, dtype=jnp.int32)
    spot = jax.random.randint(second, (), 0, FILS, dtype=jnp.int32)
    return jnp.where(jnp.arange(FILS, dtype=jnp.int32) == spot, SEG_FIL, counts).astype(jnp.int32)


def place_ends(array, rng, least, largest):
    dims = array.shape
    index_at = [jax.random.randint(jax.random.fold_in(rng, axis), (), 0, dims[axis]) for axis in range(len(dims))]
    array = array.at[tuple(index_at)].set(least)
    longest = dims.index(max(dims))
    index_at[longest] = (index_at[longest] + 1) % dims[longest]
    return array.at[tuple(index_at)].set(largest)


def shard_levels(key, shape, shards, low, high):
    level, own = 1.0, jax.random.fold_in(key, 6)
    for dim, parts in shards:
        draws = jnp.exp(jax.random.uniform(jax.random.fold_in(own, dim), (parts,), jnp.float32, low / len(shards), high / len(shards)))
        level = level * jnp.repeat(draws, shape[dim] // parts).reshape([-1 if axis == dim else 1 for axis in range(len(shape))])
    return level


def bell_draw(own_key, shape, deviation, bound, pieces=(), held_as=jnp.bfloat16):
    factor_of = shard_levels(own_key, shape, pieces, -0.22, 0.18) if pieces else 1.0
    array = jax.random.normal(own_key, shape, jnp.float32) * deviation * factor_of
    return jnp.minimum(jnp.maximum(array, -bound), bound).astype(held_as)


def setup_inputs(seed: int = 0) -> dict:
    streams_of = jax.random.split(jax.random.key(seed), 8)
    return {
        "images": bell_draw(streams_of[0], (SEGS, 2, FROWS, FCOLS), 1.0, 6.0, ((0, 128), (2, 4))),
        "defocus": jnp.clip(jnp.exp(math.log(2.0) - 1.3862944 * jax.random.uniform(streams_of[1], (SEGS,), jnp.float32) ** shard_levels(streams_of[1], (SEGS,), ((0, 128),), -0.2, 0.2)), 0.5, 2.0),
        "references": bell_draw(streams_of[2], (REFS, 2, FROWS, FCOLS), (2 * FROWS * FCOLS) ** -0.5, 0.0234375, ((0, 128), (2, 4))),
        "offsets": place_ends(jax.random.randint(streams_of[3], (SEGS, SHIFTS, 2), -8, 9), jax.random.fold_in(streams_of[3], 1), -8, 8).astype(jnp.int32),
        "posterior": place_ends(jax.random.randint(streams_of[4], (SEGS, SHIFTS), 0, 256), jax.random.fold_in(streams_of[4], 1), 0, 255).astype(jnp.int32),
        "class_ids": place_ends(jax.random.randint(streams_of[5], (SEGS,), 0, CLASSES), jax.random.fold_in(streams_of[5], 1), 0, CLASSES - 1).astype(jnp.int32),
        "seg_count": draw_seg_count(jax.random.fold_in(streams_of[7], 71), 0),
    }


def wave_tables(shift_rows, shift_cols, row_freq, col_freq, box):
    row_angle = (shift_rows[..., None] * row_freq % box).astype(jnp.float32) * (-2.0 * math.pi / box)
    col_angle = (shift_cols[..., None] * col_freq % box).astype(jnp.float32) * (-2.0 * math.pi / box)
    row_cos = jnp.cos(row_angle)[..., :, None]
    row_sin = jnp.sin(row_angle)[..., :, None]
    col_cos = jnp.cos(col_angle)[..., None, :]
    col_sin = jnp.sin(col_angle)[..., None, :]
    phase_re = row_cos * col_cos - row_sin * col_sin
    phase_im = row_cos * col_sin + row_sin * col_cos
    return (phase_re, phase_im)

def contrast(defocus_vals, row_freq, col_freq, box):
    radius = (row_freq[:, None] * row_freq[:, None] + col_freq[None, :] * col_freq[None, :]).astype(jnp.float32) / float(box * box)
    return -jnp.sin(200.0 * defocus_vals[:, None, None] * radius[None] + 0.1)

def aligned_rows(block_images, gain, block_offsets, row_freq, col_freq, box):
    phase_re, phase_im = wave_tables(block_offsets[..., 0], block_offsets[..., 1], row_freq, col_freq, box)
    scaled = gain[:, None]
    real_part = block_images[:, 0].astype(jnp.float32)[:, None]
    imag_part = block_images[:, 1].astype(jnp.float32)[:, None]
    aligned_re = scaled * (real_part * phase_re - imag_part * phase_im)
    aligned_im = scaled * (real_part * phase_im + imag_part * phase_re)
    stacked = jnp.stack([aligned_re, aligned_im], axis=3).astype(jnp.bfloat16)
    return stacked.reshape(stacked.shape[0] * stacked.shape[1], -1)

def reference(images, defocus, references, offsets, posterior, class_ids, seg_count):
    segs = images.shape[0]
    box = FROWS
    rows = images.shape[2]
    cols = images.shape[3]
    row_freq = (jnp.arange(rows, dtype=jnp.int32) + box // 2) % box - box // 2
    col_freq = jnp.arange(cols, dtype=jnp.int32)
    live = (jnp.arange(SEG_FIL, dtype=jnp.int32)[None, :] < seg_count[:, None]).reshape(-1).astype(jnp.float32)
    weight = live[:, None] * posterior.astype(jnp.float32) / 256.0
    panel = jnp.transpose(references, (0, 2, 1, 3)).reshape(references.shape[0], -1)
    classes = jnp.arange(CLASSES, dtype=jnp.int32)
    blocks = segs // 8

    def step(carry, inputs):
        numer, denom = carry
        block_images, block_defocus, block_offsets, block_weight, block_live, block_ids = inputs
        ctf = contrast(block_defocus, row_freq, col_freq, box)
        aligned = aligned_rows(block_images, ctf * block_live[:, None, None], block_offsets, row_freq, col_freq, box)
        block_scores = lax.dot_general(aligned, panel, (((1,), (1,)), ((), ())), preferred_element_type=jnp.float32)
        member = (block_ids[None, :] == classes[:, None]).astype(jnp.float32)
        spread = (member[:, :, None] * block_weight[None]).astype(jnp.bfloat16).reshape(CLASSES, -1)
        numer = numer + jnp.dot(spread, aligned, preferred_element_type=jnp.float32)
        totals = member * lax.optimization_barrier(jnp.sum(block_weight, axis=1))[None, :]
        denom = denom + jnp.dot(totals, (ctf * ctf).reshape(ctf.shape[0], -1), precision=lax.Precision.HIGHEST, preferred_element_type=jnp.float32)
        return ((numer, denom), block_scores.reshape(8, SHIFTS, -1))
    inputs = (images.reshape(blocks, 8, 2, rows, cols), defocus.reshape(blocks, 8), offsets.reshape(blocks, 8, SHIFTS, 2), weight.reshape(blocks, 8, SHIFTS), live.reshape(blocks, 8), class_ids.reshape(blocks, 8))
    start = (jnp.zeros((CLASSES, rows * 2 * cols), jnp.float32), jnp.zeros((CLASSES, rows * cols), jnp.float32))
    (numer, denom), scores = lax.scan(step, start, inputs)
    wide = jnp.broadcast_to(denom.reshape(CLASSES, rows, 1, cols), (CLASSES, rows, 2, cols)).reshape(CLASSES, -1)
    averages = numer * lax.rsqrt(wide + 1.0)
    return (scores.reshape(segs, SHIFTS, -1), averages)
```

```python
import math

import jax
import jax.numpy as jnp
from jax import lax
from jax.experimental import pallas as pl
from jax.experimental.pallas import tpu as pltpu
from jax.sharding import Mesh
from jax.sharding import PartitionSpec as P

BOX = 256
SHIFTS = 32
CLASSES = 16
SEG = 8
NX = 4
NYZ = 32
KY = 16
COLS = 128
META = 16
FIL = ("x", "yh", "z")
ROW = ("yl", "core")
bf16 = jnp.bfloat16
f32 = jnp.float32


def small_sincos(theta):
    t2 = theta * theta
    sin = theta * (1.0 + t2 * (-1.0 / 6 + t2 * (1.0 / 120 + t2 * (-1.0 / 5040 + t2 * (1.0 / 362880)))))
    cos = 1.0 + t2 * (-0.5 + t2 * (1.0 / 24 + t2 * (-1.0 / 720 + t2 * (1.0 / 40320 + t2 * (-1.0 / 3628800)))))
    return sin, cos


def turn(m):
    n = jnp.floor(m * (1.0 / 64) + 0.5)
    sin, cos = small_sincos((m - 64.0 * n) * (math.pi / 128))
    quad = n - 4.0 * jnp.floor(n * 0.25)
    odd = (quad == 1.0) | (quad == 3.0)
    c = jnp.where(odd, sin, cos)
    s = jnp.where(odd, cos, sin)
    c = jnp.where((quad == 1.0) | (quad == 2.0), -c, c)
    s = jnp.where(quad >= 2.0, s, -s)
    return c, s


def align_kernel(kw_ref, img_ref, meta_ref, gain_ref, spread_ref, aligned_ref, numer_ref, x_ref):
    step = pl.program_id(0)
    kw0 = kw_ref[0].astype(f32)
    lane = lax.broadcasted_iota(jnp.int32, (SHIFTS, COLS), 1)
    sub = lax.broadcasted_iota(jnp.int32, (SHIFTS, COLS), 0)
    kx = lane.astype(f32)

    @pl.when(step == 0)
    def _():
        numer_ref[...] = jnp.zeros_like(numer_ref)

    def segment(i, carry):
        row = meta_ref[pl.ds(i, 1), :]
        wide = jnp.broadcast_to(row, (SHIFTS, COLS))
        sy = jnp.sum(jnp.where(lane == sub, wide, 0.0), axis=1, keepdims=True)
        sx = jnp.sum(jnp.where(lane == sub + SHIFTS, wide, 0.0), axis=1, keepdims=True)
        sy = jnp.broadcast_to(sy, (SHIFTS, COLS))
        pr, pi = turn(sy * kw0 + sx * kx)
        si, cr = small_sincos(sy * (-2.0 * math.pi / BOX))
        base = pl.multiple_of(i * 2 * KY, 2 * KY)
        img = img_ref[0, pl.ds(base, 2 * KY), :].astype(f32)
        gain = gain_ref[i]
        x_ref[0:KY, :] = img[0:KY] * gain
        x_ref[KY : 2 * KY, :] = img[KY : 2 * KY] * gain
        rows = pl.ds(pl.multiple_of(i * SHIFTS, SHIFTS), SHIFTS)
        for ky in range(KY):
            xr = x_ref[ky : ky + 1, :]
            xi = x_ref[KY + ky : KY + ky + 1, :]
            aligned_ref[rows, 2 * ky * COLS : (2 * ky + 1) * COLS] = (xr * pr - xi * pi).astype(bf16)
            aligned_ref[rows, (2 * ky + 1) * COLS : (2 * ky + 2) * COLS] = (xr * pi + xi * pr).astype(bf16)
            if ky < KY - 1:
                pr, pi = pr * cr - pi * si, pr * si + pi * cr
        return carry

    lax.fori_loop(0, SEG, segment, 0)
    part = jnp.dot(spread_ref[...], aligned_ref[...], preferred_element_type=f32)
    for d in range(2 * KY):
        numer_ref[d] += part[:, d * COLS : (d + 1) * COLS]


def align(kw0, recv, meta, gain, spread):
    segs = NX * SEG
    return pl.pallas_call(
        align_kernel,
        grid=(NX,),
        in_specs=[
            pl.BlockSpec(memory_space=pltpu.SMEM),
            pl.BlockSpec((1, SEG * 2 * KY, COLS), lambda j: (j, 0, 0)),
            pl.BlockSpec((SEG, COLS), lambda j: (j, 0)),
            pl.BlockSpec((SEG, KY, COLS), lambda j: (j, 0, 0)),
            pl.BlockSpec((CLASSES, SEG * SHIFTS), lambda j: (0, j)),
        ],
        out_specs=[
            pl.BlockSpec((SEG * SHIFTS, 2 * KY * COLS), lambda j: (j, 0)),
            pl.BlockSpec((2 * KY, CLASSES, COLS), lambda j: (0, 0, 0)),
        ],
        out_shape=[
            jax.ShapeDtypeStruct((segs * SHIFTS, 2 * KY * COLS), bf16),
            jax.ShapeDtypeStruct((2 * KY, CLASSES, COLS), f32),
        ],
        scratch_shapes=[pltpu.VMEM((2 * KY, COLS), f32)],
        compiler_params=pltpu.CompilerParams(vmem_limit_bytes=32 << 20),
        cost_estimate=pl.CostEstimate(flops=600_000_000, bytes_accessed=9_000_000, transcendentals=0),
        name="align",
    )(kw0, recv, meta, gain, spread)


def score_kernel(panel_ref, aligned_ref, out_ref, wide_ref, packed_ref):
    step = pl.program_id(0)
    rows = NX * 2 * KY

    @pl.when(step == 0)
    def _():
        def widen(j, carry):
            wide_ref[pl.ds(pl.multiple_of(j * rows, rows), rows), :] = panel_ref[j, 0:rows, :].astype(f32)
            return carry

        lax.fori_loop(0, NYZ, widen, 0)
        for d in range(2 * KY):
            parts = [wide_ref[pl.ds(x * 2 * KY + d, NYZ, stride=rows), :] for x in range(NX)]
            packed_ref[:, d * COLS : (d + 1) * COLS] = jnp.concatenate(parts, axis=0).astype(bf16)

    res = lax.dot_general(
        aligned_ref[...], packed_ref[...], (((1,), (1,)), ((), ())), preferred_element_type=f32
    )
    for i in range(SEG):
        for r in range(4):
            out_ref[0, r, i] = res[i * SHIFTS + r * 8 : i * SHIFTS + (r + 1) * 8, :]


def score(panel, aligned):
    refs = NX * NYZ
    return pl.pallas_call(
        score_kernel,
        grid=(NX,),
        in_specs=[
            pl.BlockSpec(panel.shape, lambda j: (0, 0, 0)),
            pl.BlockSpec((SEG * SHIFTS, 2 * KY * COLS), lambda j: (j, 0)),
        ],
        out_specs=pl.BlockSpec((1, 4, SEG, 8, refs), lambda j: (j, 0, 0, 0, 0)),
        out_shape=jax.ShapeDtypeStruct((NX, 4, SEG, 8, refs), f32),
        scratch_shapes=[
            pltpu.VMEM((NYZ * NX * 2 * KY, COLS), f32),
            pltpu.VMEM((refs, 2 * KY * COLS), bf16),
        ],
        compiler_params=pltpu.CompilerParams(vmem_limit_bytes=32 << 20),
        cost_estimate=pl.CostEstimate(flops=1_100_000_000, bytes_accessed=10_000_000, transcendentals=0),
        name="score",
    )(panel, aligned)


def three_parts(v):
    hi = lax.reduce_precision(v, 8, 7)
    rest = v - hi
    mid = lax.reduce_precision(rest, 8, 7)
    return hi, mid, rest - mid


def contrast(defocus, kw, kx):
    radius = (kw * kw + kx * kx).astype(f32) / float(BOX * BOX)
    return -jnp.sin(200.0 * defocus * radius + 0.1)


def per_device(images, defocus, references, offsets, posterior, class_ids, seg_count):
    row = lax.axis_index(ROW)
    my_x = lax.axis_index("x")
    fil = lax.axis_index(FIL)
    kx = jnp.arange(COLS, dtype=jnp.int32)

    live = (jnp.arange(SEG, dtype=jnp.int32) < seg_count[0]).astype(f32)
    weights = live[:, None] * posterior.astype(f32)
    scalars = jnp.stack([*three_parts(defocus), class_ids.astype(f32), live], axis=1)
    meta = jnp.concatenate(
        [offsets[:, :, 0].astype(f32), offsets[:, :, 1].astype(f32), weights, scalars], axis=1
    )
    meta = jnp.pad(meta, ((0, META - SEG), (0, COLS - meta.shape[1]))).astype(bf16)
    send = jnp.concatenate(
        [
            images.reshape(SEG, 2, NX, KY, COLS).transpose(2, 0, 1, 3, 4).reshape(NX, SEG * 2 * KY, COLS),
            references.reshape(2, NX, KY, COLS).transpose(1, 2, 0, 3).reshape(NX, 2 * KY, COLS),
            jnp.broadcast_to(meta[None], (NX, META, COLS)),
        ],
        axis=1,
    )
    recv = lax.all_to_all(send, "x", 0, 0, tiled=True)
    img_rows = SEG * 2 * KY
    own_refs = recv[:, img_rows : img_rows + 2 * KY]
    meta = recv[:, img_rows + 2 * KY : img_rows + 2 * KY + SEG].reshape(NX * SEG, COLS).astype(f32)
    weights = meta[:, 2 * SHIFTS : 3 * SHIFTS]
    own_defocus = meta[:, 96] + meta[:, 97] + meta[:, 98]
    own_class = meta[:, 99]
    own_live = meta[:, 100]

    ky_first = row * 64 + my_x * KY
    kw_first = (ky_first + BOX // 2) % BOX - BOX // 2
    kw = kw_first + jnp.arange(KY, dtype=jnp.int32)
    gain = contrast(own_defocus[:, None, None], kw[:, None], kx[None, :]) * own_live[:, None, None]
    classes = jnp.arange(CLASSES, dtype=f32)
    member = (own_class[None, :] == classes[:, None]).astype(f32)
    spread = (member[:, :, None] * (weights * (1.0 / 256))[None]).astype(bf16).reshape(CLASSES, -1)

    total = jnp.sum(weights, axis=1)
    total_hi = jnp.floor(total * (1.0 / 32))
    facts = jnp.stack(
        [meta[:, 96], meta[:, 97], meta[:, 98], total_hi, total - 32.0 * total_hi, own_class], axis=0
    )
    facts = jnp.pad(facts, ((0, META - 6), (0, COLS - NX * SEG))).astype(bf16)
    chunk = jnp.concatenate([own_refs.reshape(NX * 2 * KY, COLS), facts], axis=0)
    panel = lax.all_to_all(
        lax.optimization_barrier(jnp.broadcast_to(chunk[None], (NYZ, *chunk.shape))),
        ("yh", "z"), 0, 0, tiled=True,
    )

    aligned, numer = align(kw_first.reshape(1), recv, meta, gain, spread)
    partial = score(panel, aligned)
    partial = lax.all_to_all(partial.reshape(16, SEG * 8, COLS), ("x", *ROW), 0, 0, tiled=True)
    scores = jnp.sum(partial, axis=0).reshape(SEG, 8, COLS)

    numer = lax.all_to_all(numer, ("yh", "z"), 0, 0, tiled=True)
    numer = jnp.sum(numer, axis=0)

    facts = panel[:, NX * 2 * KY : NX * 2 * KY + 6, : NX * SEG].astype(f32)
    all_defocus = (facts[:, 0] + facts[:, 1] + facts[:, 2]).reshape(-1)
    all_total = ((facts[:, 3] * 32.0 + facts[:, 4]) * (1.0 / 256)).reshape(-1)
    all_class = facts[:, 5].reshape(-1)
    ky_mine = row * 64 + fil // 2
    kw_mine = (ky_mine + BOX // 2) % BOX - BOX // 2
    ctf = contrast(all_defocus[:, None], kw_mine, kx[None, :])
    totals = jnp.where(all_class[None, :] == classes[:, None], all_total[None, :], 0.0)
    denom = jnp.dot(totals, ctf * ctf, precision=lax.Precision.HIGHEST, preferred_element_type=f32)
    averages = numer * lax.rsqrt(denom + 1.0)
    return scores, averages


def solution(mesh):
    fine = Mesh(mesh.devices.reshape(4, 4, 8, 2, 2), (*FIL, *ROW))
    placed = (
        P(FIL, None, ROW, None),
        P(FIL),
        P(FIL, None, ROW, None),
        P(FIL, None, None),
        P(FIL, None),
        P(FIL),
        P(FIL),
    )
    return jax.shard_map(
        per_device,
        mesh=fine,
        in_specs=placed,
        out_specs=(P(FIL, ROW, None), P(None, (*ROW, *FIL))),
        check_vma=False,
    )
```

```python
import math

import jax
import jax.numpy as jnp
from jax import lax
from jax.experimental import pallas as pl
from jax.experimental.pallas import tpu as pltpu
from jax.sharding import Mesh
from jax.sharding import PartitionSpec as P

BOX = 256
SHIFTS = 32
CLASSES = 16
SEG = 8
NA = 8
NB = 16
NROW = 4
KY = 8
D = 2 * KY
COLS = 128
META = 16
FIL = ("x", "yh", "zh", "zl")
ROW = ("yl", "core")
bf16 = jnp.bfloat16
f32 = jnp.float32
PARTIAL = f32


def small_sincos(theta):
    t2 = theta * theta
    sin = theta * (1.0 + t2 * (-1.0 / 6 + t2 * (1.0 / 120 + t2 * (-1.0 / 5040 + t2 * (1.0 / 362880)))))
    cos = 1.0 + t2 * (-0.5 + t2 * (1.0 / 24 + t2 * (-1.0 / 720 + t2 * (1.0 / 40320 + t2 * (-1.0 / 3628800)))))
    return sin, cos


def turn(m):
    n = jnp.floor(m * (1.0 / 64) + 0.5)
    sin, cos = small_sincos((m - 64.0 * n) * (math.pi / 128))
    quad = n - 4.0 * jnp.floor(n * 0.25)
    odd = (quad == 1.0) | (quad == 3.0)
    c = jnp.where(odd, sin, cos)
    s = jnp.where(odd, cos, sin)
    c = jnp.where((quad == 1.0) | (quad == 2.0), -c, c)
    s = jnp.where(quad >= 2.0, s, -s)
    return c, s


def parts_of(v):
    hi = v.astype(bf16).astype(f32)
    rest = v - hi
    mid = rest.astype(bf16).astype(f32)
    return hi, mid, rest - mid


def pack_kernel(defocus_ref, class_ref, count_ref, img_ref, ref_ref, off_ref, post_ref, out_ref, meta_ref):
    sub = lax.broadcasted_iota(jnp.int32, (META, COLS), 0)
    lane = lax.broadcasted_iota(jnp.int32, (META, COLS), 1)
    live = (sub < count_ref[0]).astype(f32)
    defocus = jnp.zeros((META, COLS), f32)
    ids = jnp.zeros((META, COLS), f32)
    for i in range(SEG):
        defocus = jnp.where(sub == i, defocus_ref[i], defocus)
        ids = jnp.where(sub == i, class_ref[i].astype(f32), ids)
    hi, mid, low = parts_of(defocus)
    facts = jnp.where(lane == 96, hi, jnp.where(lane == 97, mid, jnp.where(lane == 98, low, 0.0)))
    facts = jnp.where(lane == 99, ids, jnp.where(lane == 100, live, facts))
    meta_ref[...] = facts
    for i in range(SEG):
        both = off_ref[i].astype(f32)
        meta_ref[i : i + 1, 0:SHIFTS] = both[0:1]
        meta_ref[i : i + 1, SHIFTS : 2 * SHIFTS] = both[1:2]
    meta_ref[0:SEG, 2 * SHIFTS : 3 * SHIFTS] = post_ref[...].astype(f32) * live[0:SEG, 0:SHIFTS]
    meta = meta_ref[...].astype(bf16)
    for j in range(NA):
        for p in range(2):
            for i in range(SEG):
                out_ref[j, i * D + p * KY : i * D + (p + 1) * KY] = img_ref[i, p, j * KY : (j + 1) * KY]
            base = SEG * D + p * KY
            out_ref[j, base : base + KY] = ref_ref[0, p, j * KY : (j + 1) * KY]
        out_ref[j, SEG * D + D : SEG * D + D + META] = meta


def pack(images, defocus, references, offsets, posterior, class_ids, seg_count):
    smem = pl.BlockSpec(memory_space=pltpu.SMEM)
    vmem = pl.BlockSpec(memory_space=pltpu.VMEM)
    return pl.pallas_call(
        pack_kernel,
        in_specs=[smem, smem, smem, vmem, vmem, vmem, vmem],
        out_specs=vmem,
        out_shape=jax.ShapeDtypeStruct((NA, SEG * D + D + META, COLS), bf16),
        scratch_shapes=[pltpu.VMEM((META, COLS), f32)],
        compiler_params=pltpu.CompilerParams(vmem_limit_bytes=4 << 20),
        cost_estimate=pl.CostEstimate(flops=100_000, bytes_accessed=700_000, transcendentals=0),
        name="pack",
    )(defocus, class_ids, seg_count, images, references, offsets.transpose(0, 2, 1), posterior)


def chunk_kernel(recv_ref, out_ref, meta_out_ref, wide_ref):
    first = SEG * D + D
    wide_ref[...] = jnp.zeros_like(wide_ref)
    for a in range(NA):
        meta = recv_ref[a, first : first + META, :].astype(f32)[0:SEG]
        wide_ref[a * SEG : (a + 1) * SEG] = meta
        meta_out_ref[a * SEG : (a + 1) * SEG] = meta
    flat = wide_ref[...].T
    total = jnp.sum(flat[2 * SHIFTS : 3 * SHIFTS], axis=0, keepdims=True)
    total_hi = jnp.floor(total * (1.0 / 32))
    sub = lax.broadcasted_iota(jnp.int32, (META, COLS), 0)
    facts = jnp.where(sub == 5, total_hi, jnp.where(sub == 6, total - 32.0 * total_hi, flat[96 : 96 + META]))
    facts = facts.astype(bf16)
    for q in range(NB):
        for a in range(NA):
            out_ref[q, a * D : (a + 1) * D] = recv_ref[a, SEG * D : SEG * D + D]
        out_ref[q, NA * D : NA * D + META] = facts


def chunk(recv):
    vmem = pl.BlockSpec(memory_space=pltpu.VMEM)
    return pl.pallas_call(
        chunk_kernel,
        in_specs=[vmem],
        out_specs=[vmem, vmem],
        out_shape=[
            jax.ShapeDtypeStruct((NB, NA * D + META, COLS), bf16),
            jax.ShapeDtypeStruct((NA * SEG, COLS), f32),
        ],
        scratch_shapes=[pltpu.VMEM((COLS, COLS), f32)],
        compiler_params=pltpu.CompilerParams(vmem_limit_bytes=4 << 20),
        cost_estimate=pl.CostEstimate(flops=100_000, bytes_accessed=1_000_000, transcendentals=0),
        name="chunk",
    )(recv)


def align_kernel(kw_ref, img_ref, meta_ref, gain_ref, spread_ref, aligned_ref, numer_ref, x_ref):
    step = pl.program_id(0)
    kw0 = kw_ref[0].astype(f32)
    lane = lax.broadcasted_iota(jnp.int32, (SHIFTS, COLS), 1)
    sub = lax.broadcasted_iota(jnp.int32, (SHIFTS, COLS), 0)
    kx = lane.astype(f32)

    @pl.when(step == 0)
    def _():
        numer_ref[...] = jnp.zeros_like(numer_ref)

    def segment(i, carry):
        row = meta_ref[pl.ds(i, 1), :]
        wide = jnp.broadcast_to(row, (SHIFTS, COLS))
        sy = jnp.sum(jnp.where(lane == sub, wide, 0.0), axis=1, keepdims=True)
        sx = jnp.sum(jnp.where(lane == sub + SHIFTS, wide, 0.0), axis=1, keepdims=True)
        sy = jnp.broadcast_to(sy, (SHIFTS, COLS))
        pr, pi = turn(sy * kw0 + sx * kx)
        si, cr = small_sincos(sy * (-2.0 * math.pi / BOX))
        img = img_ref[0, pl.ds(pl.multiple_of(i * D, D), D), :].astype(f32)
        gain = gain_ref[i]
        x_ref[0:KY, :] = img[0:KY] * gain
        x_ref[KY:D, :] = img[KY:D] * gain
        rows = pl.ds(pl.multiple_of(i * SHIFTS, SHIFTS), SHIFTS)
        for ky in range(KY):
            xr = x_ref[ky : ky + 1, :]
            xi = x_ref[KY + ky : KY + ky + 1, :]
            aligned_ref[rows, ky * COLS : (ky + 1) * COLS] = (xr * pr - xi * pi).astype(bf16)
            aligned_ref[rows, (KY + ky) * COLS : (KY + ky + 1) * COLS] = (xr * pi + xi * pr).astype(bf16)
            if ky < KY - 1:
                pr, pi = pr * cr - pi * si, pr * si + pi * cr
        return carry

    lax.fori_loop(0, SEG, segment, 0)
    part = jnp.dot(spread_ref[...], aligned_ref[...], preferred_element_type=f32)
    for d in range(D):
        numer_ref[d] += part[:, d * COLS : (d + 1) * COLS]


def align(kw0, recv, meta, gain, spread):
    return pl.pallas_call(
        align_kernel,
        grid=(NA,),
        in_specs=[
            pl.BlockSpec(memory_space=pltpu.SMEM),
            pl.BlockSpec((1, SEG * D, COLS), lambda j: (j, 0, 0)),
            pl.BlockSpec((SEG, COLS), lambda j: (j, 0)),
            pl.BlockSpec((SEG, KY, COLS), lambda j: (j, 0, 0)),
            pl.BlockSpec((CLASSES, SEG * SHIFTS), lambda j: (0, j)),
        ],
        out_specs=[
            pl.BlockSpec((SEG * SHIFTS, D * COLS), lambda j: (j, 0)),
            pl.BlockSpec((D, CLASSES, COLS), lambda j: (0, 0, 0)),
        ],
        out_shape=[
            jax.ShapeDtypeStruct((NA * SEG * SHIFTS, D * COLS), bf16),
            jax.ShapeDtypeStruct((D, CLASSES, COLS), f32),
        ],
        scratch_shapes=[pltpu.VMEM((D, COLS), f32)],
        compiler_params=pltpu.CompilerParams(vmem_limit_bytes=57 << 20),
        cost_estimate=pl.CostEstimate(flops=600_000_000, bytes_accessed=9_000_000, transcendentals=0),
        name="align",
    )(kw0, recv, meta, gain, spread)


def score_kernel(panel_ref, aligned_ref, out_ref, wide_ref, packed_ref):
    step = pl.program_id(0)
    refs = NA * NB

    @pl.when(step == 0)
    def _():
        def widen(q, carry):
            for x in range(4):
                for zl in range(2):
                    a = 2 * x + zl
                    base = pl.multiple_of((x * 2 * NB + zl) * D + q * 2 * D, D)
                    wide_ref[pl.ds(base, D), :] = panel_ref[q, a * D : (a + 1) * D, :].astype(f32)
            return carry

        lax.fori_loop(0, NB, widen, 0)
        for d in range(D):
            packed_ref[:, d * COLS : (d + 1) * COLS] = wide_ref[pl.ds(d, refs, stride=D), :].astype(bf16)

    res = lax.dot_general(
        aligned_ref[...], packed_ref[...], (((1,), (1,)), ((), ())), preferred_element_type=f32
    )
    for i in range(SEG):
        for r in range(NROW):
            out_ref[0, r, i] = res[i * SHIFTS + r * 8 : i * SHIFTS + (r + 1) * 8, :].astype(out_ref.dtype)


def score(panel, aligned):
    refs = NA * NB
    return pl.pallas_call(
        score_kernel,
        grid=(NA,),
        in_specs=[
            pl.BlockSpec(panel.shape, lambda j: (0, 0, 0)),
            pl.BlockSpec((SEG * SHIFTS, D * COLS), lambda j: (j, 0)),
        ],
        out_specs=pl.BlockSpec((1, NROW, SEG, 8, refs), lambda j: (j, 0, 0, 0, 0)),
        out_shape=jax.ShapeDtypeStruct((NA, NROW, SEG, 8, refs), PARTIAL),
        scratch_shapes=[
            pltpu.VMEM((refs * D, COLS), f32),
            pltpu.VMEM((refs, D * COLS), bf16),
        ],
        compiler_params=pltpu.CompilerParams(vmem_limit_bytes=57 << 20),
        cost_estimate=pl.CostEstimate(flops=1_100_000_000, bytes_accessed=10_000_000, transcendentals=0),
        name="score",
    )(panel, aligned)


def contrast(defocus, kw, kx):
    radius = (kw * kw + kx * kx).astype(f32) / float(BOX * BOX)
    return -jnp.sin(200.0 * defocus * radius + 0.1)


def centred(ky):
    return (ky + BOX // 2) % BOX - BOX // 2


def per_device(images, defocus, references, offsets, posterior, class_ids, seg_count):
    row = lax.axis_index(ROW)
    group = lax.axis_index(("x", "zl"))
    fil = lax.axis_index(FIL)
    kx = jnp.arange(COLS, dtype=jnp.int32)

    send = pack(images, defocus, references, offsets, posterior, class_ids, seg_count)
    recv = lax.all_to_all(send, ("x", "zl"), 0, 0, tiled=True)
    sent_refs, meta = chunk(recv)
    panel = lax.all_to_all(sent_refs, ("yh", "zh"), 0, 0, tiled=True)

    weights = meta[:, 2 * SHIFTS : 3 * SHIFTS]
    own_defocus = meta[:, 96] + meta[:, 97] + meta[:, 98]
    own_class = meta[:, 99]
    own_live = meta[:, 100]
    kw_first = centred(row * 64 + group * KY)
    kw = kw_first + jnp.arange(KY, dtype=jnp.int32)
    gain = contrast(own_defocus[:, None, None], kw[:, None], kx[None, :]) * own_live[:, None, None]
    classes = jnp.arange(CLASSES, dtype=f32)
    member = (own_class[None, :] == classes[:, None]).astype(f32)
    spread = (member[:, :, None] * (weights * (1.0 / 256))[None]).astype(bf16).reshape(CLASSES, -1)

    aligned, numer = align(kw_first.reshape(1), recv, meta, gain, spread)
    numer = lax.all_to_all(numer, ("yh", "zh"), 0, 0, tiled=True)
    partial = score(panel, aligned)
    partial = lax.all_to_all(
        partial.reshape(NA * NROW, SEG * 8, COLS), ("x", "zl", *ROW), 0, 0, tiled=True
    )
    scores = jnp.sum(partial.astype(f32), axis=0).reshape(SEG, 8, COLS)

    numer = jnp.sum(numer, axis=0)
    swap = [
        (((hi * 2 + lo) * 4 + zh) * 2 + zl, ((zl * 2 + lo) * 4 + zh) * 2 + hi)
        for hi in range(2) for lo in range(2) for zh in range(4) for zl in range(2)
    ]
    numer = lax.ppermute(numer, ("yh", "zh", "zl"), swap)

    facts = panel[:, NA * D : NA * D + 7, : NA * SEG].astype(f32)
    all_defocus = (facts[:, 0] + facts[:, 1] + facts[:, 2]).reshape(-1)
    all_class = facts[:, 3].reshape(-1)
    all_total = ((facts[:, 5] * 32.0 + facts[:, 6]) * (1.0 / 256)).reshape(-1)
    ctf = contrast(all_defocus[:, None], centred(row * 64 + fil // 2), kx[None, :])
    totals = jnp.where(all_class[None, :] == classes[:, None], all_total[None, :], 0.0)
    denom = jnp.dot(totals, ctf * ctf, precision=lax.Precision.HIGHEST, preferred_element_type=f32)
    averages = numer * lax.rsqrt(denom + 1.0)
    return scores, averages


def solution(mesh):
    fine = Mesh(mesh.devices.reshape(4, 4, 4, 2, 2, 2), (*FIL, *ROW))
    placed = (
        P(FIL, None, ROW, None),
        P(FIL),
        P(FIL, None, ROW, None),
        P(FIL, None, None),
        P(FIL, None),
        P(FIL),
        P(FIL),
    )
    return jax.shard_map(
        per_device,
        mesh=fine,
        in_specs=placed,
        out_specs=(P(FIL, ROW, None), P(None, (*ROW, *FIL))),
        check_vma=False,
    )
```

```python
import math

import jax
import jax.numpy as jnp
from jax import lax
from jax.experimental import pallas as pl
from jax.experimental.pallas import tpu as pltpu
from jax.sharding import Mesh
from jax.sharding import PartitionSpec as P

BOX = 256
SHIFTS = 32
CLASSES = 16
SEG = 8
NA = 8
NB = 16
NROW = 4
KY = 8
D = 2 * KY
COLS = 128
META = 16
FIL = ("x", "yh", "zh", "zl")
ROW = ("yl", "core")
bf16 = jnp.bfloat16
f32 = jnp.float32
PARTIAL = bf16


def small_sincos(theta):
    t2 = theta * theta
    sin = theta * (1.0 + t2 * (-1.0 / 6 + t2 * (1.0 / 120 + t2 * (-1.0 / 5040 + t2 * (1.0 / 362880)))))
    cos = 1.0 + t2 * (-0.5 + t2 * (1.0 / 24 + t2 * (-1.0 / 720 + t2 * (1.0 / 40320 + t2 * (-1.0 / 3628800)))))
    return sin, cos


def turn(m):
    n = jnp.floor(m * (1.0 / 64) + 0.5)
    sin, cos = small_sincos((m - 64.0 * n) * (math.pi / 128))
    quad = n - 4.0 * jnp.floor(n * 0.25)
    odd = (quad == 1.0) | (quad == 3.0)
    c = jnp.where(odd, sin, cos)
    s = jnp.where(odd, cos, sin)
    c = jnp.where((quad == 1.0) | (quad == 2.0), -c, c)
    s = jnp.where(quad >= 2.0, s, -s)
    return c, s


def parts_of(v):
    hi = v.astype(bf16).astype(f32)
    rest = v - hi
    mid = rest.astype(bf16).astype(f32)
    return hi, mid, rest - mid


def pack_kernel(*refs):
    count_ref, given, out_ref, held, meta_ref, sems = refs[0], refs[1:7], refs[7], refs[8:14], refs[14], refs[15]
    copies = [pltpu.make_async_copy(src, dst, sems.at[k]) for k, (src, dst) in enumerate(zip(given, held))]
    for copy in copies:
        copy.start()
    for copy in copies:
        copy.wait()
    defocus_ref, class_ref, img_ref, ref_ref, off_ref, post_ref = held
    sub = lax.broadcasted_iota(jnp.int32, (META, COLS), 0)
    lane = lax.broadcasted_iota(jnp.int32, (META, COLS), 1)
    live = (sub < count_ref[0]).astype(f32)
    defocus = jnp.zeros((META, COLS), f32)
    ids = jnp.zeros((META, COLS), f32)
    for i in range(SEG):
        defocus = jnp.where(sub == i, defocus_ref[i], defocus)
        ids = jnp.where(sub == i, class_ref[i].astype(f32), ids)
    hi, mid, low = parts_of(defocus)
    facts = jnp.where(lane == 96, hi, jnp.where(lane == 97, mid, jnp.where(lane == 98, low, 0.0)))
    facts = jnp.where(lane == 99, ids, jnp.where(lane == 100, live, facts))
    meta_ref[...] = facts
    for i in range(SEG):
        both = off_ref[i].astype(f32)
        meta_ref[i : i + 1, 0:SHIFTS] = both[0:1]
        meta_ref[i : i + 1, SHIFTS : 2 * SHIFTS] = both[1:2]
    meta_ref[0:SEG, 2 * SHIFTS : 3 * SHIFTS] = post_ref[...].astype(f32) * live[0:SEG, 0:SHIFTS]
    meta = meta_ref[...].astype(bf16)
    for j in range(NA):
        for p in range(2):
            for i in range(SEG):
                out_ref[j, i * D + p * KY : i * D + (p + 1) * KY] = img_ref[i, p, j * KY : (j + 1) * KY]
            base = SEG * D + p * KY
            out_ref[j, base : base + KY] = ref_ref[0, p, j * KY : (j + 1) * KY]
        out_ref[j, SEG * D + D : SEG * D + D + META] = meta


def pack(images, defocus, references, offsets, posterior, class_ids, seg_count):
    given = (defocus, class_ids, images, references, offsets.transpose(0, 2, 1), posterior)
    places = (pltpu.SMEM,) * 2 + (pltpu.VMEM,) * 4
    return pl.pallas_call(
        pack_kernel,
        in_specs=[pl.BlockSpec(memory_space=pltpu.SMEM)] + [pl.BlockSpec(memory_space=pltpu.HBM)] * 6,
        out_specs=pl.BlockSpec(memory_space=pltpu.VMEM),
        out_shape=jax.ShapeDtypeStruct((NA, SEG * D + D + META, COLS), bf16),
        scratch_shapes=[place(v.shape, v.dtype) for place, v in zip(places, given)]
        + [pltpu.VMEM((META, COLS), f32), pltpu.SemaphoreType.DMA((6,))],
        compiler_params=pltpu.CompilerParams(vmem_limit_bytes=63 << 20),
        cost_estimate=pl.CostEstimate(flops=100_000, bytes_accessed=700_000, transcendentals=0),
        name="pack",
    )(seg_count, *given)


def chunk_kernel(recv_ref, out_ref, meta_out_ref, wide_ref):
    first = SEG * D + D
    wide_ref[...] = jnp.zeros_like(wide_ref)
    for a in range(NA):
        meta = recv_ref[a, first : first + META, :].astype(f32)[0:SEG]
        wide_ref[a * SEG : (a + 1) * SEG] = meta
        meta_out_ref[a * SEG : (a + 1) * SEG] = meta
    flat = wide_ref[...].T
    total = jnp.sum(flat[2 * SHIFTS : 3 * SHIFTS], axis=0, keepdims=True)
    total_hi = jnp.floor(total * (1.0 / 32))
    sub = lax.broadcasted_iota(jnp.int32, (META, COLS), 0)
    facts = jnp.where(sub == 5, total_hi, jnp.where(sub == 6, total - 32.0 * total_hi, flat[96 : 96 + META]))
    facts = facts.astype(bf16)
    for q in range(NB):
        for a in range(NA):
            out_ref[q, a * D : (a + 1) * D] = recv_ref[a, SEG * D : SEG * D + D]
        out_ref[q, NA * D : NA * D + META] = facts


def chunk(recv):
    vmem = pl.BlockSpec(memory_space=pltpu.VMEM)
    return pl.pallas_call(
        chunk_kernel,
        in_specs=[vmem],
        out_specs=[vmem, vmem],
        out_shape=[
            jax.ShapeDtypeStruct((NB, NA * D + META, COLS), bf16),
            jax.ShapeDtypeStruct((NA * SEG, COLS), f32),
        ],
        scratch_shapes=[pltpu.VMEM((COLS, COLS), f32)],
        compiler_params=pltpu.CompilerParams(vmem_limit_bytes=4 << 20),
        cost_estimate=pl.CostEstimate(flops=100_000, bytes_accessed=1_000_000, transcendentals=0),
        name="chunk",
    )(recv)


def align_kernel(kw_ref, img_ref, meta_ref, gain_ref, spread_ref, aligned_ref, numer_ref, x_ref):
    step = pl.program_id(0)
    kw0 = kw_ref[0].astype(f32)
    owned = kw_ref[1] * D
    lane = lax.broadcasted_iota(jnp.int32, (SHIFTS, COLS), 1)
    sub = lax.broadcasted_iota(jnp.int32, (SHIFTS, COLS), 0)
    kx = lane.astype(f32)

    @pl.when(step == 0)
    def _():
        numer_ref[...] = jnp.zeros_like(numer_ref)

    def segment(i, carry):
        row = meta_ref[pl.ds(i, 1), :]
        wide = jnp.broadcast_to(row, (SHIFTS, COLS))
        sy = jnp.sum(jnp.where(lane == sub, wide, 0.0), axis=1, keepdims=True)
        sx = jnp.sum(jnp.where(lane == sub + SHIFTS, wide, 0.0), axis=1, keepdims=True)
        sy = jnp.broadcast_to(sy, (SHIFTS, COLS))
        pr, pi = turn(sy * kw0 + sx * kx)
        si, cr = small_sincos(sy * (-2.0 * math.pi / BOX))
        img = img_ref[0, pl.ds(pl.multiple_of(i * D, D), D), :].astype(f32)
        gain = gain_ref[i]
        x_ref[0:KY, :] = img[0:KY] * gain
        x_ref[KY:D, :] = img[KY:D] * gain
        rows = pl.ds(pl.multiple_of(i * SHIFTS, SHIFTS), SHIFTS)
        for ky in range(KY):
            xr = x_ref[ky : ky + 1, :]
            xi = x_ref[KY + ky : KY + ky + 1, :]
            aligned_ref[rows, ky * COLS : (ky + 1) * COLS] = (xr * pr - xi * pi).astype(bf16)
            aligned_ref[rows, (KY + ky) * COLS : (KY + ky + 1) * COLS] = (xr * pi + xi * pr).astype(bf16)
            if ky < KY - 1:
                pr, pi = pr * cr - pi * si, pr * si + pi * cr
        return carry

    lax.fori_loop(0, SEG, segment, 0)
    part = jnp.dot(spread_ref[...], aligned_ref[...], preferred_element_type=f32)
    for p in range(2):
        for ky in range(KY):
            d = p * KY + ky
            numer_ref[owned + 2 * ky + p] += part[:, d * COLS : (d + 1) * COLS]


def align(kw0, recv, meta, gain, spread):
    return pl.pallas_call(
        align_kernel,
        grid=(NA,),
        in_specs=[
            pl.BlockSpec(memory_space=pltpu.SMEM),
            pl.BlockSpec((1, SEG * D, COLS), lambda j: (j, 0, 0)),
            pl.BlockSpec((SEG, COLS), lambda j: (j, 0)),
            pl.BlockSpec((SEG, KY, COLS), lambda j: (j, 0, 0)),
            pl.BlockSpec((CLASSES, SEG * SHIFTS), lambda j: (0, j)),
        ],
        out_specs=[
            pl.BlockSpec((SEG * SHIFTS, D * COLS), lambda j: (j, 0)),
            pl.BlockSpec((2 * D, CLASSES, COLS), lambda j: (0, 0, 0)),
        ],
        out_shape=[
            jax.ShapeDtypeStruct((NA * SEG * SHIFTS, D * COLS), bf16),
            jax.ShapeDtypeStruct((2 * D, CLASSES, COLS), f32),
        ],
        scratch_shapes=[pltpu.VMEM((D, COLS), f32)],
        compiler_params=pltpu.CompilerParams(vmem_limit_bytes=57 << 20),
        cost_estimate=pl.CostEstimate(flops=600_000_000, bytes_accessed=9_000_000, transcendentals=0),
        name="align",
    )(kw0, recv, meta, gain, spread)


def score_kernel(panel_ref, aligned_ref, out_ref, wide_ref, packed_ref):
    step = pl.program_id(0)
    refs = NA * NB

    @pl.when(step == 0)
    def _():
        def widen(q, carry):
            for x in range(4):
                for zl in range(2):
                    a = 2 * x + zl
                    base = pl.multiple_of((x * 2 * NB + zl) * D + q * 2 * D, D)
                    wide_ref[pl.ds(base, D), :] = panel_ref[q, a * D : (a + 1) * D, :].astype(f32)
            return carry

        lax.fori_loop(0, NB, widen, 0)
        for d in range(D):
            packed_ref[d * COLS : (d + 1) * COLS, :] = wide_ref[pl.ds(d, refs, stride=D), :].T.astype(bf16)

    res = jnp.dot(aligned_ref[...], packed_ref[...], preferred_element_type=f32)
    for i in range(SEG):
        for r in range(NROW):
            out_ref[0, r, i] = res[i * SHIFTS + r * 8 : i * SHIFTS + (r + 1) * 8, :].astype(out_ref.dtype)


def score(panel, aligned):
    refs = NA * NB
    return pl.pallas_call(
        score_kernel,
        grid=(NA,),
        in_specs=[
            pl.BlockSpec(panel.shape, lambda j: (0, 0, 0)),
            pl.BlockSpec((SEG * SHIFTS, D * COLS), lambda j: (j, 0)),
        ],
        out_specs=pl.BlockSpec((1, NROW, SEG, 8, refs), lambda j: (j, 0, 0, 0, 0)),
        out_shape=jax.ShapeDtypeStruct((NA, NROW, SEG, 8, refs), PARTIAL),
        scratch_shapes=[
            pltpu.VMEM((refs * D, COLS), f32),
            pltpu.VMEM((D * COLS, refs), bf16),
        ],
        compiler_params=pltpu.CompilerParams(vmem_limit_bytes=57 << 20),
        cost_estimate=pl.CostEstimate(flops=1_100_000_000, bytes_accessed=10_000_000, transcendentals=0),
        name="score",
    )(panel, aligned)


def contrast(defocus, kw, kx):
    radius = (kw * kw + kx * kx).astype(f32) / float(BOX * BOX)
    return -jnp.sin(200.0 * defocus * radius + 0.1)


def centred(ky):
    return (ky + BOX // 2) % BOX - BOX // 2


def per_device(images, defocus, references, offsets, posterior, class_ids, seg_count):
    row = lax.axis_index(ROW)
    group = lax.axis_index(("x", "zl"))
    fil = lax.axis_index(FIL)
    kx = jnp.arange(COLS, dtype=jnp.int32)

    send = pack(images, defocus, references, offsets, posterior, class_ids, seg_count)
    recv = lax.all_to_all(send, ("x", "zl"), 0, 0, tiled=True)
    sent_refs, meta = chunk(recv)
    panel = lax.all_to_all(sent_refs, ("yh", "zh"), 0, 0, tiled=True)

    weights = meta[:, 2 * SHIFTS : 3 * SHIFTS]
    own_defocus = meta[:, 96] + meta[:, 97] + meta[:, 98]
    own_class = meta[:, 99]
    own_live = meta[:, 100]
    kw_first = centred(row * 64 + group * KY)
    kw = kw_first + jnp.arange(KY, dtype=jnp.int32)
    gain = contrast(own_defocus[:, None, None], kw[:, None], kx[None, :]) * own_live[:, None, None]
    classes = jnp.arange(CLASSES, dtype=f32)
    member = (own_class[None, :] == classes[:, None]).astype(f32)
    spread = (member[:, :, None] * (weights * (1.0 / 256))[None]).astype(bf16).reshape(CLASSES, -1)

    aligned, numer = align(jnp.stack([kw_first, lax.axis_index("zl")]), recv, meta, gain, spread)
    numer = lax.all_to_all(numer, ("yh", "zh", "zl"), 0, 0, tiled=True)
    partial = score(panel, aligned)
    partial = lax.all_to_all(
        partial.reshape(NA * NROW, SEG * 8, COLS), ("x", "zl", *ROW), 0, 0, tiled=True
    )
    scores = jnp.sum(partial.astype(f32), axis=0).reshape(SEG, 8, COLS)

    numer = jnp.sum(numer, axis=0)

    facts = panel[:, NA * D : NA * D + 7, : NA * SEG].astype(f32)
    all_defocus = (facts[:, 0] + facts[:, 1] + facts[:, 2]).reshape(-1)
    all_class = facts[:, 3].reshape(-1)
    all_total = ((facts[:, 5] * 32.0 + facts[:, 6]) * (1.0 / 256)).reshape(-1)
    ctf = contrast(all_defocus[:, None], centred(row * 64 + fil // 2), kx[None, :])
    totals = jnp.where(all_class[None, :] == classes[:, None], all_total[None, :], 0.0)
    denom = jnp.dot(totals, ctf * ctf, precision=lax.Precision.HIGHEST, preferred_element_type=f32)
    averages = numer * lax.rsqrt(denom + 1.0)
    return scores, averages


def solution(mesh):
    fine = Mesh(mesh.devices.reshape(4, 4, 4, 2, 2, 2), (*FIL, *ROW))
    placed = (
        P(FIL, None, ROW, None),
        P(FIL),
        P(FIL, None, ROW, None),
        P(FIL, None, None),
        P(FIL, None),
        P(FIL),
        P(FIL),
    )
    return jax.shard_map(
        per_device,
        mesh=fine,
        in_specs=placed,
        out_specs=(P(FIL, ROW, None), P(None, (*ROW, *FIL))),
        check_vma=False,
    )
```

```python
import math

import jax
import jax.numpy as jnp
from jax import lax
from jax.experimental import pallas as pl
from jax.experimental.pallas import tpu as pltpu
from jax.sharding import Mesh
from jax.sharding import PartitionSpec as P

BOX = 256
SHIFTS = 32
CLASSES = 16
SEG = 8
NA = 8
NB = 32
NX = 4
NROW = 4
SEGS = NA * SEG
KY = 8
D = 2 * KY
COLS = 128
META = 8
A_REF = SEG * D
A_META = A_REF + 2 * D
A_ROWS = A_META + META
B_NUM = NX * D
B_FACT = B_NUM + CLASSES
B_ROWS = B_FACT + META
FIL = ("x", "yh", "zh", "zl")
ROW = ("yl", "core")
bf16 = jnp.bfloat16
f32 = jnp.float32
PARTIAL = bf16


def small_sincos(theta):
    t2 = theta * theta
    sin = theta * (1.0 + t2 * (-1.0 / 6 + t2 * (1.0 / 120 + t2 * (-1.0 / 5040 + t2 * (1.0 / 362880)))))
    cos = 1.0 + t2 * (-0.5 + t2 * (1.0 / 24 + t2 * (-1.0 / 720 + t2 * (1.0 / 40320 + t2 * (-1.0 / 3628800)))))
    return sin, cos


def quarter(n, sin, cos):
    quad = n - 4.0 * jnp.floor(n * 0.25)
    odd = (quad == 1.0) | (quad == 3.0)
    c = jnp.where(odd, sin, cos)
    s = jnp.where(odd, cos, sin)
    c = jnp.where((quad == 1.0) | (quad == 2.0), -c, c)
    return jnp.where(quad >= 2.0, -s, s), c


def turn(m):
    n = jnp.floor(m * (1.0 / 64) + 0.5)
    sin, cos = quarter(n, *small_sincos((m - 64.0 * n) * (math.pi / 128)))
    return cos, -sin


def sine(arg):
    n = jnp.floor(arg * (2.0 / math.pi) + 0.5)
    rest = ((arg - n * 1.5703125) - n * 4.837512969970703125e-4) - n * 7.54978995489188216e-8
    return quarter(n, *small_sincos(rest))[0]


def halves(v):
    hi = v.astype(bf16)
    return hi, (v - hi.astype(f32)).astype(bf16)


def parts_of(v):
    hi = v.astype(bf16).astype(f32)
    rest = v - hi
    mid = rest.astype(bf16).astype(f32)
    return hi, mid, rest - mid


def pack_kernel(*refs):
    count_ref, given, out_ref, held, meta_ref, sems = refs[0], refs[1:7], refs[7], refs[8:14], refs[14], refs[15]
    copies = [pltpu.make_async_copy(src, dst, sems.at[k]) for k, (src, dst) in enumerate(zip(given, held))]
    for copy in copies:
        copy.start()
    for copy in copies:
        copy.wait()
    defocus_ref, class_ref, img_ref, ref_ref, off_ref, post_ref = held
    sub = lax.broadcasted_iota(jnp.int32, (META, COLS), 0)
    lane = lax.broadcasted_iota(jnp.int32, (META, COLS), 1)
    live = (sub < count_ref[0]).astype(f32)
    defocus = jnp.zeros((META, COLS), f32)
    ids = jnp.zeros((META, COLS), f32)
    for i in range(SEG):
        defocus = jnp.where(sub == i, defocus_ref[i], defocus)
        ids = jnp.where(sub == i, class_ref[i].astype(f32), ids)
    hi, mid, low = parts_of(defocus)
    facts = jnp.where(lane == 96, hi, jnp.where(lane == 97, mid, jnp.where(lane == 98, low, 0.0)))
    facts = jnp.where(lane == 99, ids, jnp.where(lane == 100, live, facts))
    meta_ref[...] = facts
    for i in range(SEG):
        both = off_ref[i].astype(f32)
        meta_ref[i : i + 1, 0:SHIFTS] = both[0:1]
        meta_ref[i : i + 1, SHIFTS : 2 * SHIFTS] = both[1:2]
    meta_ref[0:SEG, 2 * SHIFTS : 3 * SHIFTS] = post_ref[...].astype(f32) * live[0:SEG, 0:SHIFTS]
    meta = meta_ref[...].astype(bf16)
    for j in range(NA):
        for p in range(2):
            for i in range(SEG):
                out_ref[j, i * D + p * KY : i * D + (p + 1) * KY] = img_ref[i, p, j * KY : (j + 1) * KY]
            for half in range(2):
                base = A_REF + half * D + p * KY
                first = (j // 2) * 2 * KY + half * KY
                out_ref[j, base : base + KY] = ref_ref[0, p, first : first + KY]
        out_ref[j, A_META:A_ROWS] = meta


def pack(images, defocus, references, offsets, posterior, class_ids, seg_count):
    given = (defocus, class_ids, images, references, offsets.transpose(0, 2, 1), posterior)
    places = (pltpu.SMEM,) * 2 + (pltpu.VMEM,) * 4
    return pl.pallas_call(
        pack_kernel,
        in_specs=[pl.BlockSpec(memory_space=pltpu.SMEM)] + [pl.BlockSpec(memory_space=pltpu.HBM)] * 6,
        out_specs=pl.BlockSpec(memory_space=pltpu.VMEM),
        out_shape=jax.ShapeDtypeStruct((NA, A_ROWS, COLS), bf16),
        scratch_shapes=[place(v.shape, v.dtype) for place, v in zip(places, given)]
        + [pltpu.VMEM((META, COLS), f32), pltpu.SemaphoreType.DMA((6,))],
        compiler_params=pltpu.CompilerParams(vmem_limit_bytes=63 << 20),
        cost_estimate=pl.CostEstimate(flops=100_000, bytes_accessed=700_000, transcendentals=0),
        name="pack",
    )(seg_count, *given)


def front_kernel(place_ref, recv_ref, out_ref, meta_out_ref, gx_ref, wide_ref, y_ref, col_ref):
    kw0 = place_ref[0]
    zl = place_ref[1]
    lane = lax.broadcasted_iota(jnp.int32, (KY, COLS), 1)
    sub = lax.broadcasted_iota(jnp.int32, (KY, COLS), 0)
    kw = (sub + kw0).astype(f32)
    kx = lane.astype(f32)
    radius = (kw * kw + kx * kx) * (1.0 / (BOX * BOX))
    first = (lane % (2 * SHIFTS)) < SHIFTS
    lane_s = lax.broadcasted_iota(jnp.int32, (SHIFTS, COLS), 1)
    sub_s = lax.broadcasted_iota(jnp.int32, (SHIFTS, COLS), 0)

    c, s = turn((sub_s - 8).astype(f32) * lane_s.astype(f32))
    (c_hi, c_lo), (s_hi, s_lo) = halves(c), halves(s)
    table = jnp.concatenate([c_hi, s_hi, c_lo, s_lo], axis=1)

    for a in range(NA):
        meta = recv_ref[a, A_META:A_ROWS].astype(f32)
        rows = slice(a * SEG, (a + 1) * SEG)
        meta_out_ref[rows] = meta
        wide_ref[rows] = meta
        wide_ref[SEGS + a * SEG : SEGS + (a + 1) * SEG] = meta

        def pick(at):
            return jnp.sum(jnp.where(lane == at, meta, 0.0), axis=1, keepdims=True)

        defocus = jnp.broadcast_to(pick(96) + pick(97) + pick(98), (SEG, COLS))
        alive = jnp.broadcast_to(pick(100), (SEG, COLS))
        sy = jnp.where(lane < SHIFTS, meta, 0.0)
        sy = sy + pltpu.roll(sy, SHIFTS, 1)
        sy = sy + pltpu.roll(sy, 2 * SHIFTS, 1)
        w = jnp.where((lane >= 2 * SHIFTS) & (lane < 3 * SHIFTS), meta, 0.0) * (1.0 / 256)
        w = w + pltpu.roll(w, SHIFTS, 1)
        w = w + pltpu.roll(w, 2 * SHIFTS, 1)

        hot = []
        for i in range(SEG):
            spread = jnp.broadcast_to(meta[i : i + 1], (SHIFTS, COLS))
            sx = jnp.sum(jnp.where(lane_s == sub_s + SHIFTS, spread, 0.0), axis=1, keepdims=True)
            hot.append((jnp.broadcast_to(sx, (SHIFTS, SHIFTS)) == (lane_s[:, :SHIFTS] - 8).astype(f32)).astype(f32).astype(bf16))
        col_ref[...] = jnp.dot(jnp.concatenate(hot, axis=0), table, preferred_element_type=f32).astype(bf16)

        for i in range(SEG):
            c, s = turn(jnp.broadcast_to(sy[i : i + 1], (KY, COLS)) * kw)
            wi = jnp.broadcast_to(w[i : i + 1], (KY, COLS))
            c, s = c * wi, s * wi
            left = jnp.concatenate([jnp.where(first, c, -s), jnp.where(first, s, c)], axis=0)
            hi, lo = halves(left)
            right = jnp.concatenate(
                [col_ref[i * SHIFTS : (i + 1) * SHIFTS, q * COLS : (q + 1) * COLS] for q in range(4)], axis=0
            )
            both = jnp.dot(jnp.concatenate([hi, lo], axis=0), right, preferred_element_type=f32)
            q_re = both[0:KY] + both[D : D + KY]
            q_im = both[KY:D] + both[D + KY : 2 * D]
            arg = (200.0 * jnp.broadcast_to(defocus[i : i + 1], (KY, COLS))) * radius + 0.1
            gain = -sine(arg) * jnp.broadcast_to(alive[i : i + 1], (KY, COLS))
            img = recv_ref[a, i * D : (i + 1) * D].astype(f32)
            xr, xi = img[0:KY] * gain, img[KY:D] * gain
            at = (a * SEG + i) * D
            gx_ref[at : at + KY] = xr
            gx_ref[at + KY : at + D] = xi
            y_ref[at : at + KY] = xr * q_re - xi * q_im
            y_ref[at + KY : at + D] = xr * q_im + xi * q_re

    flat = wide_ref[...].T
    ids = jnp.broadcast_to(flat[99:100], (CLASSES, COLS))
    member = (ids == lax.broadcasted_iota(jnp.int32, (CLASSES, COLS), 0).astype(f32)).astype(f32).astype(bf16)
    for p in range(2):
        for ky in range(KY):
            hi, lo = halves(y_ref[pl.ds(p * KY + ky, SEGS, stride=D), :])
            sums = jnp.dot(member, jnp.concatenate([hi, lo], axis=0), preferred_element_type=f32)
            out_ref[zl * D + 2 * ky + p, B_NUM:B_FACT] = sums.astype(bf16)
            out_ref[(1 - zl) * D + 2 * ky + p, B_NUM:B_FACT] = jnp.zeros((CLASSES, COLS), bf16)

    for x in range(NX):
        wide_ref[x * SEG : (x + 1) * SEG] = recv_ref[2 * x + zl, A_META:A_ROWS].astype(f32)
    flat = wide_ref[...].T
    total = jnp.sum(flat[2 * SHIFTS : 3 * SHIFTS], axis=0, keepdims=True)
    total_hi = jnp.floor(total * (1.0 / 32))
    facts = jnp.where(sub == 5, total_hi, jnp.where(sub == 6, total - 32.0 * total_hi, flat[96:104]))
    facts = facts.astype(bf16)
    for q in range(NB):
        for x in range(NX):
            base = A_REF + (q % 2) * D
            out_ref[q, x * D : (x + 1) * D] = recv_ref[2 * x + zl, base : base + D]
        out_ref[q, B_FACT:B_ROWS] = facts


def front(place, recv):
    vmem = pl.BlockSpec(memory_space=pltpu.VMEM)
    return pl.pallas_call(
        front_kernel,
        in_specs=[pl.BlockSpec(memory_space=pltpu.SMEM), vmem],
        out_specs=[vmem, vmem, vmem],
        out_shape=[
            jax.ShapeDtypeStruct((NB, B_ROWS, COLS), bf16),
            jax.ShapeDtypeStruct((SEGS, COLS), f32),
            jax.ShapeDtypeStruct((SEGS * D, COLS), f32),
        ],
        scratch_shapes=[
            pltpu.VMEM((COLS, COLS), f32),
            pltpu.VMEM((SEGS * D, COLS), f32),
            pltpu.VMEM((SEG * SHIFTS, 4 * COLS), bf16),
        ],
        compiler_params=pltpu.CompilerParams(vmem_limit_bytes=8 << 20),
        cost_estimate=pl.CostEstimate(flops=100_000_000, bytes_accessed=2_000_000, transcendentals=0),
        name="front",
    )(place, recv)


def align_kernel(place_ref, gx_ref, meta_ref, aligned_ref):
    kw0 = place_ref[0].astype(f32)
    lane = lax.broadcasted_iota(jnp.int32, (SHIFTS, COLS), 1)
    sub = lax.broadcasted_iota(jnp.int32, (SHIFTS, COLS), 0)
    kx = lane.astype(f32)

    def segment(i, carry):
        wide = jnp.broadcast_to(meta_ref[pl.ds(i, 1), :], (SHIFTS, COLS))
        sy = jnp.sum(jnp.where(lane == sub, wide, 0.0), axis=1, keepdims=True)
        sx = jnp.sum(jnp.where(lane == sub + SHIFTS, wide, 0.0), axis=1, keepdims=True)
        sy = jnp.broadcast_to(sy, (SHIFTS, COLS))
        pr, pi = turn(sy * kw0 + sx * kx)
        si, cr = small_sincos(sy * (-2.0 * math.pi / BOX))
        rows = pl.ds(pl.multiple_of(i * SHIFTS, SHIFTS), SHIFTS)
        for ky in range(KY):
            xr = gx_ref[pl.ds(i * D + ky, 1), :]
            xi = gx_ref[pl.ds(i * D + KY + ky, 1), :]
            aligned_ref[rows, ky * COLS : (ky + 1) * COLS] = (xr * pr - xi * pi).astype(bf16)
            aligned_ref[rows, (KY + ky) * COLS : (KY + ky + 1) * COLS] = (xr * pi + xi * pr).astype(bf16)
            if ky < KY - 1:
                pr, pi = pr * cr - pi * si, pr * si + pi * cr
        return carry

    lax.fori_loop(0, SEG, segment, 0)


def align(place, gx, meta):
    return pl.pallas_call(
        align_kernel,
        grid=(NA,),
        in_specs=[
            pl.BlockSpec(memory_space=pltpu.SMEM),
            pl.BlockSpec((SEG * D, COLS), lambda j: (j, 0)),
            pl.BlockSpec((SEG, COLS), lambda j: (j, 0)),
        ],
        out_specs=pl.BlockSpec((SEG * SHIFTS, D * COLS), lambda j: (j, 0)),
        out_shape=jax.ShapeDtypeStruct((SEGS * SHIFTS, D * COLS), bf16),
        compiler_params=pltpu.CompilerParams(vmem_limit_bytes=57 << 20),
        cost_estimate=pl.CostEstimate(flops=600_000_000, bytes_accessed=9_000_000, transcendentals=0),
        name="align",
    )(place, gx, meta)


def score_kernel(panel_ref, aligned_ref, out_ref, wide_ref, packed_ref):
    step = pl.program_id(0)
    refs = NX * NB

    @pl.when(step == 0)
    def _():
        def widen(q, carry):
            for x in range(NX):
                base = pl.multiple_of((x * NB + q) * D, D)
                wide_ref[pl.ds(base, D), :] = panel_ref[q, x * D : (x + 1) * D, :].astype(f32)
            return carry

        lax.fori_loop(0, NB, widen, 0)
        for d in range(D):
            packed_ref[d * COLS : (d + 1) * COLS, :] = wide_ref[pl.ds(d, refs, stride=D), :].T.astype(bf16)

    res = jnp.dot(aligned_ref[...], packed_ref[...], preferred_element_type=f32)
    for i in range(SEG):
        for r in range(NROW):
            out_ref[0, r, i] = res[i * SHIFTS + r * 8 : i * SHIFTS + (r + 1) * 8, :].astype(out_ref.dtype)


def score(panel, aligned):
    refs = NX * NB
    return pl.pallas_call(
        score_kernel,
        grid=(NA,),
        in_specs=[
            pl.BlockSpec(panel.shape, lambda j: (0, 0, 0)),
            pl.BlockSpec((SEG * SHIFTS, D * COLS), lambda j: (j, 0)),
        ],
        out_specs=pl.BlockSpec((1, NROW, SEG, 8, refs), lambda j: (j, 0, 0, 0, 0)),
        out_shape=jax.ShapeDtypeStruct((NA, NROW, SEG, 8, refs), PARTIAL),
        scratch_shapes=[
            pltpu.VMEM((refs * D, COLS), f32),
            pltpu.VMEM((D * COLS, refs), bf16),
        ],
        compiler_params=pltpu.CompilerParams(vmem_limit_bytes=57 << 20),
        cost_estimate=pl.CostEstimate(flops=1_100_000_000, bytes_accessed=10_000_000, transcendentals=0),
        name="score",
    )(panel, aligned)


def contrast(defocus, kw, kx):
    radius = (kw * kw + kx * kx).astype(f32) / float(BOX * BOX)
    return -jnp.sin(200.0 * defocus * radius + 0.1)


def centred(ky):
    return (ky + BOX // 2) % BOX - BOX // 2


def per_device(images, defocus, references, offsets, posterior, class_ids, seg_count):
    row = lax.axis_index(ROW)
    fil = lax.axis_index(FIL)
    kx = jnp.arange(COLS, dtype=jnp.int32)
    kw_first = centred(row * 64 + lax.axis_index(("x", "zl")) * KY)
    place = jnp.stack([kw_first, lax.axis_index("zl")])

    send = pack(images, defocus, references, offsets, posterior, class_ids, seg_count)
    recv = lax.all_to_all(send, ("x", "zl"), 0, 0, tiled=True)
    sent, meta, gx = front(place, recv)
    panel = lax.all_to_all(sent, ("yh", "zh", "zl"), 0, 0, tiled=True)
    aligned = align(place, gx, meta)
    partial = score(panel, aligned)
    partial = lax.all_to_all(
        partial.reshape(NA * NROW, SEG * 8, COLS), ("x", "zl", *ROW), 0, 0, tiled=True
    )
    scores = jnp.sum(partial.astype(f32), axis=0).reshape(SEG, 8, COLS)

    numer = jnp.sum(panel[:, B_NUM:B_FACT].astype(f32), axis=0)
    facts = panel[:, B_FACT:B_ROWS, : NX * SEG].astype(f32)
    all_defocus = (facts[:, 0] + facts[:, 1] + facts[:, 2]).reshape(-1)
    all_class = facts[:, 3].reshape(-1)
    all_total = ((facts[:, 5] * 32.0 + facts[:, 6]) * (1.0 / 256)).reshape(-1)
    ctf = contrast(all_defocus[:, None], centred(row * 64 + fil // 2), kx[None, :])
    classes = jnp.arange(CLASSES, dtype=f32)
    totals = jnp.where(all_class[None, :] == classes[:, None], all_total[None, :], 0.0)
    denom = jnp.dot(totals, ctf * ctf, precision=lax.Precision.HIGHEST, preferred_element_type=f32)
    averages = numer * lax.rsqrt(denom + 1.0)
    return scores, averages


def solution(mesh):
    fine = Mesh(mesh.devices.reshape(4, 4, 4, 2, 2, 2), (*FIL, *ROW))
    placed = (
        P(FIL, None, ROW, None),
        P(FIL),
        P(FIL, None, ROW, None),
        P(FIL, None, None),
        P(FIL, None),
        P(FIL),
        P(FIL),
    )
    return jax.shard_map(
        per_device,
        mesh=fine,
        in_specs=placed,
        out_specs=(P(FIL, ROW, None), P(None, (*ROW, *FIL))),
        check_vma=False,
    )
```

```python
import math

import jax
import jax.numpy as jnp
from jax import lax
from jax.experimental import pallas as pl
from jax.experimental.pallas import tpu as pltpu
from jax.sharding import Mesh
from jax.sharding import PartitionSpec as P

BOX = 256
SHIFTS = 32
CLASSES = 16
SEG = 8
NA = 8
NB = 32
NX = 4
NROW = 4
SEGS = NA * SEG
KY = 8
D = 2 * KY
COLS = 128
META = 8
A_REF = SEG * D
A_META = A_REF + 2 * D
A_ROWS = A_META + META
B_NUM = NX * D
B_FACT = B_NUM + CLASSES
B_ROWS = B_FACT + META
FIL = ("x", "yh", "zh", "zl")
ROW = ("yl", "core")
bf16 = jnp.bfloat16
f32 = jnp.float32
PARTIAL = bf16


def small_sincos(theta):
    t2 = theta * theta
    sin = theta * (1.0 + t2 * (-1.0 / 6 + t2 * (1.0 / 120 + t2 * (-1.0 / 5040 + t2 * (1.0 / 362880)))))
    cos = 1.0 + t2 * (-0.5 + t2 * (1.0 / 24 + t2 * (-1.0 / 720 + t2 * (1.0 / 40320 + t2 * (-1.0 / 3628800)))))
    return sin, cos


def quarter(n, sin, cos):
    quad = n - 4.0 * jnp.floor(n * 0.25)
    odd = (quad == 1.0) | (quad == 3.0)
    c = jnp.where(odd, sin, cos)
    s = jnp.where(odd, cos, sin)
    c = jnp.where((quad == 1.0) | (quad == 2.0), -c, c)
    return jnp.where(quad >= 2.0, -s, s), c


def turn(m):
    n = jnp.floor(m * (1.0 / 64) + 0.5)
    sin, cos = quarter(n, *small_sincos((m - 64.0 * n) * (math.pi / 128)))
    return cos, -sin


def sine(arg):
    n = jnp.floor(arg * (2.0 / math.pi) + 0.5)
    rest = ((arg - n * 1.5703125) - n * 4.837512969970703125e-4) - n * 7.54978995489188216e-8
    return quarter(n, *small_sincos(rest))[0]


def halves(v):
    hi = v.astype(bf16)
    return hi, (v - hi.astype(f32)).astype(bf16)


def parts_of(v):
    hi = v.astype(bf16).astype(f32)
    rest = v - hi
    mid = rest.astype(bf16).astype(f32)
    return hi, mid, rest - mid


def pack_kernel(*refs):
    count_ref, given, out_ref, held, meta_ref, sems = refs[0], refs[1:7], refs[7], refs[8:14], refs[14], refs[15]
    copies = [pltpu.make_async_copy(src, dst, sems.at[k]) for k, (src, dst) in enumerate(zip(given, held))]
    for copy in copies:
        copy.start()
    for copy in copies:
        copy.wait()
    defocus_ref, class_ref, img_ref, ref_ref, off_ref, post_ref = held
    sub = lax.broadcasted_iota(jnp.int32, (META, COLS), 0)
    lane = lax.broadcasted_iota(jnp.int32, (META, COLS), 1)
    live = (sub < count_ref[0]).astype(f32)
    defocus = jnp.zeros((META, COLS), f32)
    ids = jnp.zeros((META, COLS), f32)
    for i in range(SEG):
        defocus = jnp.where(sub == i, defocus_ref[i], defocus)
        ids = jnp.where(sub == i, class_ref[i].astype(f32), ids)
    hi, mid, low = parts_of(defocus)
    facts = jnp.where(lane == 96, hi, jnp.where(lane == 97, mid, jnp.where(lane == 98, low, 0.0)))
    facts = jnp.where(lane == 99, ids, jnp.where(lane == 100, live, facts))
    meta_ref[...] = facts
    for i in range(SEG):
        both = off_ref[i].astype(f32)
        meta_ref[i : i + 1, 0:SHIFTS] = both[0:1]
        meta_ref[i : i + 1, SHIFTS : 2 * SHIFTS] = both[1:2]
    meta_ref[0:SEG, 2 * SHIFTS : 3 * SHIFTS] = post_ref[...].astype(f32) * live[0:SEG, 0:SHIFTS]
    meta = meta_ref[...].astype(bf16)
    for j in range(NA):
        for p in range(2):
            for i in range(SEG):
                out_ref[j, i * D + p * KY : i * D + (p + 1) * KY] = img_ref[i, p, j * KY : (j + 1) * KY]
            for half in range(2):
                base = A_REF + half * D + p * KY
                first = (j // 2) * 2 * KY + half * KY
                out_ref[j, base : base + KY] = ref_ref[0, p, first : first + KY]
        out_ref[j, A_META:A_ROWS] = meta


def pack(images, defocus, references, offsets, posterior, class_ids, seg_count):
    given = (defocus, class_ids, images, references, offsets.transpose(0, 2, 1), posterior)
    places = (pltpu.SMEM,) * 2 + (pltpu.VMEM,) * 4
    return pl.pallas_call(
        pack_kernel,
        in_specs=[pl.BlockSpec(memory_space=pltpu.SMEM)] + [pl.BlockSpec(memory_space=pltpu.HBM)] * 6,
        out_specs=pl.BlockSpec(memory_space=pltpu.VMEM),
        out_shape=jax.ShapeDtypeStruct((NA, A_ROWS, COLS), bf16),
        scratch_shapes=[place(v.shape, v.dtype) for place, v in zip(places, given)]
        + [pltpu.VMEM((META, COLS), f32), pltpu.SemaphoreType.DMA((6,))],
        compiler_params=pltpu.CompilerParams(vmem_limit_bytes=4 << 20),
        cost_estimate=pl.CostEstimate(flops=100_000, bytes_accessed=700_000, transcendentals=0),
        name="pack",
    )(seg_count, *(pltpu.with_memory_space_constraint(v, pltpu.HBM) for v in given))


def front_kernel(place_ref, recv_ref, out_ref, meta_out_ref, gx_ref, wide_ref, y_ref, col_ref):
    kw0 = place_ref[0]
    zl = place_ref[1]
    lane = lax.broadcasted_iota(jnp.int32, (KY, COLS), 1)
    sub = lax.broadcasted_iota(jnp.int32, (KY, COLS), 0)
    kw = (sub + kw0).astype(f32)
    kx = lane.astype(f32)
    radius = (kw * kw + kx * kx) * (1.0 / (BOX * BOX))
    first = (lane % (2 * SHIFTS)) < SHIFTS
    lane_s = lax.broadcasted_iota(jnp.int32, (SHIFTS, COLS), 1)
    sub_s = lax.broadcasted_iota(jnp.int32, (SHIFTS, COLS), 0)

    c, s = turn((sub_s - 8).astype(f32) * lane_s.astype(f32))
    (c_hi, c_lo), (s_hi, s_lo) = halves(c), halves(s)
    table = jnp.concatenate([c_hi, s_hi, c_lo, s_lo], axis=1)

    for a in range(NA):
        meta = recv_ref[a, A_META:A_ROWS].astype(f32)
        rows = slice(a * SEG, (a + 1) * SEG)
        meta_out_ref[rows] = meta
        wide_ref[rows] = meta
        wide_ref[SEGS + a * SEG : SEGS + (a + 1) * SEG] = meta

        def pick(at):
            return jnp.sum(jnp.where(lane == at, meta, 0.0), axis=1, keepdims=True)

        defocus = jnp.broadcast_to(pick(96) + pick(97) + pick(98), (SEG, COLS))
        alive = jnp.broadcast_to(pick(100), (SEG, COLS))
        sy = jnp.where(lane < SHIFTS, meta, 0.0)
        sy = sy + pltpu.roll(sy, SHIFTS, 1)
        sy = sy + pltpu.roll(sy, 2 * SHIFTS, 1)
        w = jnp.where((lane >= 2 * SHIFTS) & (lane < 3 * SHIFTS), meta, 0.0) * (1.0 / 256)
        w = w + pltpu.roll(w, SHIFTS, 1)
        w = w + pltpu.roll(w, 2 * SHIFTS, 1)

        hot = []
        for i in range(SEG):
            spread = jnp.broadcast_to(meta[i : i + 1], (SHIFTS, COLS))
            sx = jnp.sum(jnp.where(lane_s == sub_s + SHIFTS, spread, 0.0), axis=1, keepdims=True)
            hot.append((jnp.broadcast_to(sx, (SHIFTS, SHIFTS)) == (lane_s[:, :SHIFTS] - 8).astype(f32)).astype(f32).astype(bf16))
        col_ref[...] = jnp.dot(jnp.concatenate(hot, axis=0), table, preferred_element_type=f32).astype(bf16)

        for i in range(SEG):
            c, s = turn(jnp.broadcast_to(sy[i : i + 1], (KY, COLS)) * kw)
            wi = jnp.broadcast_to(w[i : i + 1], (KY, COLS))
            c, s = c * wi, s * wi
            left = jnp.concatenate([jnp.where(first, c, -s), jnp.where(first, s, c)], axis=0)
            hi, lo = halves(left)
            right = jnp.concatenate(
                [col_ref[i * SHIFTS : (i + 1) * SHIFTS, q * COLS : (q + 1) * COLS] for q in range(4)], axis=0
            )
            both = jnp.dot(jnp.concatenate([hi, lo], axis=0), right, preferred_element_type=f32)
            q_re = both[0:KY] + both[D : D + KY]
            q_im = both[KY:D] + both[D + KY : 2 * D]
            arg = (200.0 * jnp.broadcast_to(defocus[i : i + 1], (KY, COLS))) * radius + 0.1
            gain = -sine(arg) * jnp.broadcast_to(alive[i : i + 1], (KY, COLS))
            img = recv_ref[a, i * D : (i + 1) * D].astype(f32)
            xr, xi = img[0:KY] * gain, img[KY:D] * gain
            at = (a * SEG + i) * D
            gx_ref[at : at + KY] = xr
            gx_ref[at + KY : at + D] = xi
            y_ref[at : at + KY] = xr * q_re - xi * q_im
            y_ref[at + KY : at + D] = xr * q_im + xi * q_re

    flat = wide_ref[...].T
    ids = jnp.broadcast_to(flat[99:100], (CLASSES, COLS))
    member = (ids == lax.broadcasted_iota(jnp.int32, (CLASSES, COLS), 0).astype(f32)).astype(f32).astype(bf16)
    for p in range(2):
        for ky in range(KY):
            hi, lo = halves(y_ref[pl.ds(p * KY + ky, SEGS, stride=D), :])
            sums = jnp.dot(member, jnp.concatenate([hi, lo], axis=0), preferred_element_type=f32)
            out_ref[zl * D + 2 * ky + p, B_NUM:B_FACT] = sums.astype(bf16)
            out_ref[(1 - zl) * D + 2 * ky + p, B_NUM:B_FACT] = jnp.zeros((CLASSES, COLS), bf16)

    for x in range(NX):
        wide_ref[x * SEG : (x + 1) * SEG] = recv_ref[2 * x + zl, A_META:A_ROWS].astype(f32)
    flat = wide_ref[...].T
    total = jnp.sum(flat[2 * SHIFTS : 3 * SHIFTS], axis=0, keepdims=True)
    total_hi = jnp.floor(total * (1.0 / 32))
    facts = jnp.where(sub == 5, total_hi, jnp.where(sub == 6, total - 32.0 * total_hi, flat[96:104]))
    facts = facts.astype(bf16)
    for q in range(NB):
        for x in range(NX):
            base = A_REF + (q % 2) * D
            out_ref[q, x * D : (x + 1) * D] = recv_ref[2 * x + zl, base : base + D]
        out_ref[q, B_FACT:B_ROWS] = facts


def front(place, recv):
    vmem = pl.BlockSpec(memory_space=pltpu.VMEM)
    return pl.pallas_call(
        front_kernel,
        in_specs=[pl.BlockSpec(memory_space=pltpu.SMEM), vmem],
        out_specs=[vmem, vmem, vmem],
        out_shape=[
            jax.ShapeDtypeStruct((NB, B_ROWS, COLS), bf16),
            jax.ShapeDtypeStruct((SEGS, COLS), f32),
            jax.ShapeDtypeStruct((SEGS * D, COLS), f32),
        ],
        scratch_shapes=[
            pltpu.VMEM((COLS, COLS), f32),
            pltpu.VMEM((SEGS * D, COLS), f32),
            pltpu.VMEM((SEG * SHIFTS, 4 * COLS), bf16),
        ],
        compiler_params=pltpu.CompilerParams(vmem_limit_bytes=8 << 20),
        cost_estimate=pl.CostEstimate(flops=100_000_000, bytes_accessed=2_000_000, transcendentals=0),
        name="front",
    )(place, recv)


def align_kernel(place_ref, gx_ref, meta_ref, aligned_ref):
    kw0 = place_ref[0].astype(f32)
    lane = lax.broadcasted_iota(jnp.int32, (SHIFTS, COLS), 1)
    sub = lax.broadcasted_iota(jnp.int32, (SHIFTS, COLS), 0)
    kx = lane.astype(f32)

    def segment(i, carry):
        wide = jnp.broadcast_to(meta_ref[pl.ds(i, 1), :], (SHIFTS, COLS))
        sy = jnp.sum(jnp.where(lane == sub, wide, 0.0), axis=1, keepdims=True)
        sx = jnp.sum(jnp.where(lane == sub + SHIFTS, wide, 0.0), axis=1, keepdims=True)
        sy = jnp.broadcast_to(sy, (SHIFTS, COLS))
        pr, pi = turn(sy * kw0 + sx * kx)
        si, cr = small_sincos(sy * (-2.0 * math.pi / BOX))
        rows = pl.ds(pl.multiple_of(i * SHIFTS, SHIFTS), SHIFTS)
        for ky in range(KY):
            xr = gx_ref[pl.ds(i * D + ky, 1), :]
            xi = gx_ref[pl.ds(i * D + KY + ky, 1), :]
            aligned_ref[rows, ky * COLS : (ky + 1) * COLS] = (xr * pr - xi * pi).astype(bf16)
            aligned_ref[rows, (KY + ky) * COLS : (KY + ky + 1) * COLS] = (xr * pi + xi * pr).astype(bf16)
            if ky < KY - 1:
                pr, pi = pr * cr - pi * si, pr * si + pi * cr
        return carry

    lax.fori_loop(0, SEG, segment, 0)


def align(place, gx, meta):
    return pl.pallas_call(
        align_kernel,
        grid=(NA,),
        in_specs=[
            pl.BlockSpec(memory_space=pltpu.SMEM),
            pl.BlockSpec((SEG * D, COLS), lambda j: (j, 0)),
            pl.BlockSpec((SEG, COLS), lambda j: (j, 0)),
        ],
        out_specs=pl.BlockSpec((SEG * SHIFTS, D * COLS), lambda j: (j, 0)),
        out_shape=pltpu.HBM((SEGS * SHIFTS, D * COLS), bf16),
        compiler_params=pltpu.CompilerParams(vmem_limit_bytes=10 << 20),
        cost_estimate=pl.CostEstimate(flops=600_000_000, bytes_accessed=9_000_000, transcendentals=0),
        name="align",
    )(place, gx, meta)


def score_kernel(panel_ref, aligned_ref, out_ref, wide_ref, packed_ref, held_ref, sems):
    refs = NX * NB
    block = SEG * SHIFTS
    copies = [
        pltpu.make_async_copy(
            aligned_ref.at[j * block : (j + 1) * block], held_ref.at[j * block : (j + 1) * block], sems.at[j]
        )
        for j in range(NA)
    ]
    for copy in copies:
        copy.start()

    def widen(q, carry):
        for x in range(NX):
            base = pl.multiple_of((x * NB + q) * D, D)
            wide_ref[pl.ds(base, D), :] = panel_ref[q, x * D : (x + 1) * D, :].astype(f32)
        return carry

    lax.fori_loop(0, NB, widen, 0)
    for d in range(D):
        packed_ref[d * COLS : (d + 1) * COLS, :] = wide_ref[pl.ds(d, refs, stride=D), :].T.astype(bf16)

    for j in range(NA):
        copies[j].wait()
        res = jnp.dot(held_ref[j * block : (j + 1) * block], packed_ref[...], preferred_element_type=f32)
        for i in range(SEG):
            for r in range(NROW):
                out_ref[j, r, i] = res[i * SHIFTS + r * 8 : i * SHIFTS + (r + 1) * 8, :].astype(out_ref.dtype)


def score(panel, aligned):
    refs = NX * NB
    vmem = pl.BlockSpec(memory_space=pltpu.VMEM)
    return pl.pallas_call(
        score_kernel,
        in_specs=[vmem, pl.BlockSpec(memory_space=pltpu.HBM)],
        out_specs=vmem,
        out_shape=jax.ShapeDtypeStruct((NA, NROW, SEG, 8, refs), PARTIAL),
        scratch_shapes=[
            pltpu.VMEM((refs * D, COLS), f32),
            pltpu.VMEM((D * COLS, refs), bf16),
            pltpu.VMEM(aligned.shape, bf16),
            pltpu.SemaphoreType.DMA((NA,)),
        ],
        compiler_params=pltpu.CompilerParams(vmem_limit_bytes=20 << 20),
        cost_estimate=pl.CostEstimate(flops=1_100_000_000, bytes_accessed=10_000_000, transcendentals=0),
        name="score",
    )(panel, pltpu.with_memory_space_constraint(aligned, pltpu.HBM))


def contrast(defocus, kw, kx):
    radius = (kw * kw + kx * kx).astype(f32) / float(BOX * BOX)
    return -jnp.sin(200.0 * defocus * radius + 0.1)


def centred(ky):
    return (ky + BOX // 2) % BOX - BOX // 2


def per_device(images, defocus, references, offsets, posterior, class_ids, seg_count):
    row = lax.axis_index(ROW)
    fil = lax.axis_index(FIL)
    kx = jnp.arange(COLS, dtype=jnp.int32)
    kw_first = centred(row * 64 + lax.axis_index(("x", "zl")) * KY)
    place = jnp.stack([kw_first, lax.axis_index("zl")])

    send = pack(images, defocus, references, offsets, posterior, class_ids, seg_count)
    recv = lax.all_to_all(send, ("x", "zl"), 0, 0, tiled=True)
    sent, meta, gx = front(place, recv)
    panel = lax.all_to_all(sent, ("yh", "zh", "zl"), 0, 0, tiled=True)
    aligned = align(place, gx, meta)
    partial = score(panel, aligned)
    partial = lax.all_to_all(
        partial.reshape(NA * NROW, SEG * 8, COLS), ("x", "zl", *ROW), 0, 0, tiled=True
    )
    scores = jnp.sum(partial.astype(f32), axis=0).reshape(SEG, 8, COLS)

    numer = jnp.sum(panel[:, B_NUM:B_FACT].astype(f32), axis=0)
    facts = panel[:, B_FACT:B_ROWS, : NX * SEG].astype(f32)
    all_defocus = (facts[:, 0] + facts[:, 1] + facts[:, 2]).reshape(-1)
    all_class = facts[:, 3].reshape(-1)
    all_total = ((facts[:, 5] * 32.0 + facts[:, 6]) * (1.0 / 256)).reshape(-1)
    ctf = contrast(all_defocus[:, None], centred(row * 64 + fil // 2), kx[None, :])
    classes = jnp.arange(CLASSES, dtype=f32)
    totals = jnp.where(all_class[None, :] == classes[:, None], all_total[None, :], 0.0)
    denom = jnp.dot(totals, ctf * ctf, precision=lax.Precision.HIGHEST, preferred_element_type=f32)
    averages = numer * lax.rsqrt(denom + 1.0)
    return scores, averages


def solution(mesh):
    fine = Mesh(mesh.devices.reshape(4, 4, 4, 2, 2, 2), (*FIL, *ROW))
    placed = (
        P(FIL, None, ROW, None),
        P(FIL),
        P(FIL, None, ROW, None),
        P(FIL, None, None),
        P(FIL, None),
        P(FIL),
        P(FIL),
    )
    return jax.shard_map(
        per_device,
        mesh=fine,
        in_specs=placed,
        out_specs=(P(FIL, ROW, None), P(None, (*ROW, *FIL))),
        check_vma=False,
    )
```

```python
import math

import jax
import jax.numpy as jnp
from jax import lax
from jax.experimental import pallas as pl
from jax.experimental.pallas import tpu as pltpu
from jax.sharding import Mesh
from jax.sharding import PartitionSpec as P

BOX = 256
SHIFTS = 32
CLASSES = 16
SEG = 8
NA = 8
NX = 4
NY = 4
NZ = 8
NROW = 4
SEGS = NA * SEG
KY = 8
D = 2 * KY
COLS = 128
META = 8
A_REF = SEG * D
A_META = A_REF + 2 * D
A_ROWS = A_META + META
Y_FACT = NX * 2 * D
Y_ROWS = Y_FACT + META
Z_NUM = NX * NY * D
Z_FACT = Z_NUM + 2 * CLASSES
Z_ROWS = Z_FACT + META
FIL = ("x", "yh", "zh", "zl")
ROW = ("yl", "core")
bf16 = jnp.bfloat16
f32 = jnp.float32
PARTIAL = bf16


def small_sincos(theta):
    t2 = theta * theta
    sin = theta * (1.0 + t2 * (-1.0 / 6 + t2 * (1.0 / 120 + t2 * (-1.0 / 5040 + t2 * (1.0 / 362880)))))
    cos = 1.0 + t2 * (-0.5 + t2 * (1.0 / 24 + t2 * (-1.0 / 720 + t2 * (1.0 / 40320 + t2 * (-1.0 / 3628800)))))
    return sin, cos


def quarter(n, sin, cos):
    quad = n - 4.0 * jnp.floor(n * 0.25)
    odd = (quad == 1.0) | (quad == 3.0)
    c = jnp.where(odd, sin, cos)
    s = jnp.where(odd, cos, sin)
    c = jnp.where((quad == 1.0) | (quad == 2.0), -c, c)
    return jnp.where(quad >= 2.0, -s, s), c


def turn(m):
    n = jnp.floor(m * (1.0 / 64) + 0.5)
    sin, cos = quarter(n, *small_sincos((m - 64.0 * n) * (math.pi / 128)))
    return cos, -sin


def sine(arg):
    n = jnp.floor(arg * (2.0 / math.pi) + 0.5)
    rest = ((arg - n * 1.5703125) - n * 4.837512969970703125e-4) - n * 7.54978995489188216e-8
    return quarter(n, *small_sincos(rest))[0]


def halves(v):
    hi = v.astype(bf16)
    return hi, (v - hi.astype(f32)).astype(bf16)


def parts_of(v):
    hi = v.astype(bf16).astype(f32)
    rest = v - hi
    mid = rest.astype(bf16).astype(f32)
    return hi, mid, rest - mid


def pack_kernel(*refs):
    count_ref, given, out_ref, held, meta_ref, sems = refs[0], refs[1:7], refs[7], refs[8:14], refs[14], refs[15]
    copies = [pltpu.make_async_copy(src, dst, sems.at[k]) for k, (src, dst) in enumerate(zip(given, held))]
    for copy in copies:
        copy.start()
    for copy in copies:
        copy.wait()
    defocus_ref, class_ref, img_ref, ref_ref, off_ref, post_ref = held
    sub = lax.broadcasted_iota(jnp.int32, (META, COLS), 0)
    lane = lax.broadcasted_iota(jnp.int32, (META, COLS), 1)
    live = (sub < count_ref[0]).astype(f32)
    defocus = jnp.zeros((META, COLS), f32)
    ids = jnp.zeros((META, COLS), f32)
    for i in range(SEG):
        defocus = jnp.where(sub == i, defocus_ref[i], defocus)
        ids = jnp.where(sub == i, class_ref[i].astype(f32), ids)
    hi, mid, low = parts_of(defocus)
    facts = jnp.where(lane == 96, hi, jnp.where(lane == 97, mid, jnp.where(lane == 98, low, 0.0)))
    facts = jnp.where(lane == 99, ids, jnp.where(lane == 100, live, facts))
    meta_ref[...] = facts
    for i in range(SEG):
        both = off_ref[i].astype(f32)
        meta_ref[i : i + 1, 0:SHIFTS] = both[0:1]
        meta_ref[i : i + 1, SHIFTS : 2 * SHIFTS] = both[1:2]
    meta_ref[0:SEG, 2 * SHIFTS : 3 * SHIFTS] = post_ref[...].astype(f32) * live[0:SEG, 0:SHIFTS]
    meta = meta_ref[...].astype(bf16)
    for j in range(NA):
        for p in range(2):
            for i in range(SEG):
                out_ref[j, i * D + p * KY : i * D + (p + 1) * KY] = img_ref[i, p, j * KY : (j + 1) * KY]
            for half in range(2):
                base = A_REF + half * D + p * KY
                first = (j // 2) * 2 * KY + half * KY
                out_ref[j, base : base + KY] = ref_ref[0, p, first : first + KY]
        out_ref[j, A_META:A_ROWS] = meta


def pack(images, defocus, references, offsets, posterior, class_ids, seg_count):
    given = (defocus, class_ids, images, references, offsets.transpose(0, 2, 1), posterior)
    places = (pltpu.SMEM,) * 2 + (pltpu.VMEM,) * 4
    return pl.pallas_call(
        pack_kernel,
        in_specs=[pl.BlockSpec(memory_space=pltpu.SMEM)] + [pl.BlockSpec(memory_space=pltpu.HBM)] * 6,
        out_specs=pl.BlockSpec(memory_space=pltpu.VMEM),
        out_shape=jax.ShapeDtypeStruct((NA, A_ROWS, COLS), bf16),
        scratch_shapes=[place(v.shape, v.dtype) for place, v in zip(places, given)]
        + [pltpu.VMEM((META, COLS), f32), pltpu.SemaphoreType.DMA((6,))],
        compiler_params=pltpu.CompilerParams(vmem_limit_bytes=4 << 20),
        cost_estimate=pl.CostEstimate(flops=100_000, bytes_accessed=700_000, transcendentals=0),
        name="pack",
    )(seg_count, *(pltpu.with_memory_space_constraint(v, pltpu.HBM) for v in given))


def chunk_kernel(place_ref, recv_ref, out_ref, wide_ref):
    zl = place_ref[1]
    wide_ref[...] = jnp.zeros_like(wide_ref)
    for x in range(NX):
        wide_ref[x * SEG : (x + 1) * SEG] = recv_ref[2 * x + zl, A_META:A_ROWS].astype(f32)
    flat = wide_ref[...].T
    total = jnp.sum(flat[2 * SHIFTS : 3 * SHIFTS], axis=0, keepdims=True)
    total_hi = jnp.floor(total * (1.0 / 32))
    sub = lax.broadcasted_iota(jnp.int32, (META, COLS), 0)
    facts = jnp.where(sub == 5, total_hi, jnp.where(sub == 6, total - 32.0 * total_hi, flat[96:104]))
    facts = facts.astype(bf16)
    for q in range(NY):
        for x in range(NX):
            out_ref[q, x * 2 * D : (x + 1) * 2 * D] = recv_ref[2 * x + zl, A_REF : A_REF + 2 * D]
        out_ref[q, Y_FACT:Y_ROWS] = facts


def chunk(place, recv):
    vmem = pl.BlockSpec(memory_space=pltpu.VMEM)
    return pl.pallas_call(
        chunk_kernel,
        in_specs=[pl.BlockSpec(memory_space=pltpu.SMEM), vmem],
        out_specs=vmem,
        out_shape=jax.ShapeDtypeStruct((NY, Y_ROWS, COLS), bf16),
        scratch_shapes=[pltpu.VMEM((COLS, COLS), f32)],
        compiler_params=pltpu.CompilerParams(vmem_limit_bytes=4 << 20),
        cost_estimate=pl.CostEstimate(flops=100_000, bytes_accessed=500_000, transcendentals=0),
        name="chunk",
    )(place, recv)


def merge_kernel(panel_ref, numer_ref, out_ref):
    lane = lax.broadcasted_iota(jnp.int32, (META, COLS), 1)
    facts = jnp.zeros((META, COLS), f32)
    for y in range(NY):
        own = jnp.where(lane < NX * SEG, panel_ref[y, Y_FACT:Y_ROWS].astype(f32), 0.0)
        facts += pltpu.roll(own, y * NX * SEG, 1) if y else own
    facts = facts.astype(bf16)
    for q in range(NZ):
        for y in range(NY):
            for x in range(NX):
                base = x * 2 * D + (q % 2) * D
                out_ref[q, (y * NX + x) * D : (y * NX + x + 1) * D] = panel_ref[y, base : base + D]
        out_ref[q, Z_NUM:Z_FACT] = numer_ref[q]
        out_ref[q, Z_FACT:Z_ROWS] = facts


def merge(panel, numer):
    vmem = pl.BlockSpec(memory_space=pltpu.VMEM)
    return pl.pallas_call(
        merge_kernel,
        in_specs=[vmem, vmem],
        out_specs=vmem,
        out_shape=jax.ShapeDtypeStruct((NZ, Z_ROWS, COLS), bf16),
        compiler_params=pltpu.CompilerParams(vmem_limit_bytes=4 << 20),
        cost_estimate=pl.CostEstimate(flops=100_000, bytes_accessed=1_000_000, transcendentals=0),
        name="merge",
    )(panel, numer)


def front_kernel(place_ref, recv_ref, numer_ref, meta_out_ref, gx_ref, wide_ref, y_ref, col_ref):
    kw0 = place_ref[0]
    lane = lax.broadcasted_iota(jnp.int32, (KY, COLS), 1)
    sub = lax.broadcasted_iota(jnp.int32, (KY, COLS), 0)
    kw = (sub + kw0).astype(f32)
    kx = lane.astype(f32)
    radius = (kw * kw + kx * kx) * (1.0 / (BOX * BOX))
    first = (lane % (2 * SHIFTS)) < SHIFTS
    lane_s = lax.broadcasted_iota(jnp.int32, (SHIFTS, COLS), 1)
    sub_s = lax.broadcasted_iota(jnp.int32, (SHIFTS, COLS), 0)

    c, s = turn((sub_s - 8).astype(f32) * lane_s.astype(f32))
    (c_hi, c_lo), (s_hi, s_lo) = halves(c), halves(s)
    table = jnp.concatenate([c_hi, s_hi, c_lo, s_lo], axis=1)

    for a in range(NA):
        meta = recv_ref[a, A_META:A_ROWS].astype(f32)
        rows = slice(a * SEG, (a + 1) * SEG)
        meta_out_ref[rows] = meta
        wide_ref[rows] = meta
        wide_ref[SEGS + a * SEG : SEGS + (a + 1) * SEG] = meta

        def pick(at):
            return jnp.sum(jnp.where(lane == at, meta, 0.0), axis=1, keepdims=True)

        defocus = jnp.broadcast_to(pick(96) + pick(97) + pick(98), (SEG, COLS))
        alive = jnp.broadcast_to(pick(100), (SEG, COLS))
        sy = jnp.where(lane < SHIFTS, meta, 0.0)
        sy = sy + pltpu.roll(sy, SHIFTS, 1)
        sy = sy + pltpu.roll(sy, 2 * SHIFTS, 1)
        w = jnp.where((lane >= 2 * SHIFTS) & (lane < 3 * SHIFTS), meta, 0.0) * (1.0 / 256)
        w = w + pltpu.roll(w, SHIFTS, 1)
        w = w + pltpu.roll(w, 2 * SHIFTS, 1)

        hot = []
        for i in range(SEG):
            spread = jnp.broadcast_to(meta[i : i + 1], (SHIFTS, COLS))
            sx = jnp.sum(jnp.where(lane_s == sub_s + SHIFTS, spread, 0.0), axis=1, keepdims=True)
            hot.append((jnp.broadcast_to(sx, (SHIFTS, SHIFTS)) == (lane_s[:, :SHIFTS] - 8).astype(f32)).astype(f32).astype(bf16))
        col_ref[...] = jnp.dot(jnp.concatenate(hot, axis=0), table, preferred_element_type=f32).astype(bf16)

        for i in range(SEG):
            c, s = turn(jnp.broadcast_to(sy[i : i + 1], (KY, COLS)) * kw)
            wi = jnp.broadcast_to(w[i : i + 1], (KY, COLS))
            c, s = c * wi, s * wi
            left = jnp.concatenate([jnp.where(first, c, -s), jnp.where(first, s, c)], axis=0)
            hi, lo = halves(left)
            right = jnp.concatenate(
                [col_ref[i * SHIFTS : (i + 1) * SHIFTS, q * COLS : (q + 1) * COLS] for q in range(4)], axis=0
            )
            both = jnp.dot(jnp.concatenate([hi, lo], axis=0), right, preferred_element_type=f32)
            q_re = both[0:KY] + both[D : D + KY]
            q_im = both[KY:D] + both[D + KY : 2 * D]
            arg = (200.0 * jnp.broadcast_to(defocus[i : i + 1], (KY, COLS))) * radius + 0.1
            gain = -sine(arg) * jnp.broadcast_to(alive[i : i + 1], (KY, COLS))
            img = recv_ref[a, i * D : (i + 1) * D].astype(f32)
            xr, xi = img[0:KY] * gain, img[KY:D] * gain
            at = (a * SEG + i) * D
            gx_ref[at : at + KY] = xr
            gx_ref[at + KY : at + D] = xi
            y_ref[at : at + KY] = xr * q_re - xi * q_im
            y_ref[at + KY : at + D] = xr * q_im + xi * q_re

    flat = wide_ref[...].T
    ids = jnp.broadcast_to(flat[99:100], (CLASSES, COLS))
    member = (ids == lax.broadcasted_iota(jnp.int32, (CLASSES, COLS), 0).astype(f32)).astype(f32).astype(bf16)
    for p in range(2):
        for ky in range(KY):
            hi, lo = halves(y_ref[pl.ds(p * KY + ky, SEGS, stride=D), :])
            sums = jnp.dot(member, jnp.concatenate([hi, lo], axis=0), preferred_element_type=f32)
            high = ky // 4
            numer_ref[2 * (ky % 4) + p, high * CLASSES : (high + 1) * CLASSES] = sums.astype(bf16)


def front(place, recv):
    vmem = pl.BlockSpec(memory_space=pltpu.VMEM)
    return pl.pallas_call(
        front_kernel,
        in_specs=[pl.BlockSpec(memory_space=pltpu.SMEM), vmem],
        out_specs=[vmem, vmem, vmem],
        out_shape=[
            jax.ShapeDtypeStruct((NZ, 2 * CLASSES, COLS), bf16),
            jax.ShapeDtypeStruct((SEGS, COLS), f32),
            jax.ShapeDtypeStruct((SEGS * D, COLS), f32),
        ],
        scratch_shapes=[
            pltpu.VMEM((COLS, COLS), f32),
            pltpu.VMEM((SEGS * D, COLS), f32),
            pltpu.VMEM((SEG * SHIFTS, 4 * COLS), bf16),
        ],
        compiler_params=pltpu.CompilerParams(vmem_limit_bytes=8 << 20),
        cost_estimate=pl.CostEstimate(flops=100_000_000, bytes_accessed=2_000_000, transcendentals=0),
        name="front",
    )(place, recv)


def align_kernel(place_ref, gx_ref, meta_ref, aligned_ref):
    kw0 = place_ref[0].astype(f32)
    lane = lax.broadcasted_iota(jnp.int32, (SHIFTS, COLS), 1)
    sub = lax.broadcasted_iota(jnp.int32, (SHIFTS, COLS), 0)
    kx = lane.astype(f32)

    def segment(i, carry):
        wide = jnp.broadcast_to(meta_ref[pl.ds(i, 1), :], (SHIFTS, COLS))
        sy = jnp.sum(jnp.where(lane == sub, wide, 0.0), axis=1, keepdims=True)
        sx = jnp.sum(jnp.where(lane == sub + SHIFTS, wide, 0.0), axis=1, keepdims=True)
        sy = jnp.broadcast_to(sy, (SHIFTS, COLS))
        pr, pi = turn(sy * kw0 + sx * kx)
        si, cr = small_sincos(sy * (-2.0 * math.pi / BOX))
        rows = pl.ds(pl.multiple_of(i * SHIFTS, SHIFTS), SHIFTS)
        for ky in range(KY):
            xr = gx_ref[pl.ds(i * D + ky, 1), :]
            xi = gx_ref[pl.ds(i * D + KY + ky, 1), :]
            aligned_ref[rows, ky * COLS : (ky + 1) * COLS] = (xr * pr - xi * pi).astype(bf16)
            aligned_ref[rows, (KY + ky) * COLS : (KY + ky + 1) * COLS] = (xr * pi + xi * pr).astype(bf16)
            if ky < KY - 1:
                pr, pi = pr * cr - pi * si, pr * si + pi * cr
        return carry

    lax.fori_loop(0, SEG, segment, 0)


def align(place, gx, meta):
    return pl.pallas_call(
        align_kernel,
        grid=(NA,),
        in_specs=[
            pl.BlockSpec(memory_space=pltpu.SMEM),
            pl.BlockSpec((SEG * D, COLS), lambda j: (j, 0)),
            pl.BlockSpec((SEG, COLS), lambda j: (j, 0)),
        ],
        out_specs=pl.BlockSpec((SEG * SHIFTS, D * COLS), lambda j: (j, 0)),
        out_shape=pltpu.HBM((SEGS * SHIFTS, D * COLS), bf16),
        compiler_params=pltpu.CompilerParams(vmem_limit_bytes=10 << 20),
        cost_estimate=pl.CostEstimate(flops=600_000_000, bytes_accessed=9_000_000, transcendentals=0),
        name="align",
    )(place, gx, meta)


def score_kernel(panel_ref, aligned_ref, out_ref, wide_ref, packed_ref, held_ref, sems):
    refs = NX * NY * NZ
    block = SEG * SHIFTS
    copies = [
        pltpu.make_async_copy(
            aligned_ref.at[j * block : (j + 1) * block], held_ref.at[j * block : (j + 1) * block], sems.at[j]
        )
        for j in range(NA)
    ]
    for copy in copies:
        copy.start()

    def widen(z, carry):
        for y in range(NY):
            for x in range(NX):
                base = pl.multiple_of(((x * NY + y) * NZ + z) * D, D)
                at = (y * NX + x) * D
                wide_ref[pl.ds(base, D), :] = panel_ref[z, at : at + D, :].astype(f32)
        return carry

    lax.fori_loop(0, NZ, widen, 0)
    for d in range(D):
        packed_ref[d * COLS : (d + 1) * COLS, :] = wide_ref[pl.ds(d, refs, stride=D), :].T.astype(bf16)

    for j in range(NA):
        copies[j].wait()
        res = jnp.dot(held_ref[j * block : (j + 1) * block], packed_ref[...], preferred_element_type=f32)
        for i in range(SEG):
            for r in range(NROW):
                out_ref[j, r, i] = res[i * SHIFTS + r * 8 : i * SHIFTS + (r + 1) * 8, :].astype(out_ref.dtype)


def score(panel, aligned):
    refs = NX * NY * NZ
    vmem = pl.BlockSpec(memory_space=pltpu.VMEM)
    return pl.pallas_call(
        score_kernel,
        in_specs=[vmem, pl.BlockSpec(memory_space=pltpu.HBM)],
        out_specs=vmem,
        out_shape=jax.ShapeDtypeStruct((NA, NROW, SEG, 8, refs), PARTIAL),
        scratch_shapes=[
            pltpu.VMEM((refs * D, COLS), f32),
            pltpu.VMEM((D * COLS, refs), bf16),
            pltpu.VMEM(aligned.shape, bf16),
            pltpu.SemaphoreType.DMA((NA,)),
        ],
        compiler_params=pltpu.CompilerParams(vmem_limit_bytes=20 << 20),
        cost_estimate=pl.CostEstimate(flops=1_100_000_000, bytes_accessed=10_000_000, transcendentals=0),
        name="score",
    )(panel, pltpu.with_memory_space_constraint(aligned, pltpu.HBM))


def contrast(defocus, kw, kx):
    radius = (kw * kw + kx * kx).astype(f32) / float(BOX * BOX)
    return -jnp.sin(200.0 * defocus * radius + 0.1)


def centred(ky):
    return (ky + BOX // 2) % BOX - BOX // 2


def per_device(images, defocus, references, offsets, posterior, class_ids, seg_count):
    row = lax.axis_index(ROW)
    fil = lax.axis_index(FIL)
    kx = jnp.arange(COLS, dtype=jnp.int32)
    kw_first = centred(row * 64 + lax.axis_index(("x", "zl")) * KY)
    place = jnp.stack([kw_first, lax.axis_index("zl")])

    send = pack(images, defocus, references, offsets, posterior, class_ids, seg_count)
    recv = lax.all_to_all(send, ("x", "zl"), 0, 0, tiled=True)
    panel = lax.all_to_all(chunk(place, recv), "yh", 0, 0, tiled=True)
    numer, meta, gx = front(place, recv)
    panel = lax.all_to_all(merge(panel, numer), ("zh", "zl"), 0, 0, tiled=True)
    aligned = align(place, gx, meta)

    numer = panel[:, Z_NUM:Z_FACT].astype(f32).reshape(NZ // 2, 2, 2, CLASSES, COLS)
    numer = jnp.sum(numer, axis=0).reshape(NY, CLASSES, COLS)
    numer, panel = lax.optimization_barrier((numer, panel))
    numer = lax.psum_scatter(numer, "yh", scatter_dimension=0, tiled=True)[0]

    partial = score(panel, aligned)
    partial = lax.all_to_all(
        partial.reshape(NA * NROW, SEG * 8, COLS), ("x", "zl", *ROW), 0, 0, tiled=True
    )
    scores = jnp.sum(partial.astype(f32), axis=0).reshape(SEG, 8, COLS)

    facts = panel[:, Z_FACT:Z_ROWS].astype(f32)
    all_defocus = (facts[:, 0] + facts[:, 1] + facts[:, 2]).reshape(-1)
    all_class = facts[:, 3].reshape(-1)
    all_total = ((facts[:, 5] * 32.0 + facts[:, 6]) * (1.0 / 256)).reshape(-1)
    ctf = contrast(all_defocus[:, None], centred(row * 64 + fil // 2), kx[None, :])
    classes = jnp.arange(CLASSES, dtype=f32)
    totals = jnp.where(all_class[None, :] == classes[:, None], all_total[None, :], 0.0)
    denom = jnp.dot(totals, ctf * ctf, precision=lax.Precision.HIGHEST, preferred_element_type=f32)
    averages = numer * lax.rsqrt(denom + 1.0)
    return scores, averages


def solution(mesh):
    fine = Mesh(mesh.devices.reshape(4, 4, 4, 2, 2, 2), (*FIL, *ROW))
    placed = (
        P(FIL, None, ROW, None),
        P(FIL),
        P(FIL, None, ROW, None),
        P(FIL, None, None),
        P(FIL, None),
        P(FIL),
        P(FIL),
    )
    return jax.shard_map(
        per_device,
        mesh=fine,
        in_specs=placed,
        out_specs=(P(FIL, ROW, None), P(None, (*ROW, *FIL))),
        check_vma=False,
    )
```

```python
import functools
import math

import jax
import jax.numpy as jnp
from jax import lax
from jax.experimental import pallas as pl
from jax.experimental.pallas import tpu as pltpu
from jax.sharding import Mesh
from jax.sharding import PartitionSpec as P

BOX = 256
SHIFTS = 32
CLASSES = 16
SEG = 8
NA = 8
NB = 32
NX = 4
NROW = 4
SEGS = NA * SEG
KY = 8
D = 2 * KY
COLS = 128
META = 8
A_REF = SEG * D
A_META = A_REF + 2 * D
A_ROWS = A_META + META
B_NUM = NX * D
B_ROWS = B_NUM + CLASSES
FIL = ("x", "yh", "zh", "zl")
ROW = ("yl", "core")
bf16 = jnp.bfloat16
f32 = jnp.float32
NEAR = 2
PARTIAL = bf16


def small_sincos(theta):
    t2 = theta * theta
    sin = theta * (1.0 + t2 * (-1.0 / 6 + t2 * (1.0 / 120 + t2 * (-1.0 / 5040 + t2 * (1.0 / 362880)))))
    cos = 1.0 + t2 * (-0.5 + t2 * (1.0 / 24 + t2 * (-1.0 / 720 + t2 * (1.0 / 40320 + t2 * (-1.0 / 3628800)))))
    return sin, cos


def quarter(n, sin, cos):
    quad = n - 4.0 * jnp.floor(n * 0.25)
    odd = (quad == 1.0) | (quad == 3.0)
    c = jnp.where(odd, sin, cos)
    s = jnp.where(odd, cos, sin)
    c = jnp.where((quad == 1.0) | (quad == 2.0), -c, c)
    return jnp.where(quad >= 2.0, -s, s), c


def turn(m):
    n = jnp.floor(m * (1.0 / 64) + 0.5)
    sin, cos = quarter(n, *small_sincos((m - 64.0 * n) * (math.pi / 128)))
    return cos, -sin


def sine(arg):
    n = jnp.floor(arg * (2.0 / math.pi) + 0.5)
    rest = ((arg - n * 1.5703125) - n * 4.837512969970703125e-4) - n * 7.54978995489188216e-8
    return quarter(n, *small_sincos(rest))[0]


def halves(v):
    hi = v.astype(bf16)
    return hi, (v - hi.astype(f32)).astype(bf16)


def parts_of(v):
    hi = v.astype(bf16).astype(f32)
    rest = v - hi
    mid = rest.astype(bf16).astype(f32)
    return hi, mid, rest - mid


def pack_kernel(*refs):
    count_ref, given, out_ref, held, meta_ref, sems = refs[0], refs[1:7], refs[7], refs[8:14], refs[14], refs[15]
    copies = [pltpu.make_async_copy(src, dst, sems.at[k]) for k, (src, dst) in enumerate(zip(given, held))]
    for copy in copies:
        copy.start()
    for copy in copies:
        copy.wait()
    defocus_ref, class_ref, img_ref, ref_ref, off_ref, post_ref = held
    sub = lax.broadcasted_iota(jnp.int32, (META, COLS), 0)
    lane = lax.broadcasted_iota(jnp.int32, (META, COLS), 1)
    live = (sub < count_ref[0]).astype(f32)
    defocus = jnp.zeros((META, COLS), f32)
    ids = jnp.zeros((META, COLS), f32)
    for i in range(SEG):
        defocus = jnp.where(sub == i, defocus_ref[i], defocus)
        ids = jnp.where(sub == i, class_ref[i].astype(f32), ids)
    hi, mid, low = parts_of(defocus)
    facts = jnp.where(lane == 96, hi, jnp.where(lane == 97, mid, jnp.where(lane == 98, low, 0.0)))
    facts = jnp.where(lane == 99, ids, jnp.where(lane == 100, live, facts))
    meta_ref[...] = facts
    for i in range(SEG):
        both = off_ref[i].astype(f32)
        meta_ref[i : i + 1, 0:SHIFTS] = both[0:1]
        meta_ref[i : i + 1, SHIFTS : 2 * SHIFTS] = both[1:2]
    meta_ref[0:SEG, 2 * SHIFTS : 3 * SHIFTS] = post_ref[...].astype(f32) * live[0:SEG, 0:SHIFTS]
    meta = meta_ref[...].astype(bf16)
    for j in range(NA):
        for p in range(2):
            for i in range(SEG):
                out_ref[j, i * D + p * KY : i * D + (p + 1) * KY] = img_ref[i, p, j * KY : (j + 1) * KY]
            for half in range(2):
                base = A_REF + half * D + p * KY
                first = (j // 2) * 2 * KY + half * KY
                out_ref[j, base : base + KY] = ref_ref[0, p, first : first + KY]
        out_ref[j, A_META:A_ROWS] = meta


def pack(images, defocus, references, offsets, posterior, class_ids, seg_count):
    given = (defocus, class_ids, images, references, offsets.transpose(0, 2, 1), posterior)
    places = (pltpu.SMEM,) * 2 + (pltpu.VMEM,) * 4
    return pl.pallas_call(
        pack_kernel,
        in_specs=[pl.BlockSpec(memory_space=pltpu.SMEM)] + [pl.BlockSpec(memory_space=pltpu.HBM)] * 6,
        out_specs=pl.BlockSpec(memory_space=pltpu.VMEM),
        out_shape=jax.ShapeDtypeStruct((NA, A_ROWS, COLS), bf16),
        scratch_shapes=[place(v.shape, v.dtype) for place, v in zip(places, given)]
        + [pltpu.VMEM((META, COLS), f32), pltpu.SemaphoreType.DMA((6,))],
        compiler_params=pltpu.CompilerParams(vmem_limit_bytes=4 << 20),
        cost_estimate=pl.CostEstimate(flops=100_000, bytes_accessed=700_000, transcendentals=0),
        name="pack",
    )(seg_count, *(pltpu.with_memory_space_constraint(v, pltpu.HBM) for v in given))


def front_kernel(place_ref, recv_ref, out_ref, meta_out_ref, gx_ref, wide_ref, y_ref, col_ref):
    kw0 = place_ref[0]
    zl = place_ref[1]
    lane = lax.broadcasted_iota(jnp.int32, (KY, COLS), 1)
    sub = lax.broadcasted_iota(jnp.int32, (KY, COLS), 0)
    kw = (sub + kw0).astype(f32)
    kx = lane.astype(f32)
    radius = (kw * kw + kx * kx) * (1.0 / (BOX * BOX))
    first = (lane % (2 * SHIFTS)) < SHIFTS
    lane_s = lax.broadcasted_iota(jnp.int32, (SHIFTS, COLS), 1)
    sub_s = lax.broadcasted_iota(jnp.int32, (SHIFTS, COLS), 0)

    c, s = turn((sub_s - 8).astype(f32) * lane_s.astype(f32))
    (c_hi, c_lo), (s_hi, s_lo) = halves(c), halves(s)
    table = jnp.concatenate([c_hi, s_hi, c_lo, s_lo], axis=1)

    for a in range(NA):
        meta = recv_ref[a, A_META:A_ROWS].astype(f32)
        rows = slice(a * SEG, (a + 1) * SEG)
        meta_out_ref[rows] = meta
        wide_ref[rows] = meta
        wide_ref[SEGS + a * SEG : SEGS + (a + 1) * SEG] = meta

        def pick(at):
            return jnp.sum(jnp.where(lane == at, meta, 0.0), axis=1, keepdims=True)

        defocus = jnp.broadcast_to(pick(96) + pick(97) + pick(98), (SEG, COLS))
        alive = jnp.broadcast_to(pick(100), (SEG, COLS))
        sy = jnp.where(lane < SHIFTS, meta, 0.0)
        sy = sy + pltpu.roll(sy, SHIFTS, 1)
        sy = sy + pltpu.roll(sy, 2 * SHIFTS, 1)
        w = jnp.where((lane >= 2 * SHIFTS) & (lane < 3 * SHIFTS), meta, 0.0) * (1.0 / 256)
        w = w + pltpu.roll(w, SHIFTS, 1)
        w = w + pltpu.roll(w, 2 * SHIFTS, 1)

        hot = []
        for i in range(SEG):
            spread = jnp.broadcast_to(meta[i : i + 1], (SHIFTS, COLS))
            sx = jnp.sum(jnp.where(lane_s == sub_s + SHIFTS, spread, 0.0), axis=1, keepdims=True)
            hot.append((jnp.broadcast_to(sx, (SHIFTS, SHIFTS)) == (lane_s[:, :SHIFTS] - 8).astype(f32)).astype(f32).astype(bf16))
        col_ref[...] = jnp.dot(jnp.concatenate(hot, axis=0), table, preferred_element_type=f32).astype(bf16)

        for i in range(SEG):
            c, s = turn(jnp.broadcast_to(sy[i : i + 1], (KY, COLS)) * kw)
            wi = jnp.broadcast_to(w[i : i + 1], (KY, COLS))
            c, s = c * wi, s * wi
            left = jnp.concatenate([jnp.where(first, c, -s), jnp.where(first, s, c)], axis=0)
            hi, lo = halves(left)
            right = jnp.concatenate(
                [col_ref[i * SHIFTS : (i + 1) * SHIFTS, q * COLS : (q + 1) * COLS] for q in range(4)], axis=0
            )
            both = jnp.dot(jnp.concatenate([hi, lo], axis=0), right, preferred_element_type=f32)
            q_re = both[0:KY] + both[D : D + KY]
            q_im = both[KY:D] + both[D + KY : 2 * D]
            arg = (200.0 * jnp.broadcast_to(defocus[i : i + 1], (KY, COLS))) * radius + 0.1
            gain = -sine(arg) * jnp.broadcast_to(alive[i : i + 1], (KY, COLS))
            img = recv_ref[a, i * D : (i + 1) * D].astype(f32)
            xr, xi = img[0:KY] * gain, img[KY:D] * gain
            at = (a * SEG + i) * D
            gx_ref[at : at + KY] = xr
            gx_ref[at + KY : at + D] = xi
            y_ref[at : at + KY] = xr * q_re - xi * q_im
            y_ref[at + KY : at + D] = xr * q_im + xi * q_re

    flat = wide_ref[...].T
    ids = jnp.broadcast_to(flat[99:100], (CLASSES, COLS))
    member = (ids == lax.broadcasted_iota(jnp.int32, (CLASSES, COLS), 0).astype(f32)).astype(f32).astype(bf16)
    for p in range(2):
        for ky in range(KY):
            hi, lo = halves(y_ref[pl.ds(p * KY + ky, SEGS, stride=D), :])
            sums = jnp.dot(member, jnp.concatenate([hi, lo], axis=0), preferred_element_type=f32)
            out_ref[zl * D + 2 * ky + p, B_NUM:B_ROWS] = sums.astype(bf16)

    total = jnp.sum(flat[2 * SHIFTS : 3 * SHIFTS], axis=0, keepdims=True)
    total_hi = jnp.floor(total * (1.0 / 32))
    facts = jnp.where(sub == 5, total_hi, jnp.where(sub == 6, total - 32.0 * total_hi, flat[96:104]))
    facts = jnp.concatenate([facts, jnp.zeros((CLASSES - META, COLS), f32)], axis=0).astype(bf16)
    for q in range(D):
        out_ref[(1 - zl) * D + q, B_NUM:B_ROWS] = facts
    for half in range(2):
        refs = [recv_ref[2 * x + zl, A_REF + half * D : A_REF + (half + 1) * D] for x in range(NX)]
        for q in range(half, NB, 2):
            for x in range(NX):
                out_ref[q, x * D : (x + 1) * D] = refs[x]


def front(place, recv):
    vmem = pl.BlockSpec(memory_space=pltpu.VMEM)
    return pl.pallas_call(
        front_kernel,
        in_specs=[pl.BlockSpec(memory_space=pltpu.SMEM), vmem],
        out_specs=[vmem, vmem, vmem],
        out_shape=[
            jax.ShapeDtypeStruct((NB, B_ROWS, COLS), bf16),
            jax.ShapeDtypeStruct((SEGS, COLS), f32),
            jax.ShapeDtypeStruct((SEGS * D, COLS), f32),
        ],
        scratch_shapes=[
            pltpu.VMEM((COLS, COLS), f32),
            pltpu.VMEM((SEGS * D, COLS), f32),
            pltpu.VMEM((SEG * SHIFTS, 4 * COLS), bf16),
        ],
        compiler_params=pltpu.CompilerParams(vmem_limit_bytes=8 << 20),
        cost_estimate=pl.CostEstimate(flops=100_000_000, bytes_accessed=2_000_000, transcendentals=0),
        name="front",
    )(place, recv)


def align_kernel(place_ref, gx_ref, meta_ref, near_ref, far_ref):
    step = pl.program_id(0)
    kw0 = place_ref[0].astype(f32)
    lane = lax.broadcasted_iota(jnp.int32, (SHIFTS, COLS), 1)
    sub = lax.broadcasted_iota(jnp.int32, (SHIFTS, COLS), 0)
    kx = lane.astype(f32)

    def segment(aligned_ref, i, carry):
        wide = jnp.broadcast_to(meta_ref[pl.ds(i, 1), :], (SHIFTS, COLS))
        sy = jnp.sum(jnp.where(lane == sub, wide, 0.0), axis=1, keepdims=True)
        sx = jnp.sum(jnp.where(lane == sub + SHIFTS, wide, 0.0), axis=1, keepdims=True)
        sy = jnp.broadcast_to(sy, (SHIFTS, COLS))
        pr, pi = turn(sy * kw0 + sx * kx)
        si, cr = small_sincos(sy * (-2.0 * math.pi / BOX))
        rows = pl.ds(pl.multiple_of(i * SHIFTS, SHIFTS), SHIFTS)
        for ky in range(KY):
            xr = gx_ref[pl.ds(i * D + ky, 1), :]
            xi = gx_ref[pl.ds(i * D + KY + ky, 1), :]
            aligned_ref[rows, ky * COLS : (ky + 1) * COLS] = (xr * pr - xi * pi).astype(bf16)
            aligned_ref[rows, (KY + ky) * COLS : (KY + ky + 1) * COLS] = (xr * pi + xi * pr).astype(bf16)
            if ky < KY - 1:
                pr, pi = pr * cr - pi * si, pr * si + pi * cr
        return carry

    @pl.when(step < NEAR)
    def _():
        lax.fori_loop(0, SEG, functools.partial(segment, near_ref), 0)

    @pl.when(step >= NEAR)
    def _():
        lax.fori_loop(0, SEG, functools.partial(segment, far_ref), 0)


def align(place, gx, meta):
    return pl.pallas_call(
        align_kernel,
        grid=(NA,),
        in_specs=[
            pl.BlockSpec(memory_space=pltpu.SMEM),
            pl.BlockSpec((SEG * D, COLS), lambda j: (j, 0)),
            pl.BlockSpec((SEG, COLS), lambda j: (j, 0)),
        ],
        out_specs=[
            pl.BlockSpec((SEG * SHIFTS, D * COLS), lambda j: (jnp.minimum(j, NEAR - 1), 0)),
            pl.BlockSpec((SEG * SHIFTS, D * COLS), lambda j: (jnp.maximum(j - NEAR, 0), 0)),
        ],
        out_shape=[
            jax.ShapeDtypeStruct((NEAR * SEG * SHIFTS, D * COLS), bf16),
            pltpu.HBM(((NA - NEAR) * SEG * SHIFTS, D * COLS), bf16),
        ],
        compiler_params=pltpu.CompilerParams(vmem_limit_bytes=10 << 20),
        cost_estimate=pl.CostEstimate(flops=600_000_000, bytes_accessed=9_000_000, transcendentals=0),
        name="align",
    )(place, gx, meta)


def score_kernel(panel_ref, near_ref, far_ref, out_ref, wide_ref, packed_ref, held_ref, sems):
    refs = NX * NB
    block = SEG * SHIFTS
    copies = [
        pltpu.make_async_copy(
            far_ref.at[j * block : (j + 1) * block], held_ref.at[j * block : (j + 1) * block], sems.at[j]
        )
        for j in range(NA - NEAR)
    ]
    for copy in copies:
        copy.start()

    def widen(q, carry):
        for x in range(NX):
            base = pl.multiple_of((x * NB + q) * D, D)
            wide_ref[pl.ds(base, D), :] = panel_ref[q, x * D : (x + 1) * D, :].astype(f32)
        return carry

    lax.fori_loop(0, NB, widen, 0)
    for d in range(D):
        packed_ref[d * COLS : (d + 1) * COLS, :] = wide_ref[pl.ds(d, refs, stride=D), :].T.astype(bf16)

    for j in range(NA):
        if j < NEAR:
            left = near_ref[j * block : (j + 1) * block]
        else:
            copies[j - NEAR].wait()
            left = held_ref[(j - NEAR) * block : (j - NEAR + 1) * block]
        res = jnp.dot(left, packed_ref[...], preferred_element_type=f32)
        for i in range(SEG):
            for r in range(NROW):
                out_ref[j, r, i] = res[i * SHIFTS + r * 8 : i * SHIFTS + (r + 1) * 8, :].astype(out_ref.dtype)


def score(panel, near, far):
    refs = NX * NB
    vmem = pl.BlockSpec(memory_space=pltpu.VMEM)
    return pl.pallas_call(
        score_kernel,
        in_specs=[vmem, vmem, pl.BlockSpec(memory_space=pltpu.HBM)],
        out_specs=vmem,
        out_shape=jax.ShapeDtypeStruct((NA, NROW, SEG, 8, refs), PARTIAL),
        scratch_shapes=[
            pltpu.VMEM((refs * D, COLS), f32),
            pltpu.VMEM((D * COLS, refs), bf16),
            pltpu.VMEM(far.shape, bf16),
            pltpu.SemaphoreType.DMA((NA - NEAR,)),
        ],
        compiler_params=pltpu.CompilerParams(vmem_limit_bytes=20 << 20),
        cost_estimate=pl.CostEstimate(flops=1_100_000_000, bytes_accessed=10_000_000, transcendentals=0),
        name="score",
    )(panel, near, pltpu.with_memory_space_constraint(far, pltpu.HBM))


def contrast(defocus, kw, kx):
    radius = (kw * kw + kx * kx).astype(f32) / float(BOX * BOX)
    return -jnp.sin(200.0 * defocus * radius + 0.1)


def centred(ky):
    return (ky + BOX // 2) % BOX - BOX // 2


def per_device(images, defocus, references, offsets, posterior, class_ids, seg_count):
    row = lax.axis_index(ROW)
    fil = lax.axis_index(FIL)
    kx = jnp.arange(COLS, dtype=jnp.int32)
    kw_first = centred(row * 64 + lax.axis_index(("x", "zl")) * KY)
    place = jnp.stack([kw_first, lax.axis_index("zl")])

    send = pack(images, defocus, references, offsets, posterior, class_ids, seg_count)
    recv = lax.all_to_all(send, ("x", "zl"), 0, 0, tiled=True)
    sent, meta, gx = front(place, recv)
    panel = lax.all_to_all(sent, ("yh", "zh", "zl"), 0, 0, tiled=True)
    near, far = align(place, gx, meta)
    partial = score(panel, near, far)
    partial = lax.all_to_all(
        partial.reshape(NA * NROW, SEG * 8, COLS), ("x", "zl", *ROW), 0, 0, tiled=True
    )
    scores = jnp.sum(partial.astype(f32), axis=0).reshape(SEG, 8, COLS)

    owner = lax.axis_index("yh") // 2
    rest = panel[:, B_NUM:B_ROWS].reshape(NB // 2, 2, CLASSES, COLS)
    numer = jnp.where(owner == 0, rest[:, 0], rest[:, 1]).astype(f32)
    numer = jnp.sum(numer, axis=0)
    facts = jnp.where(owner == 0, rest[:, 1, :, :SEGS], rest[:, 0, :, :SEGS]).astype(f32)
    all_defocus = (facts[:, 0] + facts[:, 1] + facts[:, 2]).reshape(-1)
    all_class = facts[:, 3].reshape(-1)
    all_total = ((facts[:, 5] * 32.0 + facts[:, 6]) * (1.0 / 256)).reshape(-1)
    ctf = contrast(all_defocus[:, None], centred(row * 64 + fil // 2), kx[None, :])
    classes = jnp.arange(CLASSES, dtype=f32)
    totals = jnp.where(all_class[None, :] == classes[:, None], all_total[None, :], 0.0)
    denom = jnp.dot(totals, ctf * ctf, precision=lax.Precision.HIGHEST, preferred_element_type=f32)
    averages = numer * lax.rsqrt(denom + 1.0)
    return scores, averages


def solution(mesh):
    fine = Mesh(mesh.devices.reshape(4, 4, 4, 2, 2, 2), (*FIL, *ROW))
    placed = (
        P(FIL, None, ROW, None),
        P(FIL),
        P(FIL, None, ROW, None),
        P(FIL, None, None),
        P(FIL, None),
        P(FIL),
        P(FIL),
    )
    return jax.shard_map(
        per_device,
        mesh=fine,
        in_specs=placed,
        out_specs=(P(FIL, ROW, None), P(None, (*ROW, *FIL))),
        check_vma=False,
    )
```

```python
import functools
import math

import jax
import jax.numpy as jnp
from jax import lax
from jax.experimental import pallas as pl
from jax.experimental.pallas import tpu as pltpu
from jax.sharding import Mesh
from jax.sharding import PartitionSpec as P

BOX = 256
SHIFTS = 32
CLASSES = 16
SEG = 8
NA = 8
NB = 32
NX = 4
NROW = 4
SEGS = NA * SEG
KY = 8
D = 2 * KY
COLS = 128
META = 8
A_REF = SEG * D
A_META = A_REF + 2 * D
A_ROWS = A_META + META
B_NUM = NX * D
B_ROWS = B_NUM + CLASSES
FIL = ("x", "yh", "zh", "zl")
ROW = ("yl", "core")
bf16 = jnp.bfloat16
f32 = jnp.float32
NEAR = 2
PARTIAL = bf16


def small_sincos(theta):
    t2 = theta * theta
    sin = theta * (1.0 + t2 * (-1.0 / 6 + t2 * (1.0 / 120 + t2 * (-1.0 / 5040 + t2 * (1.0 / 362880)))))
    cos = 1.0 + t2 * (-0.5 + t2 * (1.0 / 24 + t2 * (-1.0 / 720 + t2 * (1.0 / 40320 + t2 * (-1.0 / 3628800)))))
    return sin, cos


def quarter(n, sin, cos):
    quad = n - 4.0 * jnp.floor(n * 0.25)
    odd = (quad == 1.0) | (quad == 3.0)
    c = jnp.where(odd, sin, cos)
    s = jnp.where(odd, cos, sin)
    c = jnp.where((quad == 1.0) | (quad == 2.0), -c, c)
    return jnp.where(quad >= 2.0, -s, s), c


def turn(m):
    n = jnp.floor(m * (1.0 / 64) + 0.5)
    sin, cos = quarter(n, *small_sincos((m - 64.0 * n) * (math.pi / 128)))
    return cos, -sin


def sine(arg):
    n = jnp.floor(arg * (2.0 / math.pi) + 0.5)
    rest = ((arg - n * 1.5703125) - n * 4.837512969970703125e-4) - n * 7.54978995489188216e-8
    return quarter(n, *small_sincos(rest))[0]


def halves(v):
    hi = v.astype(bf16)
    return hi, (v - hi.astype(f32)).astype(bf16)


def parts_of(v):
    hi = v.astype(bf16).astype(f32)
    rest = v - hi
    mid = rest.astype(bf16).astype(f32)
    return hi, mid, rest - mid


def pack_kernel(*refs):
    count_ref, given, out_ref, held, meta_ref, sems = refs[0], refs[1:7], refs[7], refs[8:14], refs[14], refs[15]
    copies = [pltpu.make_async_copy(src, dst, sems.at[k]) for k, (src, dst) in enumerate(zip(given, held))]
    for copy in copies:
        copy.start()
    for copy in copies:
        copy.wait()
    defocus_ref, class_ref, img_ref, ref_ref, off_ref, post_ref = held
    sub = lax.broadcasted_iota(jnp.int32, (META, COLS), 0)
    lane = lax.broadcasted_iota(jnp.int32, (META, COLS), 1)
    live = (sub < count_ref[0]).astype(f32)
    defocus = jnp.zeros((META, COLS), f32)
    ids = jnp.zeros((META, COLS), f32)
    for i in range(SEG):
        defocus = jnp.where(sub == i, defocus_ref[i], defocus)
        ids = jnp.where(sub == i, class_ref[i].astype(f32), ids)
    hi, mid, low = parts_of(defocus)
    facts = jnp.where(lane == 96, hi, jnp.where(lane == 97, mid, jnp.where(lane == 98, low, 0.0)))
    facts = jnp.where(lane == 99, ids, jnp.where(lane == 100, live, facts))
    meta_ref[...] = facts
    for i in range(SEG):
        both = off_ref[i].astype(f32)
        meta_ref[i : i + 1, 0:SHIFTS] = both[0:1]
        meta_ref[i : i + 1, SHIFTS : 2 * SHIFTS] = both[1:2]
    meta_ref[0:SEG, 2 * SHIFTS : 3 * SHIFTS] = post_ref[...].astype(f32) * live[0:SEG, 0:SHIFTS]
    meta = meta_ref[...].astype(bf16)
    for j in range(NA):
        for p in range(2):
            for i in range(SEG):
                out_ref[j, i * D + p * KY : i * D + (p + 1) * KY] = img_ref[i, p, j * KY : (j + 1) * KY]
            for half in range(2):
                base = A_REF + half * D + p * KY
                first = (j // 2) * 2 * KY + half * KY
                out_ref[j, base : base + KY] = ref_ref[0, p, first : first + KY]
        out_ref[j, A_META:A_ROWS] = meta


def pack(images, defocus, references, offsets, posterior, class_ids, seg_count):
    given = (defocus, class_ids, images, references, offsets.transpose(0, 2, 1), posterior)
    places = (pltpu.SMEM,) * 2 + (pltpu.VMEM,) * 4
    return pl.pallas_call(
        pack_kernel,
        in_specs=[pl.BlockSpec(memory_space=pltpu.SMEM)] + [pl.BlockSpec(memory_space=pltpu.HBM)] * 6,
        out_specs=pl.BlockSpec(memory_space=pltpu.VMEM),
        out_shape=jax.ShapeDtypeStruct((NA, A_ROWS, COLS), bf16),
        scratch_shapes=[place(v.shape, v.dtype) for place, v in zip(places, given)]
        + [pltpu.VMEM((META, COLS), f32), pltpu.SemaphoreType.DMA((6,))],
        compiler_params=pltpu.CompilerParams(vmem_limit_bytes=4 << 20),
        cost_estimate=pl.CostEstimate(flops=100_000, bytes_accessed=700_000, transcendentals=0),
        name="pack",
    )(seg_count, *(pltpu.with_memory_space_constraint(v, pltpu.HBM) for v in given))


def front_kernel(place_ref, recv_ref, out_ref, meta_out_ref, gx_ref, wide_ref, y_ref, col_ref):
    kw0 = place_ref[0]
    zl = place_ref[1]
    lane = lax.broadcasted_iota(jnp.int32, (KY, COLS), 1)
    sub = lax.broadcasted_iota(jnp.int32, (KY, COLS), 0)
    kw = (sub + kw0).astype(f32)
    kx = lane.astype(f32)
    radius = (kw * kw + kx * kx) * (1.0 / (BOX * BOX))
    first = (lane % (2 * SHIFTS)) < SHIFTS
    lane_s = lax.broadcasted_iota(jnp.int32, (SHIFTS, COLS), 1)
    sub_s = lax.broadcasted_iota(jnp.int32, (SHIFTS, COLS), 0)

    c, s = turn((sub_s - 8).astype(f32) * lane_s.astype(f32))
    (c_hi, c_lo), (s_hi, s_lo) = halves(c), halves(s)
    table = jnp.concatenate([c_hi, s_hi, c_lo, s_lo], axis=1)

    for a in range(NA):
        meta = recv_ref[a, A_META:A_ROWS].astype(f32)
        rows = slice(a * SEG, (a + 1) * SEG)
        meta_out_ref[rows] = meta
        wide_ref[rows] = meta
        wide_ref[SEGS + a * SEG : SEGS + (a + 1) * SEG] = meta

        def pick(at):
            return jnp.sum(jnp.where(lane == at, meta, 0.0), axis=1, keepdims=True)

        defocus = jnp.broadcast_to(pick(96) + pick(97) + pick(98), (SEG, COLS))
        alive = jnp.broadcast_to(pick(100), (SEG, COLS))
        sy = jnp.where(lane < SHIFTS, meta, 0.0)
        sy = sy + pltpu.roll(sy, SHIFTS, 1)
        sy = sy + pltpu.roll(sy, 2 * SHIFTS, 1)
        w = jnp.where((lane >= 2 * SHIFTS) & (lane < 3 * SHIFTS), meta, 0.0) * (1.0 / 256)
        w = w + pltpu.roll(w, SHIFTS, 1)
        w = w + pltpu.roll(w, 2 * SHIFTS, 1)

        hot = []
        for i in range(SEG):
            spread = jnp.broadcast_to(meta[i : i + 1], (SHIFTS, COLS))
            sx = jnp.sum(jnp.where(lane_s == sub_s + SHIFTS, spread, 0.0), axis=1, keepdims=True)
            hot.append((jnp.broadcast_to(sx, (SHIFTS, SHIFTS)) == (lane_s[:, :SHIFTS] - 8).astype(f32)).astype(f32).astype(bf16))
        col_ref[...] = jnp.dot(jnp.concatenate(hot, axis=0), table, preferred_element_type=f32).astype(bf16)

        for i in range(SEG):
            c, s = turn(jnp.broadcast_to(sy[i : i + 1], (KY, COLS)) * kw)
            wi = jnp.broadcast_to(w[i : i + 1], (KY, COLS))
            c, s = c * wi, s * wi
            left = jnp.concatenate([jnp.where(first, c, -s), jnp.where(first, s, c)], axis=0)
            hi, lo = halves(left)
            right = jnp.concatenate(
                [col_ref[i * SHIFTS : (i + 1) * SHIFTS, q * COLS : (q + 1) * COLS] for q in range(4)], axis=0
            )
            both = jnp.dot(jnp.concatenate([hi, lo], axis=0), right, preferred_element_type=f32)
            q_re = both[0:KY] + both[D : D + KY]
            q_im = both[KY:D] + both[D + KY : 2 * D]
            arg = (200.0 * jnp.broadcast_to(defocus[i : i + 1], (KY, COLS))) * radius + 0.1
            gain = -sine(arg) * jnp.broadcast_to(alive[i : i + 1], (KY, COLS))
            img = recv_ref[a, i * D : (i + 1) * D].astype(f32)
            xr, xi = img[0:KY] * gain, img[KY:D] * gain
            at = (a * SEG + i) * D
            gx_ref[at : at + KY] = xr
            gx_ref[at + KY : at + D] = xi
            y_ref[at : at + KY] = xr * q_re - xi * q_im
            y_ref[at + KY : at + D] = xr * q_im + xi * q_re

    flat = wide_ref[...].T
    ids = jnp.broadcast_to(flat[99:100], (CLASSES, COLS))
    member = (ids == lax.broadcasted_iota(jnp.int32, (CLASSES, COLS), 0).astype(f32)).astype(f32).astype(bf16)
    for p in range(2):
        for ky in range(KY):
            hi, lo = halves(y_ref[pl.ds(p * KY + ky, SEGS, stride=D), :])
            sums = jnp.dot(member, jnp.concatenate([hi, lo], axis=0), preferred_element_type=f32)
            out_ref[zl * D + 2 * ky + p, B_NUM:B_ROWS] = sums.astype(bf16)

    total = jnp.sum(flat[2 * SHIFTS : 3 * SHIFTS], axis=0, keepdims=True)
    total_hi = jnp.floor(total * (1.0 / 32))
    facts = jnp.where(sub == 5, total_hi, jnp.where(sub == 6, total - 32.0 * total_hi, flat[96:104]))
    facts = jnp.concatenate([facts, jnp.zeros((CLASSES - META, COLS), f32)], axis=0).astype(bf16)
    for q in range(D):
        out_ref[(1 - zl) * D + q, B_NUM:B_ROWS] = facts
    for half in range(2):
        refs = [recv_ref[2 * x + zl, A_REF + half * D : A_REF + (half + 1) * D] for x in range(NX)]
        for q in range(half, NB, 2):
            for x in range(NX):
                out_ref[q, x * D : (x + 1) * D] = refs[x]


def front(place, recv):
    vmem = pl.BlockSpec(memory_space=pltpu.VMEM)
    return pl.pallas_call(
        front_kernel,
        in_specs=[pl.BlockSpec(memory_space=pltpu.SMEM), vmem],
        out_specs=[vmem, vmem, vmem],
        out_shape=[
            jax.ShapeDtypeStruct((NB, B_ROWS, COLS), bf16),
            jax.ShapeDtypeStruct((SEGS, COLS), f32),
            jax.ShapeDtypeStruct((SEGS * D, COLS), f32),
        ],
        scratch_shapes=[
            pltpu.VMEM((COLS, COLS), f32),
            pltpu.VMEM((SEGS * D + D, COLS), f32),
            pltpu.VMEM((SEG * SHIFTS, 4 * COLS), bf16),
        ],
        compiler_params=pltpu.CompilerParams(vmem_limit_bytes=8 << 20),
        cost_estimate=pl.CostEstimate(flops=100_000_000, bytes_accessed=2_000_000, transcendentals=0),
        name="front",
    )(place, recv)


def align_kernel(place_ref, gx_ref, meta_ref, near_ref, far_ref):
    step = pl.program_id(0)
    kw0 = place_ref[0].astype(f32)
    lane = lax.broadcasted_iota(jnp.int32, (SHIFTS, COLS), 1)
    sub = lax.broadcasted_iota(jnp.int32, (SHIFTS, COLS), 0)
    kx = lane.astype(f32)

    def segment(aligned_ref, i, carry):
        wide = jnp.broadcast_to(meta_ref[pl.ds(i, 1), :], (SHIFTS, COLS))
        sy = jnp.sum(jnp.where(lane == sub, wide, 0.0), axis=1, keepdims=True)
        sx = jnp.sum(jnp.where(lane == sub + SHIFTS, wide, 0.0), axis=1, keepdims=True)
        sy = jnp.broadcast_to(sy, (SHIFTS, COLS))
        pr, pi = turn(sy * kw0 + sx * kx)
        si, cr = small_sincos(sy * (-2.0 * math.pi / BOX))
        rows = pl.ds(pl.multiple_of(i * SHIFTS, SHIFTS), SHIFTS)
        for ky in range(KY):
            xr = gx_ref[pl.ds(i * D + ky, 1), :]
            xi = gx_ref[pl.ds(i * D + KY + ky, 1), :]
            aligned_ref[rows, ky * COLS : (ky + 1) * COLS] = (xr * pr - xi * pi).astype(bf16)
            aligned_ref[rows, (KY + ky) * COLS : (KY + ky + 1) * COLS] = (xr * pi + xi * pr).astype(bf16)
            if ky < KY - 1:
                pr, pi = pr * cr - pi * si, pr * si + pi * cr
        return carry

    @pl.when(step < NEAR)
    def _():
        lax.fori_loop(0, SEG, functools.partial(segment, near_ref), 0)

    @pl.when(step >= NEAR)
    def _():
        lax.fori_loop(0, SEG, functools.partial(segment, far_ref), 0)


def align(place, gx, meta):
    return pl.pallas_call(
        align_kernel,
        grid=(NA,),
        in_specs=[
            pl.BlockSpec(memory_space=pltpu.SMEM),
            pl.BlockSpec((SEG * D, COLS), lambda j: (j, 0)),
            pl.BlockSpec((SEG, COLS), lambda j: (j, 0)),
        ],
        out_specs=[
            pl.BlockSpec((SEG * SHIFTS, D * COLS), lambda j: (jnp.minimum(j, NEAR - 1), 0)),
            pl.BlockSpec((SEG * SHIFTS, D * COLS), lambda j: (jnp.maximum(j - NEAR, 0), 0)),
        ],
        out_shape=[
            jax.ShapeDtypeStruct((NEAR * SEG * SHIFTS, D * COLS), bf16),
            pltpu.HBM(((NA - NEAR) * SEG * SHIFTS, D * COLS), bf16),
        ],
        compiler_params=pltpu.CompilerParams(vmem_limit_bytes=10 << 20),
        cost_estimate=pl.CostEstimate(flops=600_000_000, bytes_accessed=9_000_000, transcendentals=0),
        name="align",
    )(place, gx, meta)


def score_kernel(panel_ref, near_ref, far_ref, out_ref, wide_ref, packed_ref, held_ref, made_ref, sems, out_sems):
    refs = NX * NB
    block = SEG * SHIFTS
    copies = [
        pltpu.make_async_copy(
            far_ref.at[j * block : (j + 1) * block], held_ref.at[j * block : (j + 1) * block], sems.at[j]
        )
        for j in range(NA - NEAR)
    ]
    for copy in copies:
        copy.start()

    def widen(q, carry):
        for x in range(NX):
            base = pl.multiple_of((x * NB + q) * D, D)
            wide_ref[pl.ds(base, D), :] = panel_ref[q, x * D : (x + 1) * D, :].astype(f32)
        return carry

    lax.fori_loop(0, NB, widen, 0)
    for d in range(D):
        packed_ref[d * COLS : (d + 1) * COLS, :] = wide_ref[pl.ds(d, refs, stride=D), :].T.astype(bf16)

    done = []
    for j in range(NA):
        if j < NEAR:
            left = near_ref[j * block : (j + 1) * block]
        else:
            copies[j - NEAR].wait()
            left = held_ref[(j - NEAR) * block : (j - NEAR + 1) * block]
        res = jnp.dot(left, packed_ref[...], preferred_element_type=f32)
        for i in range(SEG):
            for r in range(NROW):
                made_ref[j, r, i] = res[i * SHIFTS + r * 8 : i * SHIFTS + (r + 1) * 8, :].astype(out_ref.dtype)
        done.append(pltpu.make_async_copy(made_ref.at[j], out_ref.at[j], out_sems.at[j]))
        done[-1].start()
    for copy in done:
        copy.wait()


def score(panel, near, far):
    refs = NX * NB
    vmem = pl.BlockSpec(memory_space=pltpu.VMEM)
    return pl.pallas_call(
        score_kernel,
        in_specs=[vmem, vmem, pl.BlockSpec(memory_space=pltpu.HBM)],
        out_specs=pl.BlockSpec(memory_space=pltpu.HBM),
        out_shape=pltpu.HBM((NA, NROW, SEG, 8, refs), PARTIAL),
        scratch_shapes=[
            pltpu.VMEM((refs * D + D, COLS), f32),
            pltpu.VMEM((D * COLS, refs), bf16),
            pltpu.VMEM(far.shape, bf16),
            pltpu.VMEM((NA, NROW, SEG, 8, refs), PARTIAL),
            pltpu.SemaphoreType.DMA((NA - NEAR,)),
            pltpu.SemaphoreType.DMA((NA,)),
        ],
        compiler_params=pltpu.CompilerParams(vmem_limit_bytes=20 << 20),
        cost_estimate=pl.CostEstimate(flops=1_100_000_000, bytes_accessed=10_000_000, transcendentals=0),
        name="score",
    )(panel, near, pltpu.with_memory_space_constraint(far, pltpu.HBM))


def contrast(defocus, kw, kx):
    radius = (kw * kw + kx * kx).astype(f32) / float(BOX * BOX)
    return -jnp.sin(200.0 * defocus * radius + 0.1)


def centred(ky):
    return (ky + BOX // 2) % BOX - BOX // 2


def per_device(images, defocus, references, offsets, posterior, class_ids, seg_count):
    row = lax.axis_index(ROW)
    fil = lax.axis_index(FIL)
    kx = jnp.arange(COLS, dtype=jnp.int32)
    kw_first = centred(row * 64 + lax.axis_index(("x", "zl")) * KY)
    place = jnp.stack([kw_first, lax.axis_index("zl")])

    send = pack(images, defocus, references, offsets, posterior, class_ids, seg_count)
    recv = lax.all_to_all(send, ("x", "zl"), 0, 0, tiled=True)
    sent, meta, gx = front(place, recv)
    panel = lax.all_to_all(sent, ("yh", "zh", "zl"), 0, 0, tiled=True)
    near, far = align(place, gx, meta)
    partial = score(panel, near, far)
    partial = lax.all_to_all(
        partial.reshape(NA * NROW, SEG * 8, COLS), ("x", "zl", *ROW), 0, 0, tiled=True
    )
    scores = jnp.sum(partial.astype(f32), axis=0).reshape(SEG, 8, COLS)

    owner = lax.axis_index("yh") // 2
    rest = panel[:, B_NUM:B_ROWS].reshape(NB // 2, 2, CLASSES, COLS)
    numer = jnp.where(owner == 0, rest[:, 0], rest[:, 1]).astype(f32)
    numer = jnp.sum(numer, axis=0)
    facts = jnp.where(owner == 0, rest[:, 1, :, :SEGS], rest[:, 0, :, :SEGS]).astype(f32)
    all_defocus = (facts[:, 0] + facts[:, 1] + facts[:, 2]).reshape(-1)
    all_class = facts[:, 3].reshape(-1)
    all_total = ((facts[:, 5] * 32.0 + facts[:, 6]) * (1.0 / 256)).reshape(-1)
    ctf = contrast(all_defocus[:, None], centred(row * 64 + fil // 2), kx[None, :])
    classes = jnp.arange(CLASSES, dtype=f32)
    totals = jnp.where(all_class[None, :] == classes[:, None], all_total[None, :], 0.0)
    denom = jnp.dot(totals, ctf * ctf, precision=lax.Precision.HIGHEST, preferred_element_type=f32)
    averages = numer * lax.rsqrt(denom + 1.0)
    return scores, averages


def solution(mesh):
    fine = Mesh(mesh.devices.reshape(4, 4, 4, 2, 2, 2), (*FIL, *ROW))
    placed = (
        P(FIL, None, ROW, None),
        P(FIL),
        P(FIL, None, ROW, None),
        P(FIL, None, None),
        P(FIL, None),
        P(FIL),
        P(FIL),
    )
    return jax.shard_map(
        per_device,
        mesh=fine,
        in_specs=placed,
        out_specs=(P(FIL, ROW, None), P(None, (*ROW, *FIL))),
        check_vma=False,
    )
```

```python
import functools
import math

import jax
import jax.numpy as jnp
from jax import lax
from jax.experimental import pallas as pl
from jax.experimental.pallas import tpu as pltpu
from jax.sharding import Mesh
from jax.sharding import PartitionSpec as P

BOX = 256
SHIFTS = 32
CLASSES = 16
SEG = 8
NA = 8
NB = 32
NX = 4
NROW = 4
SEGS = NA * SEG
KY = 8
D = 2 * KY
COLS = 128
META = 8
A_REF = SEG * D
A_META = A_REF + 2 * D
A_ROWS = A_META + META
B_NUM = NX * D
B_ROWS = B_NUM + CLASSES
FIL = ("x", "yh", "zh", "zl")
ROW = ("yl", "core")
bf16 = jnp.bfloat16
f32 = jnp.float32
NEAR = 2
PARTIAL = bf16


def small_sincos(theta):
    t2 = theta * theta
    sin = theta * (1.0 + t2 * (-1.0 / 6 + t2 * (1.0 / 120 + t2 * (-1.0 / 5040 + t2 * (1.0 / 362880)))))
    cos = 1.0 + t2 * (-0.5 + t2 * (1.0 / 24 + t2 * (-1.0 / 720 + t2 * (1.0 / 40320 + t2 * (-1.0 / 3628800)))))
    return sin, cos


def quarter(n, sin, cos):
    quad = n - 4.0 * jnp.floor(n * 0.25)
    odd = (quad == 1.0) | (quad == 3.0)
    c = jnp.where(odd, sin, cos)
    s = jnp.where(odd, cos, sin)
    c = jnp.where((quad == 1.0) | (quad == 2.0), -c, c)
    return jnp.where(quad >= 2.0, -s, s), c


def turn(m):
    n = jnp.floor(m * (1.0 / 64) + 0.5)
    sin, cos = quarter(n, *small_sincos((m - 64.0 * n) * (math.pi / 128)))
    return cos, -sin


def sine(arg):
    n = jnp.floor(arg * (2.0 / math.pi) + 0.5)
    rest = ((arg - n * 1.5703125) - n * 4.837512969970703125e-4) - n * 7.54978995489188216e-8
    return quarter(n, *small_sincos(rest))[0]


def halves(v):
    hi = v.astype(bf16)
    return hi, (v - hi.astype(f32)).astype(bf16)


def parts_of(v):
    hi = v.astype(bf16).astype(f32)
    rest = v - hi
    mid = rest.astype(bf16).astype(f32)
    return hi, mid, rest - mid


def pack_kernel(*refs):
    count_ref, given, out_ref, held, meta_ref, sems = refs[0], refs[1:7], refs[7], refs[8:14], refs[14], refs[15]
    copies = [pltpu.make_async_copy(src, dst, sems.at[k]) for k, (src, dst) in enumerate(zip(given, held))]
    for copy in copies:
        copy.start()
    for copy in copies:
        copy.wait()
    defocus_ref, class_ref, img_ref, ref_ref, off_ref, post_ref = held
    sub = lax.broadcasted_iota(jnp.int32, (META, COLS), 0)
    lane = lax.broadcasted_iota(jnp.int32, (META, COLS), 1)
    live = (sub < count_ref[0]).astype(f32)
    defocus = jnp.zeros((META, COLS), f32)
    ids = jnp.zeros((META, COLS), f32)
    for i in range(SEG):
        defocus = jnp.where(sub == i, defocus_ref[i], defocus)
        ids = jnp.where(sub == i, class_ref[i].astype(f32), ids)
    hi, mid, low = parts_of(defocus)
    facts = jnp.where(lane == 96, hi, jnp.where(lane == 97, mid, jnp.where(lane == 98, low, 0.0)))
    facts = jnp.where(lane == 99, ids, jnp.where(lane == 100, live, facts))
    meta_ref[...] = facts
    for i in range(SEG):
        both = off_ref[i].astype(f32)
        meta_ref[i : i + 1, 0:SHIFTS] = both[0:1]
        meta_ref[i : i + 1, SHIFTS : 2 * SHIFTS] = both[1:2]
    meta_ref[0:SEG, 2 * SHIFTS : 3 * SHIFTS] = post_ref[...].astype(f32) * live[0:SEG, 0:SHIFTS]
    meta = meta_ref[...].astype(bf16)
    for j in range(NA):
        for p in range(2):
            for i in range(SEG):
                out_ref[j, i * D + p * KY : i * D + (p + 1) * KY] = img_ref[i, p, j * KY : (j + 1) * KY]
            for half in range(2):
                base = A_REF + half * D + p * KY
                first = (j // 2) * 2 * KY + half * KY
                out_ref[j, base : base + KY] = ref_ref[0, p, first : first + KY]
        out_ref[j, A_META:A_ROWS] = meta


def pack(images, defocus, references, offsets, posterior, class_ids, seg_count):
    given = (defocus, class_ids, images, references, offsets.transpose(0, 2, 1), posterior)
    places = (pltpu.SMEM,) * 2 + (pltpu.VMEM,) * 4
    return pl.pallas_call(
        pack_kernel,
        in_specs=[pl.BlockSpec(memory_space=pltpu.SMEM)] + [pl.BlockSpec(memory_space=pltpu.HBM)] * 6,
        out_specs=pl.BlockSpec(memory_space=pltpu.VMEM),
        out_shape=jax.ShapeDtypeStruct((NA, A_ROWS, COLS), bf16),
        scratch_shapes=[place(v.shape, v.dtype) for place, v in zip(places, given)]
        + [pltpu.VMEM((META, COLS), f32), pltpu.SemaphoreType.DMA((6,))],
        compiler_params=pltpu.CompilerParams(vmem_limit_bytes=4 << 20),
        cost_estimate=pl.CostEstimate(flops=100_000, bytes_accessed=700_000, transcendentals=0),
        name="pack",
    )(seg_count, *(pltpu.with_memory_space_constraint(v, pltpu.HBM) for v in given))


def front_kernel(place_ref, recv_ref, out_ref, meta_out_ref, gx_ref, wide_ref, y_ref, col_ref):
    kw0 = place_ref[0]
    zl = place_ref[1]
    lane = lax.broadcasted_iota(jnp.int32, (KY, COLS), 1)
    sub = lax.broadcasted_iota(jnp.int32, (KY, COLS), 0)
    kw = (sub + kw0).astype(f32)
    kx = lane.astype(f32)
    radius = (kw * kw + kx * kx) * (1.0 / (BOX * BOX))
    first = (lane % (2 * SHIFTS)) < SHIFTS
    lane_s = lax.broadcasted_iota(jnp.int32, (SHIFTS, COLS), 1)
    sub_s = lax.broadcasted_iota(jnp.int32, (SHIFTS, COLS), 0)

    c, s = turn((sub_s - 8).astype(f32) * lane_s.astype(f32))
    (c_hi, c_lo), (s_hi, s_lo) = halves(c), halves(s)
    table = jnp.concatenate([c_hi, s_hi, c_lo, s_lo], axis=1)

    for a in range(NA):
        meta = recv_ref[a, A_META:A_ROWS].astype(f32)
        rows = slice(a * SEG, (a + 1) * SEG)
        meta_out_ref[rows] = meta
        wide_ref[rows] = meta
        wide_ref[SEGS + a * SEG : SEGS + (a + 1) * SEG] = meta

        def pick(at):
            return jnp.sum(jnp.where(lane == at, meta, 0.0), axis=1, keepdims=True)

        defocus = jnp.broadcast_to(pick(96) + pick(97) + pick(98), (SEG, COLS))
        alive = jnp.broadcast_to(pick(100), (SEG, COLS))
        sy = jnp.where(lane < SHIFTS, meta, 0.0)
        sy = sy + pltpu.roll(sy, SHIFTS, 1)
        sy = sy + pltpu.roll(sy, 2 * SHIFTS, 1)
        w = jnp.where((lane >= 2 * SHIFTS) & (lane < 3 * SHIFTS), meta, 0.0) * (1.0 / 256)
        w = w + pltpu.roll(w, SHIFTS, 1)
        w = w + pltpu.roll(w, 2 * SHIFTS, 1)

        hot = []
        for i in range(SEG):
            spread = jnp.broadcast_to(meta[i : i + 1], (SHIFTS, COLS))
            sx = jnp.sum(jnp.where(lane_s == sub_s + SHIFTS, spread, 0.0), axis=1, keepdims=True)
            hot.append((jnp.broadcast_to(sx, (SHIFTS, SHIFTS)) == (lane_s[:, :SHIFTS] - 8).astype(f32)).astype(f32).astype(bf16))
        col_ref[...] = jnp.dot(jnp.concatenate(hot, axis=0), table, preferred_element_type=f32).astype(bf16)

        for i in range(SEG):
            c, s = turn(jnp.broadcast_to(sy[i : i + 1], (KY, COLS)) * kw)
            wi = jnp.broadcast_to(w[i : i + 1], (KY, COLS))
            c, s = c * wi, s * wi
            left = jnp.concatenate([jnp.where(first, c, -s), jnp.where(first, s, c)], axis=0)
            hi, lo = halves(left)
            right = jnp.concatenate(
                [col_ref[i * SHIFTS : (i + 1) * SHIFTS, q * COLS : (q + 1) * COLS] for q in range(4)], axis=0
            )
            both = jnp.dot(jnp.concatenate([hi, lo], axis=0), right, preferred_element_type=f32)
            q_re = both[0:KY] + both[D : D + KY]
            q_im = both[KY:D] + both[D + KY : 2 * D]
            arg = (200.0 * jnp.broadcast_to(defocus[i : i + 1], (KY, COLS))) * radius + 0.1
            gain = -sine(arg) * jnp.broadcast_to(alive[i : i + 1], (KY, COLS))
            img = recv_ref[a, i * D : (i + 1) * D].astype(f32)
            xr, xi = img[0:KY] * gain, img[KY:D] * gain
            at = (a * SEG + i) * D
            gx_ref[at : at + KY] = xr
            gx_ref[at + KY : at + D] = xi
            y_ref[at : at + KY] = xr * q_re - xi * q_im
            y_ref[at + KY : at + D] = xr * q_im + xi * q_re

    flat = wide_ref[...].T
    ids = jnp.broadcast_to(flat[99:100], (CLASSES, COLS))
    member = (ids == lax.broadcasted_iota(jnp.int32, (CLASSES, COLS), 0).astype(f32)).astype(f32).astype(bf16)
    for p in range(2):
        for ky in range(KY):
            hi, lo = halves(y_ref[pl.ds(p * KY + ky, SEGS, stride=D), :])
            sums = jnp.dot(member, jnp.concatenate([hi, lo], axis=0), preferred_element_type=f32)
            out_ref[(2 * (ky % 4) + p) * 4 + 2 * zl + ky // 4, B_NUM:B_ROWS] = sums.astype(bf16)

    total = jnp.sum(flat[2 * SHIFTS : 3 * SHIFTS], axis=0, keepdims=True)
    total_hi = jnp.floor(total * (1.0 / 32))
    facts = jnp.where(sub == 5, total_hi, jnp.where(sub == 6, total - 32.0 * total_hi, flat[96:104]))
    facts = jnp.concatenate([facts, jnp.zeros((CLASSES - META, COLS), f32)], axis=0).astype(bf16)
    for q in range(D):
        out_ref[(q // 2) * 4 + 2 * (1 - zl) + q % 2, B_NUM:B_ROWS] = facts
    for half in range(2):
        refs = [recv_ref[2 * x + zl, A_REF + half * D : A_REF + (half + 1) * D] for x in range(NX)]
        for q in range(NB):
            if (q // 4) % 2 == half:
                for x in range(NX):
                    out_ref[q, x * D : (x + 1) * D] = refs[x]


def front(place, recv):
    vmem = pl.BlockSpec(memory_space=pltpu.VMEM)
    return pl.pallas_call(
        front_kernel,
        in_specs=[pl.BlockSpec(memory_space=pltpu.SMEM), vmem],
        out_specs=[vmem, vmem, vmem],
        out_shape=[
            jax.ShapeDtypeStruct((NB, B_ROWS, COLS), bf16),
            jax.ShapeDtypeStruct((SEGS, COLS), f32),
            jax.ShapeDtypeStruct((SEGS * D, COLS), f32),
        ],
        scratch_shapes=[
            pltpu.VMEM((COLS, COLS), f32),
            pltpu.VMEM((SEGS * D + D, COLS), f32),
            pltpu.VMEM((SEG * SHIFTS, 4 * COLS), bf16),
        ],
        compiler_params=pltpu.CompilerParams(vmem_limit_bytes=8 << 20),
        cost_estimate=pl.CostEstimate(flops=100_000_000, bytes_accessed=2_000_000, transcendentals=0),
        name="front",
    )(place, recv)


def align_kernel(place_ref, gx_ref, meta_ref, near_ref, far_ref):
    step = pl.program_id(0)
    kw0 = place_ref[0].astype(f32)
    lane = lax.broadcasted_iota(jnp.int32, (SHIFTS, COLS), 1)
    sub = lax.broadcasted_iota(jnp.int32, (SHIFTS, COLS), 0)
    kx = lane.astype(f32)

    def segment(aligned_ref, i, carry):
        wide = jnp.broadcast_to(meta_ref[pl.ds(i, 1), :], (SHIFTS, COLS))
        sy = jnp.sum(jnp.where(lane == sub, wide, 0.0), axis=1, keepdims=True)
        sx = jnp.sum(jnp.where(lane == sub + SHIFTS, wide, 0.0), axis=1, keepdims=True)
        sy = jnp.broadcast_to(sy, (SHIFTS, COLS))
        pr, pi = turn(sy * kw0 + sx * kx)
        si, cr = small_sincos(sy * (-2.0 * math.pi / BOX))
        rows = pl.ds(pl.multiple_of(i * SHIFTS, SHIFTS), SHIFTS)
        for ky in range(KY):
            xr = gx_ref[pl.ds(i * D + ky, 1), :]
            xi = gx_ref[pl.ds(i * D + KY + ky, 1), :]
            aligned_ref[rows, ky * COLS : (ky + 1) * COLS] = (xr * pr - xi * pi).astype(bf16)
            aligned_ref[rows, (KY + ky) * COLS : (KY + ky + 1) * COLS] = (xr * pi + xi * pr).astype(bf16)
            if ky < KY - 1:
                pr, pi = pr * cr - pi * si, pr * si + pi * cr
        return carry

    @pl.when(step < NEAR)
    def _():
        lax.fori_loop(0, SEG, functools.partial(segment, near_ref), 0)

    @pl.when(step >= NEAR)
    def _():
        lax.fori_loop(0, SEG, functools.partial(segment, far_ref), 0)


def align(place, gx, meta):
    return pl.pallas_call(
        align_kernel,
        grid=(NA,),
        in_specs=[
            pl.BlockSpec(memory_space=pltpu.SMEM),
            pl.BlockSpec((SEG * D, COLS), lambda j: (j, 0)),
            pl.BlockSpec((SEG, COLS), lambda j: (j, 0)),
        ],
        out_specs=[
            pl.BlockSpec((SEG * SHIFTS, D * COLS), lambda j: (jnp.minimum(j, NEAR - 1), 0)),
            pl.BlockSpec((SEG * SHIFTS, D * COLS), lambda j: (jnp.maximum(j - NEAR, 0), 0)),
        ],
        out_shape=[
            jax.ShapeDtypeStruct((NEAR * SEG * SHIFTS, D * COLS), bf16),
            pltpu.HBM(((NA - NEAR) * SEG * SHIFTS, D * COLS), bf16),
        ],
        compiler_params=pltpu.CompilerParams(vmem_limit_bytes=10 << 20),
        cost_estimate=pl.CostEstimate(flops=600_000_000, bytes_accessed=9_000_000, transcendentals=0),
        name="align",
    )(place, gx, meta)


def score_kernel(panel_ref, near_ref, far_ref, out_ref, wide_ref, packed_ref, held_ref, made_ref, sems, out_sems):
    refs = NX * NB
    block = SEG * SHIFTS
    copies = [
        pltpu.make_async_copy(
            far_ref.at[j * block : (j + 1) * block], held_ref.at[j * block : (j + 1) * block], sems.at[j]
        )
        for j in range(NA - NEAR)
    ]
    for copy in copies:
        copy.start()

    def widen(q, carry):
        for x in range(NX):
            base = pl.multiple_of((x * NB + (q % 4) * (NB // 4) + q // 4) * D, D)
            wide_ref[pl.ds(base, D), :] = panel_ref[q, x * D : (x + 1) * D, :].astype(f32)
        return carry

    lax.fori_loop(0, NB, widen, 0)
    for d in range(D):
        packed_ref[d * COLS : (d + 1) * COLS, :] = wide_ref[pl.ds(d, refs, stride=D), :].T.astype(bf16)

    done = []
    for j in range(NA):
        if j < NEAR:
            left = near_ref[j * block : (j + 1) * block]
        else:
            copies[j - NEAR].wait()
            left = held_ref[(j - NEAR) * block : (j - NEAR + 1) * block]
        res = jnp.dot(left, packed_ref[...], preferred_element_type=f32)
        for i in range(SEG):
            for r in range(NROW):
                made_ref[j, r, i] = res[i * SHIFTS + r * 8 : i * SHIFTS + (r + 1) * 8, :].astype(out_ref.dtype)
        done.append(pltpu.make_async_copy(made_ref.at[j], out_ref.at[:, j % 2, j // 2], out_sems.at[j]))
        done[-1].start()
    for copy in done:
        copy.wait()


def score(panel, near, far):
    refs = NX * NB
    vmem = pl.BlockSpec(memory_space=pltpu.VMEM)
    return pl.pallas_call(
        score_kernel,
        in_specs=[vmem, vmem, pl.BlockSpec(memory_space=pltpu.HBM)],
        out_specs=pl.BlockSpec(memory_space=pltpu.HBM),
        out_shape=pltpu.HBM((NROW, 2, NX, SEG, 8, refs), PARTIAL),
        scratch_shapes=[
            pltpu.VMEM((refs * D + D, COLS), f32),
            pltpu.VMEM((D * COLS, refs), bf16),
            pltpu.VMEM(far.shape, bf16),
            pltpu.VMEM((NA, NROW, SEG, 8, refs), PARTIAL),
            pltpu.SemaphoreType.DMA((NA - NEAR,)),
            pltpu.SemaphoreType.DMA((NA,)),
        ],
        compiler_params=pltpu.CompilerParams(vmem_limit_bytes=20 << 20),
        cost_estimate=pl.CostEstimate(flops=1_100_000_000, bytes_accessed=10_000_000, transcendentals=0),
        name="score",
    )(panel, near, pltpu.with_memory_space_constraint(far, pltpu.HBM))


def contrast(defocus, kw, kx):
    radius = (kw * kw + kx * kx).astype(f32) / float(BOX * BOX)
    return -jnp.sin(200.0 * defocus * radius + 0.1)


def centred(ky):
    return (ky + BOX // 2) % BOX - BOX // 2


def per_device(images, defocus, references, offsets, posterior, class_ids, seg_count):
    row = lax.axis_index(ROW)
    fil = lax.axis_index(FIL)
    kx = jnp.arange(COLS, dtype=jnp.int32)
    kw_first = centred(row * 64 + lax.axis_index(("x", "zl")) * KY)
    place = jnp.stack([kw_first, lax.axis_index("zl")])

    send = pack(images, defocus, references, offsets, posterior, class_ids, seg_count)
    recv = lax.all_to_all(send, ("x", "zl"), 0, 0, tiled=True)
    sent, meta, gx = front(place, recv)
    panel = lax.all_to_all(sent, ("zh", "zl", "yh"), 0, 0, tiled=True)
    near, far = align(place, gx, meta)
    partial = score(panel, near, far)
    partial = lax.all_to_all(
        partial.reshape(NA * NROW, SEG * 8, COLS), (*ROW, "zl", "x"), 0, 0, tiled=True
    )
    scores = jnp.sum(partial.astype(f32), axis=0).reshape(SEG, 8, COLS)

    owner = lax.axis_index("yh") // 2
    rest = panel[:, B_NUM:B_ROWS].reshape(NB // 8, 2, 4, CLASSES, COLS)
    numer = jnp.where(owner == 0, rest[:, 0], rest[:, 1]).astype(f32)
    numer = jnp.sum(numer, axis=(0, 1))
    facts = jnp.where(owner == 0, rest[:, 1, :, :, :SEGS], rest[:, 0, :, :, :SEGS]).astype(f32)
    facts = facts.reshape(NB // 2, CLASSES, SEGS)
    all_defocus = (facts[:, 0] + facts[:, 1] + facts[:, 2]).reshape(-1)
    all_class = facts[:, 3].reshape(-1)
    all_total = ((facts[:, 5] * 32.0 + facts[:, 6]) * (1.0 / 256)).reshape(-1)
    ctf = contrast(all_defocus[:, None], centred(row * 64 + fil // 2), kx[None, :])
    classes = jnp.arange(CLASSES, dtype=f32)
    totals = jnp.where(all_class[None, :] == classes[:, None], all_total[None, :], 0.0)
    denom = jnp.dot(totals, ctf * ctf, precision=lax.Precision.HIGHEST, preferred_element_type=f32)
    averages = numer * lax.rsqrt(denom + 1.0)
    return scores, averages


def solution(mesh):
    fine = Mesh(mesh.devices.reshape(4, 4, 4, 2, 2, 2), (*FIL, *ROW))
    placed = (
        P(FIL, None, ROW, None),
        P(FIL),
        P(FIL, None, ROW, None),
        P(FIL, None, None),
        P(FIL, None),
        P(FIL),
        P(FIL),
    )
    return jax.shard_map(
        per_device,
        mesh=fine,
        in_specs=placed,
        out_specs=(P(FIL, ROW, None), P(None, (*ROW, *FIL))),
        check_vma=False,
    )
```

```python
import functools
import math

import jax
import jax.numpy as jnp
from jax import lax
from jax.experimental import pallas as pl
from jax.experimental.pallas import tpu as pltpu
from jax.sharding import Mesh
from jax.sharding import PartitionSpec as P

BOX = 256
SHIFTS = 32
CLASSES = 16
SEG = 8
NA = 8
NB = 32
NX = 4
NROW = 4
SEGS = NA * SEG
KY = 8
D = 2 * KY
COLS = 128
META = 8
A_REF = SEG * D
A_META = A_REF + 2 * D
A_ROWS = A_META + META
B_NUM = NX * D
B_ROWS = B_NUM + CLASSES
FIL = ("x", "yh", "zh", "zl")
ROW = ("yl", "core")
bf16 = jnp.bfloat16
f32 = jnp.float32
NEAR = 2
PARTIAL = bf16


def small_sincos(theta):
    t2 = theta * theta
    sin = theta * (1.0 + t2 * (-1.0 / 6 + t2 * (1.0 / 120 + t2 * (-1.0 / 5040 + t2 * (1.0 / 362880)))))
    cos = 1.0 + t2 * (-0.5 + t2 * (1.0 / 24 + t2 * (-1.0 / 720 + t2 * (1.0 / 40320 + t2 * (-1.0 / 3628800)))))
    return sin, cos


def quarter(n, sin, cos):
    quad = n - 4.0 * jnp.floor(n * 0.25)
    odd = (quad == 1.0) | (quad == 3.0)
    c = jnp.where(odd, sin, cos)
    s = jnp.where(odd, cos, sin)
    c = jnp.where((quad == 1.0) | (quad == 2.0), -c, c)
    return jnp.where(quad >= 2.0, -s, s), c


def turn(m):
    n = jnp.floor(m * (1.0 / 64) + 0.5)
    sin, cos = quarter(n, *small_sincos((m - 64.0 * n) * (math.pi / 128)))
    return cos, -sin


def sine(arg):
    n = jnp.floor(arg * (2.0 / math.pi) + 0.5)
    rest = ((arg - n * 1.5703125) - n * 4.837512969970703125e-4) - n * 7.54978995489188216e-8
    return quarter(n, *small_sincos(rest))[0]


def halves(v):
    hi = v.astype(bf16)
    return hi, (v - hi.astype(f32)).astype(bf16)


def parts_of(v):
    hi = v.astype(bf16).astype(f32)
    rest = v - hi
    mid = rest.astype(bf16).astype(f32)
    return hi, mid, rest - mid


def pack_kernel(*refs):
    count_ref, given, out_hbm, held = refs[0], refs[1:7], refs[7], refs[8:14]
    meta_ref, out_ref, sems, out_sems = refs[14:18]
    copies = [pltpu.make_async_copy(src, dst, sems.at[k]) for k, (src, dst) in enumerate(zip(given, held))]
    for copy in copies:
        copy.start()
    for copy in copies[:2] + copies[4:]:
        copy.wait()
    defocus_ref, class_ref, img_ref, ref_ref, off_ref, post_ref = held
    sub = lax.broadcasted_iota(jnp.int32, (META, COLS), 0)
    lane = lax.broadcasted_iota(jnp.int32, (META, COLS), 1)
    live = (sub < count_ref[0]).astype(f32)
    defocus = jnp.zeros((META, COLS), f32)
    ids = jnp.zeros((META, COLS), f32)
    for i in range(SEG):
        defocus = jnp.where(sub == i, defocus_ref[i], defocus)
        ids = jnp.where(sub == i, class_ref[i].astype(f32), ids)
    hi, mid, low = parts_of(defocus)
    facts = jnp.where(lane == 96, hi, jnp.where(lane == 97, mid, jnp.where(lane == 98, low, 0.0)))
    facts = jnp.where(lane == 99, ids, jnp.where(lane == 100, live, facts))
    meta_ref[...] = facts
    for i in range(SEG):
        both = off_ref[i].astype(f32)
        meta_ref[i : i + 1, 0:SHIFTS] = both[0:1]
        meta_ref[i : i + 1, SHIFTS : 2 * SHIFTS] = both[1:2]
    meta_ref[0:SEG, 2 * SHIFTS : 3 * SHIFTS] = post_ref[...].astype(f32) * live[0:SEG, 0:SHIFTS]
    meta = meta_ref[...].astype(bf16)
    copies[2].wait()
    copies[3].wait()
    done = []
    for j in range(NA):
        for p in range(2):
            for i in range(SEG):
                out_ref[j, i * D + p * KY : i * D + (p + 1) * KY] = img_ref[i, p, j * KY : (j + 1) * KY]
            for half in range(2):
                base = A_REF + half * D + p * KY
                first = (j // 2) * 2 * KY + half * KY
                out_ref[j, base : base + KY] = ref_ref[0, p, first : first + KY]
        out_ref[j, A_META:A_ROWS] = meta
        done.append(pltpu.make_async_copy(out_ref.at[j], out_hbm.at[j], out_sems.at[j]))
        done[-1].start()
    for copy in done:
        copy.wait()


def pack(images, defocus, references, offsets, posterior, class_ids, seg_count):
    given = (defocus, class_ids, images, references, offsets.transpose(0, 2, 1), posterior)
    places = (pltpu.SMEM,) * 2 + (pltpu.VMEM,) * 4
    return pl.pallas_call(
        pack_kernel,
        in_specs=[pl.BlockSpec(memory_space=pltpu.SMEM)] + [pl.BlockSpec(memory_space=pltpu.HBM)] * 6,
        out_specs=pl.BlockSpec(memory_space=pltpu.HBM),
        out_shape=pltpu.HBM((NA, A_ROWS, COLS), bf16),
        scratch_shapes=[place(v.shape, v.dtype) for place, v in zip(places, given)]
        + [pltpu.VMEM((META, COLS), f32), pltpu.VMEM((NA, A_ROWS, COLS), bf16), pltpu.SemaphoreType.DMA((6,)), pltpu.SemaphoreType.DMA((NA,))],
        compiler_params=pltpu.CompilerParams(vmem_limit_bytes=4 << 20),
        cost_estimate=pl.CostEstimate(flops=100_000, bytes_accessed=700_000, transcendentals=0),
        name="pack",
    )(seg_count, *(pltpu.with_memory_space_constraint(v, pltpu.HBM) for v in given))


def front_kernel(place_ref, recv_ref, out_ref, meta_out_ref, gx_ref, wide_ref, y_ref, col_ref):
    kw0 = place_ref[0]
    zl = place_ref[1]
    lane = lax.broadcasted_iota(jnp.int32, (KY, COLS), 1)
    sub = lax.broadcasted_iota(jnp.int32, (KY, COLS), 0)
    kw = (sub + kw0).astype(f32)
    kx = lane.astype(f32)
    radius = (kw * kw + kx * kx) * (1.0 / (BOX * BOX))
    first = (lane % (2 * SHIFTS)) < SHIFTS
    lane_s = lax.broadcasted_iota(jnp.int32, (SHIFTS, COLS), 1)
    sub_s = lax.broadcasted_iota(jnp.int32, (SHIFTS, COLS), 0)

    c, s = turn((sub_s - 8).astype(f32) * lane_s.astype(f32))
    (c_hi, c_lo), (s_hi, s_lo) = halves(c), halves(s)
    table = jnp.concatenate([c_hi, s_hi, c_lo, s_lo], axis=1)

    for a in range(NA):
        meta = recv_ref[a, A_META:A_ROWS].astype(f32)
        rows = slice(a * SEG, (a + 1) * SEG)
        meta_out_ref[rows] = meta
        wide_ref[rows] = meta
        wide_ref[SEGS + a * SEG : SEGS + (a + 1) * SEG] = meta

        def pick(at):
            return jnp.sum(jnp.where(lane == at, meta, 0.0), axis=1, keepdims=True)

        defocus = jnp.broadcast_to(pick(96) + pick(97) + pick(98), (SEG, COLS))
        alive = jnp.broadcast_to(pick(100), (SEG, COLS))
        sy = jnp.where(lane < SHIFTS, meta, 0.0)
        sy = sy + pltpu.roll(sy, SHIFTS, 1)
        sy = sy + pltpu.roll(sy, 2 * SHIFTS, 1)
        w = jnp.where((lane >= 2 * SHIFTS) & (lane < 3 * SHIFTS), meta, 0.0) * (1.0 / 256)
        w = w + pltpu.roll(w, SHIFTS, 1)
        w = w + pltpu.roll(w, 2 * SHIFTS, 1)

        hot = []
        for i in range(SEG):
            spread = jnp.broadcast_to(meta[i : i + 1], (SHIFTS, COLS))
            sx = jnp.sum(jnp.where(lane_s == sub_s + SHIFTS, spread, 0.0), axis=1, keepdims=True)
            hot.append((jnp.broadcast_to(sx, (SHIFTS, SHIFTS)) == (lane_s[:, :SHIFTS] - 8).astype(f32)).astype(f32).astype(bf16))
        col_ref[...] = jnp.dot(jnp.concatenate(hot, axis=0), table, preferred_element_type=f32).astype(bf16)

        for i in range(SEG):
            c, s = turn(jnp.broadcast_to(sy[i : i + 1], (KY, COLS)) * kw)
            wi = jnp.broadcast_to(w[i : i + 1], (KY, COLS))
            c, s = c * wi, s * wi
            left = jnp.concatenate([jnp.where(first, c, -s), jnp.where(first, s, c)], axis=0)
            hi, lo = halves(left)
            right = jnp.concatenate(
                [col_ref[i * SHIFTS : (i + 1) * SHIFTS, q * COLS : (q + 1) * COLS] for q in range(4)], axis=0
            )
            both = jnp.dot(jnp.concatenate([hi, lo], axis=0), right, preferred_element_type=f32)
            q_re = both[0:KY] + both[D : D + KY]
            q_im = both[KY:D] + both[D + KY : 2 * D]
            arg = (200.0 * jnp.broadcast_to(defocus[i : i + 1], (KY, COLS))) * radius + 0.1
            gain = -sine(arg) * jnp.broadcast_to(alive[i : i + 1], (KY, COLS))
            img = recv_ref[a, i * D : (i + 1) * D].astype(f32)
            xr, xi = img[0:KY] * gain, img[KY:D] * gain
            at = (a * SEG + i) * D
            gx_ref[at : at + KY] = xr
            gx_ref[at + KY : at + D] = xi
            y_ref[at : at + KY] = xr * q_re - xi * q_im
            y_ref[at + KY : at + D] = xr * q_im + xi * q_re

    flat = wide_ref[...].T
    ids = jnp.broadcast_to(flat[99:100], (CLASSES, COLS))
    member = (ids == lax.broadcasted_iota(jnp.int32, (CLASSES, COLS), 0).astype(f32)).astype(f32).astype(bf16)
    for p in range(2):
        for ky in range(KY):
            hi, lo = halves(y_ref[pl.ds(p * KY + ky, SEGS, stride=D), :])
            sums = jnp.dot(member, jnp.concatenate([hi, lo], axis=0), preferred_element_type=f32)
            out_ref[zl * D + 2 * ky + p, B_NUM:B_ROWS] = sums.astype(bf16)

    total = jnp.sum(flat[2 * SHIFTS : 3 * SHIFTS], axis=0, keepdims=True)
    total_hi = jnp.floor(total * (1.0 / 32))
    facts = jnp.where(sub == 5, total_hi, jnp.where(sub == 6, total - 32.0 * total_hi, flat[96:104]))
    facts = jnp.concatenate([facts, jnp.zeros((CLASSES - META, COLS), f32)], axis=0).astype(bf16)
    for q in range(D):
        out_ref[(1 - zl) * D + q, B_NUM:B_ROWS] = facts
    for half in range(2):
        refs = [recv_ref[2 * x + zl, A_REF + half * D : A_REF + (half + 1) * D] for x in range(NX)]
        for q in range(half, NB, 2):
            for x in range(NX):
                out_ref[q, x * D : (x + 1) * D] = refs[x]


def front(place, recv):
    vmem = pl.BlockSpec(memory_space=pltpu.VMEM)
    return pl.pallas_call(
        front_kernel,
        in_specs=[pl.BlockSpec(memory_space=pltpu.SMEM), vmem],
        out_specs=[vmem, vmem, vmem],
        out_shape=[
            jax.ShapeDtypeStruct((NB, B_ROWS, COLS), bf16),
            jax.ShapeDtypeStruct((SEGS, COLS), f32),
            jax.ShapeDtypeStruct((SEGS * D, COLS), f32),
        ],
        scratch_shapes=[
            pltpu.VMEM((COLS, COLS), f32),
            pltpu.VMEM((SEGS * D + D, COLS), f32),
            pltpu.VMEM((SEG * SHIFTS, 4 * COLS), bf16),
        ],
        compiler_params=pltpu.CompilerParams(vmem_limit_bytes=8 << 20),
        cost_estimate=pl.CostEstimate(flops=100_000_000, bytes_accessed=2_000_000, transcendentals=0),
        name="front",
    )(place, recv)


def align_kernel(place_ref, gx_ref, meta_ref, near_ref, far_ref):
    step = pl.program_id(0)
    kw0 = place_ref[0].astype(f32)
    lane = lax.broadcasted_iota(jnp.int32, (SHIFTS, COLS), 1)
    sub = lax.broadcasted_iota(jnp.int32, (SHIFTS, COLS), 0)
    kx = lane.astype(f32)

    def segment(aligned_ref, i, carry):
        wide = jnp.broadcast_to(meta_ref[pl.ds(i, 1), :], (SHIFTS, COLS))
        sy = jnp.sum(jnp.where(lane == sub, wide, 0.0), axis=1, keepdims=True)
        sx = jnp.sum(jnp.where(lane == sub + SHIFTS, wide, 0.0), axis=1, keepdims=True)
        sy = jnp.broadcast_to(sy, (SHIFTS, COLS))
        pr, pi = turn(sy * kw0 + sx * kx)
        si, cr = small_sincos(sy * (-2.0 * math.pi / BOX))
        rows = pl.ds(pl.multiple_of(i * SHIFTS, SHIFTS), SHIFTS)
        for ky in range(KY):
            xr = gx_ref[pl.ds(i * D + ky, 1), :]
            xi = gx_ref[pl.ds(i * D + KY + ky, 1), :]
            aligned_ref[rows, ky * COLS : (ky + 1) * COLS] = (xr * pr - xi * pi).astype(bf16)
            aligned_ref[rows, (KY + ky) * COLS : (KY + ky + 1) * COLS] = (xr * pi + xi * pr).astype(bf16)
            if ky < KY - 1:
                pr, pi = pr * cr - pi * si, pr * si + pi * cr
        return carry

    @pl.when(step < NEAR)
    def _():
        lax.fori_loop(0, SEG, functools.partial(segment, near_ref), 0)

    @pl.when(step >= NEAR)
    def _():
        lax.fori_loop(0, SEG, functools.partial(segment, far_ref), 0)


def align(place, gx, meta):
    return pl.pallas_call(
        align_kernel,
        grid=(NA,),
        in_specs=[
            pl.BlockSpec(memory_space=pltpu.SMEM),
            pl.BlockSpec((SEG * D, COLS), lambda j: (j, 0)),
            pl.BlockSpec((SEG, COLS), lambda j: (j, 0)),
        ],
        out_specs=[
            pl.BlockSpec((SEG * SHIFTS, D * COLS), lambda j: (jnp.minimum(j, NEAR - 1), 0)),
            pl.BlockSpec((SEG * SHIFTS, D * COLS), lambda j: (jnp.maximum(j - NEAR, 0), 0)),
        ],
        out_shape=[
            jax.ShapeDtypeStruct((NEAR * SEG * SHIFTS, D * COLS), bf16),
            pltpu.HBM(((NA - NEAR) * SEG * SHIFTS, D * COLS), bf16),
        ],
        compiler_params=pltpu.CompilerParams(vmem_limit_bytes=10 << 20),
        cost_estimate=pl.CostEstimate(flops=600_000_000, bytes_accessed=9_000_000, transcendentals=0),
        name="align",
    )(place, gx, meta)


def score_kernel(panel_ref, near_ref, far_ref, out_ref, wide_ref, packed_ref, held_ref, made_ref, sems, out_sems):
    refs = NX * NB
    block = SEG * SHIFTS
    copies = [
        pltpu.make_async_copy(
            far_ref.at[j * block : (j + 1) * block], held_ref.at[j * block : (j + 1) * block], sems.at[j]
        )
        for j in range(NA - NEAR)
    ]
    for copy in copies:
        copy.start()

    def widen(q, carry):
        for x in range(NX):
            base = pl.multiple_of((x * NB + q) * D, D)
            wide_ref[pl.ds(base, D), :] = panel_ref[q, x * D : (x + 1) * D, :].astype(f32)
        return carry

    lax.fori_loop(0, NB, widen, 0)
    for d in range(D):
        packed_ref[d * COLS : (d + 1) * COLS, :] = wide_ref[pl.ds(d, refs, stride=D), :].T.astype(bf16)

    done = []
    for j in range(NA):
        if j < NEAR:
            left = near_ref[j * block : (j + 1) * block]
        else:
            copies[j - NEAR].wait()
            left = held_ref[(j - NEAR) * block : (j - NEAR + 1) * block]
        res = jnp.dot(left, packed_ref[...], preferred_element_type=f32)
        for i in range(SEG):
            for r in range(NROW):
                made_ref[j, r, i] = res[i * SHIFTS + r * 8 : i * SHIFTS + (r + 1) * 8, :].astype(out_ref.dtype)
        done.append(pltpu.make_async_copy(made_ref.at[j], out_ref.at[j], out_sems.at[j]))
        done[-1].start()
    for copy in done:
        copy.wait()


def score(panel, near, far):
    refs = NX * NB
    vmem = pl.BlockSpec(memory_space=pltpu.VMEM)
    return pl.pallas_call(
        score_kernel,
        in_specs=[vmem, vmem, pl.BlockSpec(memory_space=pltpu.HBM)],
        out_specs=pl.BlockSpec(memory_space=pltpu.HBM),
        out_shape=pltpu.HBM((NA, NROW, SEG, 8, refs), PARTIAL),
        scratch_shapes=[
            pltpu.VMEM((refs * D + D, COLS), f32),
            pltpu.VMEM((D * COLS, refs), bf16),
            pltpu.VMEM(far.shape, bf16),
            pltpu.VMEM((NA, NROW, SEG, 8, refs), PARTIAL),
            pltpu.SemaphoreType.DMA((NA - NEAR,)),
            pltpu.SemaphoreType.DMA((NA,)),
        ],
        compiler_params=pltpu.CompilerParams(vmem_limit_bytes=20 << 20),
        cost_estimate=pl.CostEstimate(flops=1_100_000_000, bytes_accessed=10_000_000, transcendentals=0),
        name="score",
    )(panel, near, pltpu.with_memory_space_constraint(far, pltpu.HBM))


def contrast(defocus, kw, kx):
    radius = (kw * kw + kx * kx).astype(f32) / float(BOX * BOX)
    return -jnp.sin(200.0 * defocus * radius + 0.1)


def centred(ky):
    return (ky + BOX // 2) % BOX - BOX // 2


def per_device(images, defocus, references, offsets, posterior, class_ids, seg_count):
    row = lax.axis_index(ROW)
    fil = lax.axis_index(FIL)
    kx = jnp.arange(COLS, dtype=jnp.int32)
    kw_first = centred(row * 64 + lax.axis_index(("x", "zl")) * KY)
    place = jnp.stack([kw_first, lax.axis_index("zl")])

    send = pack(images, defocus, references, offsets, posterior, class_ids, seg_count)
    recv = lax.all_to_all(send, ("x", "zl"), 0, 0, tiled=True)
    sent, meta, gx = front(place, recv)
    panel = lax.all_to_all(sent, ("yh", "zh", "zl"), 0, 0, tiled=True)
    near, far = align(place, gx, meta)
    partial = score(panel, near, far)
    partial = lax.all_to_all(
        partial.reshape(NA * NROW, SEG * 8, COLS), ("x", "zl", *ROW), 0, 0, tiled=True
    )
    scores = jnp.sum(partial.astype(f32), axis=0).reshape(SEG, 8, COLS)

    owner = lax.axis_index("yh") // 2
    rest = panel[:, B_NUM:B_ROWS].reshape(NB // 2, 2, CLASSES, COLS)
    numer = jnp.where(owner == 0, rest[:, 0], rest[:, 1]).astype(f32)
    numer = jnp.sum(numer, axis=0)
    facts = jnp.where(owner == 0, rest[:, 1, :, :SEGS], rest[:, 0, :, :SEGS]).astype(f32)
    all_defocus = (facts[:, 0] + facts[:, 1] + facts[:, 2]).reshape(-1)
    all_class = facts[:, 3].reshape(-1)
    all_total = ((facts[:, 5] * 32.0 + facts[:, 6]) * (1.0 / 256)).reshape(-1)
    ctf = contrast(all_defocus[:, None], centred(row * 64 + fil // 2), kx[None, :])
    classes = jnp.arange(CLASSES, dtype=f32)
    totals = jnp.where(all_class[None, :] == classes[:, None], all_total[None, :], 0.0)
    denom = jnp.dot(totals, ctf * ctf, precision=lax.Precision.HIGHEST, preferred_element_type=f32)
    averages = numer * lax.rsqrt(denom + 1.0)
    return scores, averages


def solution(mesh):
    fine = Mesh(mesh.devices.reshape(4, 4, 4, 2, 2, 2), (*FIL, *ROW))
    placed = (
        P(FIL, None, ROW, None),
        P(FIL),
        P(FIL, None, ROW, None),
        P(FIL, None, None),
        P(FIL, None),
        P(FIL),
        P(FIL),
    )
    return jax.shard_map(
        per_device,
        mesh=fine,
        in_specs=placed,
        out_specs=(P(FIL, ROW, None), P(None, (*ROW, *FIL))),
        check_vma=False,
    )
```

```python
import functools
import math

import jax
import jax.numpy as jnp
from jax import lax
from jax.experimental import pallas as pl
from jax.experimental.pallas import tpu as pltpu
from jax.sharding import Mesh
from jax.sharding import PartitionSpec as P

BOX = 256
SHIFTS = 32
CLASSES = 16
SEG = 8
NA = 8
NB = 32
NX = 4
NROW = 4
SEGS = NA * SEG
KY = 8
D = 2 * KY
COLS = 128
META = 8
A_REF = SEG * D
A_META = A_REF + 2 * D
A_ROWS = A_META + META
B_NUM = NX * D
B_ROWS = B_NUM + CLASSES
FIL = ("x", "yh", "zh", "zl")
ROW = ("yl", "core")
bf16 = jnp.bfloat16
f32 = jnp.float32
NEAR = 2
PARTIAL = bf16


def small_sincos(theta):
    t2 = theta * theta
    sin = theta * (1.0 + t2 * (-1.0 / 6 + t2 * (1.0 / 120 + t2 * (-1.0 / 5040 + t2 * (1.0 / 362880)))))
    cos = 1.0 + t2 * (-0.5 + t2 * (1.0 / 24 + t2 * (-1.0 / 720 + t2 * (1.0 / 40320 + t2 * (-1.0 / 3628800)))))
    return sin, cos


def quarter(n, sin, cos):
    quad = n - 4.0 * jnp.floor(n * 0.25)
    odd = (quad == 1.0) | (quad == 3.0)
    c = jnp.where(odd, sin, cos)
    s = jnp.where(odd, cos, sin)
    c = jnp.where((quad == 1.0) | (quad == 2.0), -c, c)
    return jnp.where(quad >= 2.0, -s, s), c


def turn(m):
    n = jnp.floor(m * (1.0 / 64) + 0.5)
    sin, cos = quarter(n, *small_sincos((m - 64.0 * n) * (math.pi / 128)))
    return cos, -sin


def sine(arg):
    n = jnp.floor(arg * (2.0 / math.pi) + 0.5)
    rest = ((arg - n * 1.5703125) - n * 4.837512969970703125e-4) - n * 7.54978995489188216e-8
    return quarter(n, *small_sincos(rest))[0]


def halves(v):
    hi = v.astype(bf16)
    return hi, (v - hi.astype(f32)).astype(bf16)


def parts_of(v):
    hi = v.astype(bf16).astype(f32)
    rest = v - hi
    mid = rest.astype(bf16).astype(f32)
    return hi, mid, rest - mid


def pack_kernel(*refs):
    count_ref, given, out_hbm, held = refs[0], refs[1:7], refs[7], refs[8:14]
    meta_ref, out_ref, sems, out_sems = refs[14:18]
    copies = [pltpu.make_async_copy(src, dst, sems.at[k]) for k, (src, dst) in enumerate(zip(given, held))]
    for copy in copies:
        copy.start()
    for copy in copies[:2] + copies[4:]:
        copy.wait()
    defocus_ref, class_ref, img_ref, ref_ref, off_ref, post_ref = held
    sub = lax.broadcasted_iota(jnp.int32, (META, COLS), 0)
    lane = lax.broadcasted_iota(jnp.int32, (META, COLS), 1)
    live = (sub < count_ref[0]).astype(f32)
    defocus = jnp.zeros((META, COLS), f32)
    ids = jnp.zeros((META, COLS), f32)
    for i in range(SEG):
        defocus = jnp.where(sub == i, defocus_ref[i], defocus)
        ids = jnp.where(sub == i, class_ref[i].astype(f32), ids)
    hi, mid, low = parts_of(defocus)
    facts = jnp.where(lane == 96, hi, jnp.where(lane == 97, mid, jnp.where(lane == 98, low, 0.0)))
    facts = jnp.where(lane == 99, ids, jnp.where(lane == 100, live, facts))
    meta_ref[...] = facts
    for i in range(SEG):
        both = off_ref[i].astype(f32)
        meta_ref[i : i + 1, 0:SHIFTS] = both[0:1]
        meta_ref[i : i + 1, SHIFTS : 2 * SHIFTS] = both[1:2]
    meta_ref[0:SEG, 2 * SHIFTS : 3 * SHIFTS] = post_ref[...].astype(f32) * live[0:SEG, 0:SHIFTS]
    meta = meta_ref[...].astype(bf16)
    copies[2].wait()
    copies[3].wait()
    done = []
    for j in range(NA):
        for p in range(2):
            for i in range(SEG):
                out_ref[j, i * D + p * KY : i * D + (p + 1) * KY] = img_ref[i, p, j * KY : (j + 1) * KY]
            for half in range(2):
                base = A_REF + half * D + p * KY
                first = (j // 2) * 2 * KY + half * KY
                out_ref[j, base : base + KY] = ref_ref[0, p, first : first + KY]
        out_ref[j, A_META:A_ROWS] = meta
        done.append(pltpu.make_async_copy(out_ref.at[j], out_hbm.at[j], out_sems.at[j]))
        done[-1].start()
    for copy in done:
        copy.wait()


def pack(images, defocus, references, offsets, posterior, class_ids, seg_count):
    given = (defocus, class_ids, images, references, offsets.transpose(0, 2, 1), posterior)
    places = (pltpu.SMEM,) * 2 + (pltpu.VMEM,) * 4
    return pl.pallas_call(
        pack_kernel,
        in_specs=[pl.BlockSpec(memory_space=pltpu.SMEM)] + [pl.BlockSpec(memory_space=pltpu.HBM)] * 6,
        out_specs=pl.BlockSpec(memory_space=pltpu.HBM),
        out_shape=pltpu.HBM((NA, A_ROWS, COLS), bf16),
        scratch_shapes=[place(v.shape, v.dtype) for place, v in zip(places, given)]
        + [pltpu.VMEM((META, COLS), f32), pltpu.VMEM((NA, A_ROWS, COLS), bf16), pltpu.SemaphoreType.DMA((6,)), pltpu.SemaphoreType.DMA((NA,))],
        compiler_params=pltpu.CompilerParams(vmem_limit_bytes=4 << 20),
        cost_estimate=pl.CostEstimate(flops=100_000, bytes_accessed=700_000, transcendentals=0),
        name="pack",
    )(seg_count, *(pltpu.with_memory_space_constraint(v, pltpu.HBM) for v in given))


def front_kernel(place_ref, recv_ref, out_ref, meta_out_ref, gx_ref, wide_ref, y_ref, col_ref):
    kw0 = place_ref[0]
    zl = place_ref[1]
    lane = lax.broadcasted_iota(jnp.int32, (KY, COLS), 1)
    sub = lax.broadcasted_iota(jnp.int32, (KY, COLS), 0)
    kw = (sub + kw0).astype(f32)
    kx = lane.astype(f32)
    radius = (kw * kw + kx * kx) * (1.0 / (BOX * BOX))
    first = (lane % (2 * SHIFTS)) < SHIFTS
    lane_s = lax.broadcasted_iota(jnp.int32, (SHIFTS, COLS), 1)
    sub_s = lax.broadcasted_iota(jnp.int32, (SHIFTS, COLS), 0)

    c, s = turn((sub_s - 8).astype(f32) * lane_s.astype(f32))
    (c_hi, c_lo), (s_hi, s_lo) = halves(c), halves(s)
    table = jnp.concatenate([c_hi, s_hi, c_lo, s_lo], axis=1)

    for a in range(NA):
        meta = recv_ref[a, A_META:A_ROWS].astype(f32)
        rows = slice(a * SEG, (a + 1) * SEG)
        meta_out_ref[rows] = meta
        wide_ref[rows] = meta
        wide_ref[SEGS + a * SEG : SEGS + (a + 1) * SEG] = meta

        def pick(at):
            return jnp.sum(jnp.where(lane == at, meta, 0.0), axis=1, keepdims=True)

        defocus = jnp.broadcast_to(pick(96) + pick(97) + pick(98), (SEG, COLS))
        alive = jnp.broadcast_to(pick(100), (SEG, COLS))
        sy = jnp.where(lane < SHIFTS, meta, 0.0)
        sy = sy + pltpu.roll(sy, SHIFTS, 1)
        sy = sy + pltpu.roll(sy, 2 * SHIFTS, 1)
        w = jnp.where((lane >= 2 * SHIFTS) & (lane < 3 * SHIFTS), meta, 0.0) * (1.0 / 256)
        w = w + pltpu.roll(w, SHIFTS, 1)
        w = w + pltpu.roll(w, 2 * SHIFTS, 1)

        hot = []
        for i in range(SEG):
            spread = jnp.broadcast_to(meta[i : i + 1], (SHIFTS, COLS))
            sx = jnp.sum(jnp.where(lane_s == sub_s + SHIFTS, spread, 0.0), axis=1, keepdims=True)
            hot.append((jnp.broadcast_to(sx, (SHIFTS, SHIFTS)) == (lane_s[:, :SHIFTS] - 8).astype(f32)).astype(f32).astype(bf16))
        col_ref[...] = jnp.dot(jnp.concatenate(hot, axis=0), table, preferred_element_type=f32).astype(bf16)

        for pair in range(0, SEG, 2):
            lefts, rights = [], []
            for i in (pair, pair + 1):
                c, s = turn(jnp.broadcast_to(sy[i : i + 1], (KY, COLS)) * kw)
                wi = jnp.broadcast_to(w[i : i + 1], (KY, COLS))
                c, s = c * wi, s * wi
                left = jnp.concatenate([jnp.where(first, c, -s), jnp.where(first, s, c)], axis=0)
                lefts += halves(left)
                rights.append(jnp.concatenate(
                    [col_ref[i * SHIFTS : (i + 1) * SHIFTS, q * COLS : (q + 1) * COLS] for q in range(4)], axis=0
                ))
            product = jnp.dot(
                jnp.concatenate(lefts, axis=0), jnp.concatenate(rights, axis=1), preferred_element_type=f32
            )
            for k in range(2):
                i = pair + k
                both = product[k * 2 * D : (k + 1) * 2 * D, k * COLS : (k + 1) * COLS]
                q_re = both[0:KY] + both[D : D + KY]
                q_im = both[KY:D] + both[D + KY : 2 * D]
                arg = (200.0 * jnp.broadcast_to(defocus[i : i + 1], (KY, COLS))) * radius + 0.1
                gain = -sine(arg) * jnp.broadcast_to(alive[i : i + 1], (KY, COLS))
                img = recv_ref[a, i * D : (i + 1) * D].astype(f32)
                xr, xi = img[0:KY] * gain, img[KY:D] * gain
                at = (a * SEG + i) * D
                gx_ref[at : at + KY] = xr
                gx_ref[at + KY : at + D] = xi
                y_ref[at : at + KY] = xr * q_re - xi * q_im
                y_ref[at + KY : at + D] = xr * q_im + xi * q_re

    flat = wide_ref[...].T
    ids = jnp.broadcast_to(flat[99:100], (CLASSES, COLS))
    member = (ids == lax.broadcasted_iota(jnp.int32, (CLASSES, COLS), 0).astype(f32)).astype(f32).astype(bf16)
    for p in range(2):
        for ky in range(KY):
            hi, lo = halves(y_ref[pl.ds(p * KY + ky, SEGS, stride=D), :])
            sums = jnp.dot(member, jnp.concatenate([hi, lo], axis=0), preferred_element_type=f32)
            out_ref[zl * D + 2 * ky + p, B_NUM:B_ROWS] = sums.astype(bf16)

    total = jnp.sum(flat[2 * SHIFTS : 3 * SHIFTS], axis=0, keepdims=True)
    total_hi = jnp.floor(total * (1.0 / 32))
    facts = jnp.where(sub == 5, total_hi, jnp.where(sub == 6, total - 32.0 * total_hi, flat[96:104]))
    facts = jnp.concatenate([facts, jnp.zeros((CLASSES - META, COLS), f32)], axis=0).astype(bf16)
    for q in range(D):
        out_ref[(1 - zl) * D + q, B_NUM:B_ROWS] = facts
    for half in range(2):
        refs = [recv_ref[2 * x + zl, A_REF + half * D : A_REF + (half + 1) * D] for x in range(NX)]
        for q in range(half, NB, 2):
            for x in range(NX):
                out_ref[q, x * D : (x + 1) * D] = refs[x]


def front(place, recv):
    vmem = pl.BlockSpec(memory_space=pltpu.VMEM)
    return pl.pallas_call(
        front_kernel,
        in_specs=[pl.BlockSpec(memory_space=pltpu.SMEM), vmem],
        out_specs=[vmem, vmem, vmem],
        out_shape=[
            jax.ShapeDtypeStruct((NB, B_ROWS, COLS), bf16),
            jax.ShapeDtypeStruct((SEGS, COLS), f32),
            jax.ShapeDtypeStruct((SEGS * D, COLS), f32),
        ],
        scratch_shapes=[
            pltpu.VMEM((COLS, COLS), f32),
            pltpu.VMEM((SEGS * D + D, COLS), f32),
            pltpu.VMEM((SEG * SHIFTS, 4 * COLS), bf16),
        ],
        compiler_params=pltpu.CompilerParams(vmem_limit_bytes=8 << 20),
        cost_estimate=pl.CostEstimate(flops=100_000_000, bytes_accessed=2_000_000, transcendentals=0),
        name="front",
    )(place, recv)


def align_kernel(place_ref, gx_ref, meta_ref, near_ref, far_ref):
    step = pl.program_id(0)
    kw0 = place_ref[0].astype(f32)
    lane = lax.broadcasted_iota(jnp.int32, (SHIFTS, COLS), 1)
    sub = lax.broadcasted_iota(jnp.int32, (SHIFTS, COLS), 0)
    kx = lane.astype(f32)

    def segment(aligned_ref, i, carry):
        wide = jnp.broadcast_to(meta_ref[pl.ds(i, 1), :], (SHIFTS, COLS))
        sy = jnp.sum(jnp.where(lane == sub, wide, 0.0), axis=1, keepdims=True)
        sx = jnp.sum(jnp.where(lane == sub + SHIFTS, wide, 0.0), axis=1, keepdims=True)
        sy = jnp.broadcast_to(sy, (SHIFTS, COLS))
        pr, pi = turn(sy * kw0 + sx * kx)
        si, cr = small_sincos(sy * (-2.0 * math.pi / BOX))
        rows = pl.ds(pl.multiple_of(i * SHIFTS, SHIFTS), SHIFTS)
        for ky in range(KY):
            xr = gx_ref[pl.ds(i * D + ky, 1), :]
            xi = gx_ref[pl.ds(i * D + KY + ky, 1), :]
            aligned_ref[rows, ky * COLS : (ky + 1) * COLS] = (xr * pr - xi * pi).astype(bf16)
            aligned_ref[rows, (KY + ky) * COLS : (KY + ky + 1) * COLS] = (xr * pi + xi * pr).astype(bf16)
            if ky < KY - 1:
                pr, pi = pr * cr - pi * si, pr * si + pi * cr
        return carry

    @pl.when(step < NEAR)
    def _():
        lax.fori_loop(0, SEG, functools.partial(segment, near_ref), 0)

    @pl.when(step >= NEAR)
    def _():
        lax.fori_loop(0, SEG, functools.partial(segment, far_ref), 0)


def align(place, gx, meta):
    return pl.pallas_call(
        align_kernel,
        grid=(NA,),
        in_specs=[
            pl.BlockSpec(memory_space=pltpu.SMEM),
            pl.BlockSpec((SEG * D, COLS), lambda j: (j, 0)),
            pl.BlockSpec((SEG, COLS), lambda j: (j, 0)),
        ],
        out_specs=[
            pl.BlockSpec((SEG * SHIFTS, D * COLS), lambda j: (jnp.minimum(j, NEAR - 1), 0)),
            pl.BlockSpec((SEG * SHIFTS, D * COLS), lambda j: (jnp.maximum(j - NEAR, 0), 0)),
        ],
        out_shape=[
            jax.ShapeDtypeStruct((NEAR * SEG * SHIFTS, D * COLS), bf16),
            pltpu.HBM(((NA - NEAR) * SEG * SHIFTS, D * COLS), bf16),
        ],
        compiler_params=pltpu.CompilerParams(vmem_limit_bytes=10 << 20),
        cost_estimate=pl.CostEstimate(flops=600_000_000, bytes_accessed=9_000_000, transcendentals=0),
        name="align",
    )(place, gx, meta)


def score_kernel(panel_ref, near_ref, far_ref, out_ref, wide_ref, packed_ref, held_ref, made_ref, sems, out_sems):
    refs = NX * NB
    block = SEG * SHIFTS
    copies = [
        pltpu.make_async_copy(
            far_ref.at[j * block : (j + 1) * block], held_ref.at[j * block : (j + 1) * block], sems.at[j]
        )
        for j in range(NA - NEAR)
    ]
    for copy in copies:
        copy.start()

    def widen(q, carry):
        for x in range(NX):
            base = pl.multiple_of((x * NB + q) * D, D)
            wide_ref[pl.ds(base, D), :] = panel_ref[q, x * D : (x + 1) * D, :].astype(f32)
        return carry

    lax.fori_loop(0, NB, widen, 0)
    for d in range(D):
        packed_ref[d * COLS : (d + 1) * COLS, :] = wide_ref[pl.ds(d, refs, stride=D), :].T.astype(bf16)

    done = []
    for j in range(NA):
        if j < NEAR:
            left = near_ref[j * block : (j + 1) * block]
        else:
            copies[j - NEAR].wait()
            left = held_ref[(j - NEAR) * block : (j - NEAR + 1) * block]
        res = jnp.dot(left, packed_ref[...], preferred_element_type=f32)
        for i in range(SEG):
            for r in range(NROW):
                made_ref[j, r, i] = res[i * SHIFTS + r * 8 : i * SHIFTS + (r + 1) * 8, :].astype(out_ref.dtype)
        done.append(pltpu.make_async_copy(made_ref.at[j], out_ref.at[j], out_sems.at[j]))
        done[-1].start()
    for copy in done:
        copy.wait()


def score(panel, near, far):
    refs = NX * NB
    vmem = pl.BlockSpec(memory_space=pltpu.VMEM)
    return pl.pallas_call(
        score_kernel,
        in_specs=[vmem, vmem, pl.BlockSpec(memory_space=pltpu.HBM)],
        out_specs=pl.BlockSpec(memory_space=pltpu.HBM),
        out_shape=pltpu.HBM((NA, NROW, SEG, 8, refs), PARTIAL),
        scratch_shapes=[
            pltpu.VMEM((refs * D + D, COLS), f32),
            pltpu.VMEM((D * COLS, refs), bf16),
            pltpu.VMEM(far.shape, bf16),
            pltpu.VMEM((NA, NROW, SEG, 8, refs), PARTIAL),
            pltpu.SemaphoreType.DMA((NA - NEAR,)),
            pltpu.SemaphoreType.DMA((NA,)),
        ],
        compiler_params=pltpu.CompilerParams(vmem_limit_bytes=20 << 20),
        cost_estimate=pl.CostEstimate(flops=1_100_000_000, bytes_accessed=10_000_000, transcendentals=0),
        name="score",
    )(panel, near, pltpu.with_memory_space_constraint(far, pltpu.HBM))


def contrast(defocus, kw, kx):
    radius = (kw * kw + kx * kx).astype(f32) / float(BOX * BOX)
    return -jnp.sin(200.0 * defocus * radius + 0.1)


def centred(ky):
    return (ky + BOX // 2) % BOX - BOX // 2


def per_device(images, defocus, references, offsets, posterior, class_ids, seg_count):
    row = lax.axis_index(ROW)
    fil = lax.axis_index(FIL)
    kx = jnp.arange(COLS, dtype=jnp.int32)
    kw_first = centred(row * 64 + lax.axis_index(("x", "zl")) * KY)
    place = jnp.stack([kw_first, lax.axis_index("zl")])

    send = pack(images, defocus, references, offsets, posterior, class_ids, seg_count)
    recv = lax.all_to_all(send, ("x", "zl"), 0, 0, tiled=True)
    sent, meta, gx = front(place, recv)
    panel = lax.all_to_all(sent, ("yh", "zh", "zl"), 0, 0, tiled=True)
    near, far = align(place, gx, meta)
    partial = score(panel, near, far)
    partial = lax.all_to_all(
        partial.reshape(NA * NROW, SEG * 8, COLS), ("x", "zl", *ROW), 0, 0, tiled=True
    )
    scores = jnp.sum(partial.astype(f32), axis=0).reshape(SEG, 8, COLS)

    owner = lax.axis_index("yh") // 2
    rest = panel[:, B_NUM:B_ROWS].reshape(NB // 2, 2, CLASSES, COLS)
    numer = jnp.where(owner == 0, rest[:, 0], rest[:, 1]).astype(f32)
    numer = jnp.sum(numer, axis=0)
    facts = jnp.where(owner == 0, rest[:, 1, :, :SEGS], rest[:, 0, :, :SEGS]).astype(f32)
    all_defocus = (facts[:, 0] + facts[:, 1] + facts[:, 2]).reshape(-1)
    all_class = facts[:, 3].reshape(-1)
    all_total = ((facts[:, 5] * 32.0 + facts[:, 6]) * (1.0 / 256)).reshape(-1)
    ctf = contrast(all_defocus[:, None], centred(row * 64 + fil // 2), kx[None, :])
    classes = jnp.arange(CLASSES, dtype=f32)
    totals = jnp.where(all_class[None, :] == classes[:, None], all_total[None, :], 0.0)
    denom = jnp.dot(totals, ctf * ctf, precision=lax.Precision.HIGHEST, preferred_element_type=f32)
    averages = numer * lax.rsqrt(denom + 1.0)
    return scores, averages


def solution(mesh):
    fine = Mesh(mesh.devices.reshape(4, 4, 4, 2, 2, 2), (*FIL, *ROW))
    placed = (
        P(FIL, None, ROW, None),
        P(FIL),
        P(FIL, None, ROW, None),
        P(FIL, None, None),
        P(FIL, None),
        P(FIL),
        P(FIL),
    )
    return jax.shard_map(
        per_device,
        mesh=fine,
        in_specs=placed,
        out_specs=(P(FIL, ROW, None), P(None, (*ROW, *FIL))),
        check_vma=False,
    )
```
